32 devices in a mesh: dp: 2 (over core), fsdp: 16 (over z, y, x).
Axes of the slice: x: 2, y: 2, z: 4, core: 2. Of those that a mesh axis runs over, the one named last changes fastest.
Arguments:
- tokens: bfloat16 [8192, 1024], P(('dp', 'fsdp')), may hold values from -27 to 27
- attn_gain: bfloat16 [1024], P(('dp', 'fsdp')), may hold values from 0.5 to 1.5
- w_query: bfloat16 [1024, 1024], P(('dp', 'fsdp')), may hold values from -0.1875 to 0.1875
- w_key: bfloat16 [1024, 1024], P(('dp', 'fsdp')), may hold values from -0.1875 to 0.1875
- w_value: bfloat16 [1024, 1024], P(('dp', 'fsdp')), may hold values from -0.1875 to 0.1875
- w_gate: bfloat16 [1024, 1024], P(('dp', 'fsdp')), may hold values from -0.1875 to 0.1875
- w_output: bfloat16 [1024, 1024], P(('dp', 'fsdp')), may hold values from -0.75 to 0.75
- ffn_gain: bfloat16 [1024], P(('dp', 'fsdp')), may hold values from 0.5 to 1.5
- w_first: bfloat16 [1024, 2816], P(('dp', 'fsdp')), may hold values from -0.1875 to 0.1875
- w_second: bfloat16 [1024, 2816], P(('dp', 'fsdp')), may hold values from -0.1875 to 0.1875
- w_down: bfloat16 [2816, 1024], P(('dp', 'fsdp')), may hold values from -0.109375 to 0.109375
- cotangent: bfloat16 [8192, 1024], P(('dp', 'fsdp')), may hold values from -6 to 6
Outputs:
- block_out: bfloat16 [8192, 1024], P(('dp', 'fsdp'))
- tokens_grad: float32 [8192, 1024], P(('dp', 'fsdp'))
- attn_gain_grad: float32 [1024], P(('dp', 'fsdp'))
- w_query_grad: float32 [1024, 1024], P(('dp', 'fsdp'))
- w_key_grad: float32 [1024, 1024], P(('dp', 'fsdp'))
- w_value_grad: float32 [1024, 1024], P(('dp', 'fsdp'))
- w_gate_grad: float32 [1024, 1024], P(('dp', 'fsdp'))
- w_output_grad: float32 [1024, 1024], P(('dp', 'fsdp'))
- ffn_gain_grad: float32 [1024], P(('dp', 'fsdp'))
- w_first_grad: float32 [1024, 2816], P(('dp', 'fsdp'))
- w_second_grad: float32 [1024, 2816], P(('dp', 'fsdp'))
- w_down_grad: float32 [2816, 1024], P(('dp', 'fsdp'))
The draws below stay inside these ranges and needn't reach their ends.
All inputs are finite; a program needn't handle non-finite values.
Results may differ from the reference program's by a relative error of at most 0.018.
Values may be sent and summed in bfloat16 or wider, within the bound.
A program may use at most 192 MiB of HBM per device.

```python
import math
import jax
import jax.numpy as jnp
from jax import lax

D = 1024
HEADS = 16
HDIM = 64
FF = 2816
BLK = 64
SEQ = 256
TOKENS = 8192


def draw_tokens(key, part):
    noise_key, row_key, column_key = jax.random.split(key, 3)
    row_scale = jnp.exp(jax.random.uniform(row_key, (TOKENS, 1), jnp.float32, math.log(0.3), math.log(3.0)))
    column_scale = jnp.exp(jax.random.uniform(column_key, (1, D), jnp.float32, math.log(0.3), math.log(3.0)))
    noise_field = jnp.clip(jax.random.normal(noise_key, (TOKENS, D), jnp.float32), -3.0, 3.0)
    return (noise_field * row_scale * column_scale).astype(jnp.bfloat16)


def levels(stream_key, extent, shards, least, largest):
    loudness = 1.0
    for axis_at, parts in shards:
        draws = jax.random.uniform(jax.random.fold_in(jax.random.fold_in(stream_key, 6), axis_at), (parts,), jnp.float32, least / len(shards), largest / len(shards))
        loudness = loudness * jnp.repeat(jnp.exp(draws), extent[axis_at] // parts).reshape((-1,) + (1,) * (len(extent) - 1 - axis_at))
    return loudness


def bell_draw(key, shape, deviation, limit, cuts=(), dtype=jnp.bfloat16):
    values = deviation * jax.random.normal(key, shape, jnp.float32)
    if cuts:
        values = values * levels(key, shape, cuts, -0.22, 0.18)
    return jnp.clip(values, -limit, limit).astype(dtype)


def setup_inputs(seed: int = 0) -> dict:
    streams_of = jax.random.split(jax.random.key(seed), 13)
    tokens = draw_tokens(jax.random.fold_in(streams_of[12], 71), 0)
    attn_gain = jnp.clip(1.0 + 0.1 * jax.random.normal(streams_of[1], (D,), jnp.float32), 0.5, 1.5).astype(jnp.bfloat16)
    w_query = bell_draw(streams_of[2], (D, D), D ** -0.5, 0.1875, ((0, 32),))
    w_key = bell_draw(streams_of[3], (D, D), D ** -0.5, 0.1875, ((0, 32),))
    w_value = bell_draw(streams_of[4], (D, D), D ** -0.5, 0.1875, ((0, 32),))
    w_gate = bell_draw(streams_of[5], (D, D), D ** -0.5, 0.1875, ((0, 32),))
    w_output = bell_draw(streams_of[6], (D, D), (D // 16) ** -0.5, 0.75, ((0, 32),))
    ffn_gain = jnp.clip(1.0 + 0.1 * jax.random.normal(streams_of[7], (D,), jnp.float32), 0.5, 1.5).astype(jnp.bfloat16)
    w_first = bell_draw(streams_of[8], (D, FF), D ** -0.5, 0.1875, ((0, 32),))
    w_second = bell_draw(streams_of[9], (D, FF), D ** -0.5, 0.1875, ((0, 32),))
    w_down = bell_draw(streams_of[10], (FF, D), FF ** -0.5, 0.109375, ((0, 32),))
    cotangent = bell_draw(streams_of[11], (TOKENS, D), 1.0, 6.0, ((0, 32),))
    return {"tokens": tokens, "attn_gain": attn_gain, "w_query": w_query, "w_key": w_key, "w_value": w_value, "w_gate": w_gate, "w_output": w_output, "ffn_gain": ffn_gain, "w_first": w_first, "w_second": w_second, "w_down": w_down, "cotangent": cotangent}


EPS = 1e-06
HIGH = lax.Precision.HIGHEST

@jax.custom_vjp
def low(v):
    return lax.optimization_barrier(v.astype(jnp.bfloat16)).astype(jnp.float32)

@jax.custom_vjp
def low_back(v):
    return v

def low_keep(v):
    return (low(v), None)

def low_pass(kept, grad):
    return (grad,)

def back_keep(v):
    return (v, None)

def back_low(kept, grad):
    return (low(grad),)
low.defvjp(low_keep, low_pass)
low_back.defvjp(back_keep, back_low)

def matmul(left, right):
    return jnp.dot(left, right, precision=HIGH, preferred_element_type=jnp.float32)

def rms_scale(values, gain):
    return values * lax.rsqrt(lax.optimization_barrier(jnp.mean(values * values, axis=-1, keepdims=True)) + EPS) * gain

def split_heads(matrix):
    return matrix.reshape(matrix.shape[0] // BLK, BLK, HEADS, HDIM)

def block_attention(queries, keys, values):
    rows = queries.shape[0]
    raw = jnp.einsum('bqhd,bkhd->bhqk', split_heads(queries), split_heads(keys), precision=HIGH)
    scores = low_back(raw * HDIM ** (-0.5))
    causal = jnp.arange(BLK)[:, None] >= jnp.arange(BLK)[None, :]
    probs = jax.nn.softmax(jnp.where(causal, scores, -1e+30), axis=-1)
    attended = jnp.einsum('bhqk,bkhd->bqhd', low(probs), split_heads(values), precision=HIGH)
    return low_back(attended.reshape(rows, D))

def layer(params, inputs):
    attn_gain, w_query, w_key, w_value, w_gate, w_output, ffn_gain, w_first, w_second, w_down = params
    normed = low(rms_scale(inputs, attn_gain))
    queries = low(low_back(matmul(normed, w_query)))
    keys = low(low_back(matmul(normed, w_key)))
    values = low(low_back(matmul(normed, w_value)))
    gate_pre = low_back(matmul(normed, w_gate))
    attended = block_attention(queries, keys, values)
    mixed = low(low_back(attended * jax.nn.silu(gate_pre)))
    resid = inputs + low_back(matmul(mixed, w_output))
    normed_two = low(rms_scale(resid, ffn_gain))
    first = low(low_back(matmul(normed_two, w_first)))
    second = low(low_back(matmul(normed_two, w_second)))
    product = low(low_back(first * second))
    return resid + low_back(matmul(product, w_down))

def reference(tokens, attn_gain, w_query, w_key, w_value, w_gate, w_output, ffn_gain, w_first, w_second, w_down, cotangent):
    params = tuple((weight.astype(jnp.float32) for weight in (attn_gain, w_query, w_key, w_value, w_gate, w_output, ffn_gain, w_first, w_second, w_down)))
    sequences = TOKENS // SEQ
    per_step = max((count for count in range(1, max(1, 4096 // SEQ) + 1) if sequences % count == 0))
    group_rows = per_step * SEQ
    groups = TOKENS // group_rows
    inputs = tokens.astype(jnp.float32).reshape(groups, group_rows, D)
    grads_in = cotangent.astype(jnp.float32).reshape(groups, group_rows, D)

    def one_group(totals, pair):
        group_in, group_grad = pair
        outputs, pull = jax.vjp(layer, params, group_in)
        param_grads, input_grad = pull(group_grad)
        totals = jax.tree.map(jnp.add, totals, param_grads)
        return (totals, (outputs.astype(jnp.bfloat16), input_grad))
    zeros = tuple((jnp.zeros_like(weight) for weight in params))
    totals, (outputs, input_grads) = lax.scan(one_group, zeros, (inputs, grads_in))
    return (outputs.reshape(TOKENS, D), input_grads.reshape(TOKENS, D), totals[0], totals[1], totals[2], totals[3], totals[4], totals[5], totals[6], totals[7], totals[8], totals[9])
```

```python
import functools

import jax
import jax.numpy as jnp
from jax import lax
from jax.experimental import pallas as pl
from jax.experimental.pallas import tpu as pltpu
from jax.sharding import PartitionSpec as P

MESH = pl.DeviceIdType.MESH

D = 1024
HEADS = 16
HDIM = 64
FF = 2816
BLK = 64


EPS = 1e-06


def rms_scale(values, gain):
    return values * lax.rsqrt(jnp.mean(values * values, axis=-1, keepdims=True) + EPS) * gain


def gated(attended, gate_pre):
    return attended * jax.nn.silu(gate_pre)


def contract_rows(left, right):
    return lax.dot_general(
        left, right, (((0,), (0,)), ((), ())), preferred_element_type=jnp.float32
    )


def contract_cols(left, right):
    return lax.dot_general(
        left, right, (((1,), (1,)), ((), ())), preferred_element_type=jnp.float32
    )


def project(left, right):
    return jnp.dot(left, right, preferred_element_type=jnp.float32)


def flatten_rows(matrix):
    return matrix.reshape(-1, 128)


def restore_rows(flat, columns):
    return flat.reshape(-1, columns)


def split_heads(matrix):
    return matrix.reshape(matrix.shape[0] // BLK, BLK, HEADS, HDIM)


def block_scores(queries, keys):
    raw = jnp.einsum(
        "bqhd,bkhd->bhqk",
        split_heads(queries),
        split_heads(keys),
        preferred_element_type=jnp.float32,
    )
    causal = jnp.arange(BLK)[:, None] >= jnp.arange(BLK)[None, :]
    return jnp.where(causal, raw * HDIM ** (-0.5), -1e30)


def attend_forward(queries, keys, values):
    scores = block_scores(queries, keys)
    highest = jnp.max(scores, axis=-1, keepdims=True)
    weights = jnp.exp(scores - highest)
    total = jnp.sum(weights, axis=-1, keepdims=True)
    probs = (weights / total).astype(jnp.bfloat16)
    attended = jnp.einsum(
        "bhqk,bkhd->bqhd", probs, split_heads(values), preferred_element_type=jnp.float32
    )
    return (attended.reshape(queries.shape[0], D), highest + jnp.log(total))


def attend_backward(queries, keys, values, log_total, attended_grad):
    scores = block_scores(queries, keys)
    probs = jnp.exp(scores - log_total)
    grad_heads = split_heads(attended_grad)
    value_grad = jnp.einsum(
        "bhqk,bqhd->bkhd",
        probs.astype(jnp.bfloat16),
        grad_heads,
        preferred_element_type=jnp.float32,
    )
    prob_grad = jnp.einsum(
        "bqhd,bkhd->bhqk", grad_heads, split_heads(values), preferred_element_type=jnp.float32
    )
    score_grad = (probs * (prob_grad - jnp.sum(probs * prob_grad, axis=-1, keepdims=True))).astype(
        jnp.bfloat16
    )
    factor = HDIM ** (-0.5)
    query_grad = (
        jnp.einsum(
            "bhqk,bkhd->bqhd", score_grad, split_heads(keys), preferred_element_type=jnp.float32
        )
        * factor
    )
    key_grad = (
        jnp.einsum(
            "bhqk,bqhd->bkhd", score_grad, split_heads(queries), preferred_element_type=jnp.float32
        )
        * factor
    )
    length = queries.shape[0]
    return (
        query_grad.reshape(length, D).astype(jnp.bfloat16),
        key_grad.reshape(length, D).astype(jnp.bfloat16),
        value_grad.reshape(length, D).astype(jnp.bfloat16),
    )


def ag_kernel(n, *refs):
    ins = refs[:n]; outs = refs[n:2*n]
    lsem, zsend, zrecv, xsend, xrecv, ysend, yrecv, csend, crecv = refs[2*n:]
    c = lax.axis_index("dp"); f = lax.axis_index("fsdp")
    z, y, x = f // 4, (f // 2) % 2, f % 2
    fid = lambda zz, yy, xx: zz * 4 + yy * 2 + xx
    xn, yn = 1 - x, 1 - y
    bar = pltpu.get_barrier_semaphore()
    zs = [(z + k) % 4 for k in (1, 2, 3)]
    peers = [(c, fid(zz, y, x)) for zz in zs] + [(c, fid(z, y, xn)), (c, fid(z, yn, x)), (1 - c, f)]
    for p in peers:
        pl.semaphore_signal(bar, inc=1, device_id=p, device_id_type=MESH)
    pl.semaphore_wait(bar, 6)
    base = c * 16
    def rc(src, dst, ss, rs, dev):
        return pltpu.make_async_remote_copy(src_ref=src, dst_ref=dst, send_sem=ss, recv_sem=rs, device_id=dev, device_id_type=MESH)
    def cp(i, s, which):
        slot = outs[i].at[base + s]
        ss, rs, dev = {"x": (xsend, xrecv, (c, fid(z, y, xn))), "y": (ysend, yrecv, (c, fid(z, yn, x))), "c": (csend, crecv, (1 - c, f))}[which]
        return rc(slot, slot, ss.at[i, s], rs.at[i, s], dev)
    started = []
    def go(i, s, which):
        d = cp(i, s, which); d.start(); started.append(d)
    def s0(i):
        l = pltpu.make_async_copy(ins[i], outs[i].at[base + f], lsem.at[i]); l.start()
        for k in range(3):
            d = rc(ins[i], outs[i].at[base + f], zsend.at[i, k], zrecv.at[i, 2 - k], (c, fid(zs[k], y, x)))
            d.start(); started.append(d)
        l.wait()
        for w in "xyc": go(i, f, w)
    def s1(i):
        for k in (0, 2, 1):
            s = fid(zs[k], y, x)
            slot = outs[i].at[base + s]
            rc(slot, slot, zsend.at[i, k], zrecv.at[i, k], (c, f)).wait_recv()
            for w in "xyc": go(i, s, w)
    def zz_of(k): return (z + k) % 4
    def s2(i):
        for k in range(4):
            zz = zz_of(k)
            par = zz % 2
            sx, sy = fid(zz, y, xn), fid(zz, yn, x)
            cp(i, sx, "x").wait_recv()
            cp(i, sy, "y").wait_recv()
            @pl.when(par == 0)
            def _(): cp(i, sx, "y").start()
            @pl.when(par == 1)
            def _(): cp(i, sy, "x").start()
            go(i, sx, "c"); go(i, sy, "c")
    def s3(i):
        for k in range(4):
            zz = zz_of(k); par = zz % 2
            sd = fid(zz, yn, xn); sx, sy = fid(zz, y, xn), fid(zz, yn, x)
            @pl.when(par == 0)
            def _():
                cp(i, sd, "y").wait_recv(); cp(i, sx, "y").wait_send()
            @pl.when(par == 1)
            def _():
                cp(i, sd, "x").wait_recv(); cp(i, sy, "x").wait_send()
            go(i, sd, "c")
    def s4(i):
        for s in range(16):
            slot = outs[i].at[(1 - c) * 16 + s]
            rc(slot, slot, csend.at[i, s], crecv.at[i, s], (1 - c, f)).wait_recv()
    stages = [s0, s1, s2, s3, s4]
    for t in range(n + 4):
        for k, st in enumerate(stages):
            i = t - k
            if 0 <= i < n: st(i)
    for d in started: d.wait_send()

def gather_whole(ws):
    n = len(ws)
    D = pltpu.SemaphoreType.DMA
    return pl.pallas_call(
        functools.partial(ag_kernel, n),
        out_shape=[jax.ShapeDtypeStruct((32,) + w.shape, w.dtype) for w in ws],
        in_specs=[pl.BlockSpec(memory_space=pl.ANY)] * n,
        out_specs=[pl.BlockSpec(memory_space=pl.ANY)] * n,
        scratch_shapes=[D((n,)), D((n, 3)), D((n, 3)), D((n, 16)), D((n, 16)), D((n, 16)), D((n, 16)), D((n, 16)), D((n, 16))],
        compiler_params=pltpu.CompilerParams(collective_id=0, has_side_effects=True),
    )(*ws)


def on_device(
    fast,
    tokens,
    attn_gain,
    w_query,
    w_key,
    w_value,
    w_gate,
    w_output,
    ffn_gain,
    w_first,
    w_second,
    w_down,
    cotangent,
):
    weights = (w_query, w_key, w_value, w_gate, w_output, w_first, w_second, w_down)
    if fast:
        whole = [full.reshape(-1, full.shape[-1]) for full in gather_whole(weights)]
    else:
        whole = [lax.all_gather(weight, ("dp", "fsdp"), axis=0, tiled=True) for weight in weights]
    w_query, w_key, w_value, w_gate, w_output, w_first, w_second, w_down = whole
    attn_whole = (
        lax.all_gather(attn_gain, ("dp", "fsdp"), axis=0, tiled=True),
        w_query,
        w_key,
        w_value,
        w_gate,
        w_output,
    )
    gain_one, query_full, key_full, value_full, gate_full, output_full = attn_whole
    inputs = tokens.astype(jnp.float32)
    normed_pre, norm_pull = jax.vjp(rms_scale, inputs, gain_one.astype(jnp.float32))
    normed = normed_pre.astype(jnp.bfloat16)
    queries = project(normed, query_full).astype(jnp.bfloat16)
    keys = project(normed, key_full).astype(jnp.bfloat16)
    values = project(normed, value_full).astype(jnp.bfloat16)
    gate_pre = project(normed, gate_full)
    attended, log_total = attend_forward(queries, keys, values)
    mixed_pre, gate_pull = jax.vjp(gated, attended, gate_pre)
    mixed = mixed_pre.astype(jnp.bfloat16)
    resid = inputs + project(mixed, output_full)
    ffn_whole = (
        lax.all_gather(ffn_gain, ("dp", "fsdp"), axis=0, tiled=True),
        w_first,
        w_second,
        w_down,
    )
    gain_two, first_full, second_full, down_full = ffn_whole
    normed_two_pre, norm_two_pull = jax.vjp(rms_scale, resid, gain_two.astype(jnp.float32))
    normed_two = normed_two_pre.astype(jnp.bfloat16)
    first = project(normed_two, first_full).astype(jnp.bfloat16)
    second = project(normed_two, second_full).astype(jnp.bfloat16)
    product = (first.astype(jnp.float32) * second.astype(jnp.float32)).astype(jnp.bfloat16)
    block_out = (resid + project(product, down_full)).astype(jnp.bfloat16)
    gain_two, first_full, second_full, down_full = (
        lax.all_gather(ffn_gain, ("dp", "fsdp"), axis=0, tiled=True),
        w_first,
        w_second,
        w_down,
    )
    product_grad = contract_cols(cotangent, down_full).astype(jnp.bfloat16)
    product_wide = product_grad.astype(jnp.float32)
    first_grad = (product_wide * second.astype(jnp.float32)).astype(jnp.bfloat16)
    second_grad = (product_wide * first.astype(jnp.float32)).astype(jnp.bfloat16)
    normed_two_grad = contract_cols(first_grad, first_full) + contract_cols(
        second_grad, second_full
    )
    resid_part, gain_two_grad = norm_two_pull(normed_two_grad)
    resid_grad = cotangent.astype(jnp.float32) + resid_part
    down_grad = contract_rows(product, cotangent)
    first_w_grad = contract_rows(normed_two, first_grad)
    second_w_grad = contract_rows(normed_two, second_grad)
    ffn_sums = (
        lax.psum_scatter(gain_two_grad, ("dp", "fsdp"), scatter_dimension=0, tiled=True),
        lax.psum_scatter(
            flatten_rows(first_w_grad), ("dp", "fsdp"), scatter_dimension=0, tiled=True
        ),
        lax.psum_scatter(
            flatten_rows(second_w_grad), ("dp", "fsdp"), scatter_dimension=0, tiled=True
        ),
        lax.psum_scatter(flatten_rows(down_grad), ("dp", "fsdp"), scatter_dimension=0, tiled=True),
    )
    gain_one, query_full, key_full, value_full, gate_full, output_full = (
        lax.all_gather(attn_gain, ("dp", "fsdp"), axis=0, tiled=True),
        w_query,
        w_key,
        w_value,
        w_gate,
        w_output,
    )
    branch_grad = resid_grad.astype(jnp.bfloat16)
    mixed_grad = contract_cols(branch_grad, output_full).astype(jnp.bfloat16)
    attended_part, gate_part = gate_pull(mixed_grad.astype(jnp.float32))
    attended_grad = attended_part.astype(jnp.bfloat16)
    gate_grad = gate_part.astype(jnp.bfloat16)
    query_grad, key_grad, value_grad = attend_backward(
        queries, keys, values, log_total, attended_grad
    )
    normed_grad = contract_cols(query_grad, query_full) + contract_cols(key_grad, key_full)
    normed_grad = (
        normed_grad + contract_cols(value_grad, value_full) + contract_cols(gate_grad, gate_full)
    )
    input_part, gain_one_grad = norm_pull(normed_grad)
    tokens_grad = resid_grad + input_part
    output_w_grad = contract_rows(mixed, branch_grad)
    query_w_grad = contract_rows(normed, query_grad)
    key_w_grad = contract_rows(normed, key_grad)
    value_w_grad = contract_rows(normed, value_grad)
    gate_w_grad = contract_rows(normed, gate_grad)
    attn_sums = (
        lax.psum_scatter(gain_one_grad, ("dp", "fsdp"), scatter_dimension=0, tiled=True),
        lax.psum_scatter(
            flatten_rows(query_w_grad), ("dp", "fsdp"), scatter_dimension=0, tiled=True
        ),
        lax.psum_scatter(flatten_rows(key_w_grad), ("dp", "fsdp"), scatter_dimension=0, tiled=True),
        lax.psum_scatter(
            flatten_rows(value_w_grad), ("dp", "fsdp"), scatter_dimension=0, tiled=True
        ),
        lax.psum_scatter(
            flatten_rows(gate_w_grad), ("dp", "fsdp"), scatter_dimension=0, tiled=True
        ),
        lax.psum_scatter(
            flatten_rows(output_w_grad), ("dp", "fsdp"), scatter_dimension=0, tiled=True
        ),
    )
    gain_two_sum, first_flat, second_flat, down_flat = ffn_sums
    gain_one_sum, query_flat, key_flat, value_flat, gate_flat, output_flat = attn_sums
    query_sum = restore_rows(query_flat, D)
    key_sum = restore_rows(key_flat, D)
    value_sum = restore_rows(value_flat, D)
    gate_sum = restore_rows(gate_flat, D)
    output_sum = restore_rows(output_flat, D)
    first_sum = restore_rows(first_flat, FF)
    second_sum = restore_rows(second_flat, FF)
    down_sum = restore_rows(down_flat, D)
    return (
        block_out,
        tokens_grad,
        gain_one_sum,
        query_sum,
        key_sum,
        value_sum,
        gate_sum,
        output_sum,
        gain_two_sum,
        first_sum,
        second_sum,
        down_sum,
    )


def solution(mesh):
    return jax.shard_map(
        functools.partial(on_device, dict(mesh.shape) == {"dp": 2, "fsdp": 16}),
        mesh=mesh,
        in_specs=(
            P(("dp", "fsdp"), None),
            P(("dp", "fsdp")),
            P(("dp", "fsdp"), None),
            P(("dp", "fsdp"), None),
            P(("dp", "fsdp"), None),
            P(("dp", "fsdp"), None),
            P(("dp", "fsdp"), None),
            P(("dp", "fsdp")),
            P(("dp", "fsdp"), None),
            P(("dp", "fsdp"), None),
            P(("dp", "fsdp"), None),
            P(("dp", "fsdp"), None),
        ),
        out_specs=(
            P(("dp", "fsdp"), None),
            P(("dp", "fsdp"), None),
            P(("dp", "fsdp")),
            P(("dp", "fsdp"), None),
            P(("dp", "fsdp"), None),
            P(("dp", "fsdp"), None),
            P(("dp", "fsdp"), None),
            P(("dp", "fsdp"), None),
            P(("dp", "fsdp")),
            P(("dp", "fsdp"), None),
            P(("dp", "fsdp"), None),
            P(("dp", "fsdp"), None),
        ),
        check_vma=False,
    )
```

```python
import functools

import jax
import jax.numpy as jnp
from jax import lax
from jax.experimental import pallas as pl
from jax.experimental.pallas import tpu as pltpu
from jax.sharding import PartitionSpec as P

D = 1024
HEADS = 16
HDIM = 64
FF = 2816
BLK = 64


EPS = 1e-06


MESH = pl.DeviceIdType.MESH
F32, BF16 = jnp.float32, jnp.bfloat16

OWN = 256
ROWS = 512
HALF = 512
FH = 1408
CHUNKS = (
    ("d", 0, 256), ("d", 256, 256),
    ("f", 0, 768), ("f", 768, 640), ("f", 1408, 768), ("f", 2176, 640),
    ("o", 0, 512),
    ("a", 0, 512), ("a", 512, 512), ("a", 1024, 512), ("a", 1536, 512),
)
NCH = len(CHUNKS)
GROUPS = ("a", "o", "f", "s", "d")


def piece_rows(kind):
    return 176 if kind == "d" else 64


def scratch_list():
    vm, dma = pltpu.VMEM, pltpu.SemaphoreType.DMA
    items = [
        ("wa", vm((D, 4 * HALF), BF16)), ("wf", vm((D, 2 * FH), BF16)),
        ("wo", vm((HALF, D), BF16)), ("wd", vm((FH, D), BF16)), ("wds", vm((2, 88, 512), BF16)),
        ("tok", vm((ROWS, D), BF16)), ("cot", vm((ROWS, D), BF16)), ("nrm", vm((ROWS, D), BF16)),
        ("qkv", vm((ROWS, 3 * HALF), BF16)), ("gp", vm((ROWS, HALF), F32)), ("att", vm((ROWS, HALF), F32)),
        ("prob", vm((ROWS, HALF), F32)), ("mix", vm((ROWS, HALF), BF16)), ("dout", vm((ROWS, HALF), BF16)),
        ("res", vm((OWN, D), F32)), ("nt", vm((ROWS, D), BF16)), ("fs", vm((ROWS, 2 * FH), BF16)),
        ("pr", vm((ROWS, FH), BF16)), ("g4", vm((ROWS, 4 * HALF), BF16)), ("bg", vm((ROWS, D), BF16)),
        ("rg", vm((OWN, D), F32)), ("po", vm((OWN, D), F32)), ("bo", vm((OWN, D), BF16)),
        ("es", vm((4, OWN, D), BF16)), ("er", vm((4, OWN, D), BF16)),
        ("gs", vm((8, 8, D), F32)), ("gr", vm((13, 8, D), F32)), ("gacc", vm((2, 8, D), F32)),
        ("sbd", vm((2, 4, 2, 176, 256), BF16)), ("sbf", vm((2, 4, 2, 64, 768), BF16)),
    ]
    for i, (kind, _, cols) in enumerate(CHUNKS):
        r = piece_rows(kind)
        items += [
            (f"rb{i}", vm((4, 2, r, cols), BF16)), (f"ow{i}", vm((4, 2, r, cols), BF16)),
            (f"yr{i}", vm((4, r, cols), BF16)), (f"zr{i}", vm((3, r, cols), BF16)),
            (f"fin{i}", vm((r, cols), F32)),
        ]
    n = len(GROUPS)
    items += [
        ("s_loc", dma((4,))), ("s_wl", dma((n,))), ("s_xs", dma((n, 2))), ("s_xr", dma((n,))),
        ("s_es", dma((8,))), ("s_er", dma((8,))),
        ("s_zs", dma((n, 3))), ("s_zr", dma((n, 3))), ("s_ys", dma((n, 4))), ("s_yr", dma((n, 4))),
        ("s_cs", dma((n, 4, 2))), ("s_cr", dma((n, 4, 2))),
        ("s_gs", dma((2, 6))), ("s_gr", dma((2, 6))),
        ("r_cs", dma((NCH,))), ("r_cr", dma((NCH,))), ("r_ys", dma((NCH,))), ("r_yr", dma((NCH,))),
        ("r_zs", dma((NCH, 3))), ("r_zr", dma((NCH, 3))), ("r_fs", dma((NCH, 2))), ("r_fr", dma((NCH, 2))),
        ("s_out", dma((4,))),
    ]
    return items


IN_NAMES = ("tokens", "gains", "wq", "wk", "wv", "wg", "wo_in", "w1", "w2", "wd_in", "cot_in")
OUT_NAMES = ("block_out", "tokens_grad", "gain_grads", "gq", "gk", "gv", "gg", "go", "g1", "g2", "gd")


class Refs:
    def __init__(self, names, refs):
        self.__dict__.update(zip(names, refs))


def rows_of(start, count, unit=8):
    return pl.ds(pl.multiple_of(start, unit), count)


def lanes_of(start, count):
    return pl.ds(pl.multiple_of(start, 128), count)


def dot(a, b):
    return jnp.dot(a, b, preferred_element_type=F32)


def dot_t(a, b):
    return lax.dot_general(a, b, (((1,), (1,)), ((), ())), preferred_element_type=F32)


def t_dot(a, b):
    return lax.dot_general(a, b, (((0,), (0,)), ((), ())), preferred_element_type=F32)


def tile_loop(total, width, fn):
    count = total // width
    if count == 1:
        fn(0, width)
    else:
        lax.fori_loop(0, count, lambda i, u: (fn(pl.multiple_of(i * width, width), width), u)[1], 0)
    if total % width:
        fn(count * width, total % width)


def row_loop(total, step, fn):
    lax.fori_loop(0, total // step, lambda i, u: (fn(pl.multiple_of(i * step, step)), u)[1], 0)


def layer_kernel(names, *refs):
    r = Refs(names, refs)
    c = lax.axis_index("dp")
    f = lax.axis_index("fsdp")
    z, y, x = f // 4, (f // 2) % 2, f % 2

    def dev(cc, zz, yy, xx):
        return (cc, zz * 4 + yy * 2 + xx)

    xn, yn, sib, diag = dev(c, z, y, 1 - x), dev(c, z, 1 - y, x), dev(1 - c, z, y, x), dev(1 - c, z, y, 1 - x)
    zk = [(z + k) % 4 for k in range(4)]
    zp = [dev(c, zk[k], y, x) for k in range(4)]

    barrier = pltpu.get_barrier_semaphore()
    for peer in (xn, yn, sib, diag, zp[1], zp[2], zp[3]):
        pl.semaphore_signal(barrier, inc=1, device_id=peer, device_id_type=MESH)
    pl.semaphore_wait(barrier, 7)

    sends = []

    def remote(src, dst, ss, rs, to):
        return pltpu.make_async_remote_copy(
            src_ref=src, dst_ref=dst, send_sem=ss, recv_sem=rs, device_id=to, device_id_type=MESH
        )

    def send(src, dst, ss, rs, to, later=True):
        copy = remote(src, dst, ss, rs, to)
        copy.start()
        if later:
            sends.append(copy)
        return copy

    def arrived(ref, sem):
        remote(ref, ref, sem, sem, xn).wait_recv()

    def local(src, dst, sem):
        copy = pltpu.make_async_copy(src, dst, sem)
        copy.start()
        return copy

    mine = x
    p = c * 8 + z * 2 + y
    m = z * 2 + y

    def piece(g, cc, zz, yy):
        if g == "a":
            return r.wa.at[rows_of(64 * (cc * 8 + zz * 2 + yy), 64, 64), :]
        if g == "f":
            return r.wf.at[rows_of(64 * (cc * 8 + zz * 2 + yy), 64, 64), pl.ds(0, FH)]
        if g == "s":
            return r.wf.at[rows_of(64 * (cc * 8 + zz * 2 + yy), 64, 64), pl.ds(FH, FH)]
        if g == "o":
            return r.wo.at[rows_of(64 * (zz * 2 + yy), 64, 64), lanes_of(512 * cc, 512)]
        return r.wd.at[rows_of(176 * (zz * 2 + yy), 176, 16), lanes_of(512 * cc, 512)]

    def col_shard(g, who):
        row = rows_of(64 * p + 32 * who, 32, 32)
        if g == "a":
            return r.wa.at[row, :]
        return r.wf.at[row, pl.ds(0 if g == "f" else FH, FH)]

    def start_cols(g):
        gi = GROUPS.index(g)
        if g == "a":
            parts = [(w, HALF, HALF * j) for j, w in enumerate((r.wq, r.wk, r.wv, r.wg))]
            full = r.wa
        else:
            parts = [(r.w1, FH, 0)] if g == "f" else [(r.w2, FH, FH)]
            full = r.wf
        row = rows_of(64 * p + 32 * x, 32, 32)
        for w, width, at in parts:
            local(w.at[:, lanes_of(width * x, width)], full.at[row, pl.ds(at, width)], r.s_wl.at[gi])
            send(
                w.at[:, lanes_of(width * (1 - x), width)], full.at[row, pl.ds(at, width)],
                r.s_xs.at[gi, 0], r.s_xr.at[gi], xn, later=False,
            )

    def start_rows(g):
        gi = GROUPS.index(g)
        w = r.wo_in if g == "o" else r.wd_in

        def place(h):
            if g == "o":
                return r.wo.at[rows_of(64 * m + 32 * x, 32, 32), lanes_of(512 * h, 512)]
            return r.wds.at[x]

        @pl.when(x == c)
        def _():
            local(w.at[:, lanes_of(512 * c, 512)], place(c), r.s_xr.at[gi])

        @pl.when(x != c)
        def _():
            send(w.at[:, lanes_of(512 * c, 512)], place(c), r.s_xs.at[gi, 0], r.s_xr.at[gi], xn, later=False)

        send(
            w.at[:, lanes_of(512 * (1 - c), 512)], place(1 - c), r.s_xs.at[gi, 1], r.s_xr.at[gi], dev(1 - c, z, y, c),
            later=False,
        )

    def piece_ready(g):
        gi = GROUPS.index(g)
        if g in ("a", "f", "s"):
            own = col_shard(g, x)
            pltpu.make_async_copy(own, own, r.s_wl.at[gi]).wait()
            arrived(col_shard(g, 1 - x), r.s_xr.at[gi])
        elif g == "o":
            arrived(piece("o", c, z, y), r.s_xr.at[gi])
        else:
            arrived(r.wds, r.s_xr.at[gi])
            both = jnp.concatenate([r.wds[0].astype(F32), r.wds[1].astype(F32)], axis=0)
            r.wd[rows_of(176 * m, 176, 16), lanes_of(512 * c, 512)] = both.astype(BF16)

    def spread_own(g):
        gi = GROUPS.index(g)
        piece_ready(g)
        own = piece(g, c, z, y)
        for k in (1, 3, 2):
            send(own, own, r.s_zs.at[gi, k - 1], r.s_zr.at[gi, 3 - k], zp[k])
        send(own, own, r.s_ys.at[gi, 0], r.s_yr.at[gi, 0], yn)
        send(own, own, r.s_cs.at[gi, 0, 0], r.s_cr.at[gi, 0, 0], sib)

    def spread_z(g):
        gi = GROUPS.index(g)
        for k in (1, 3, 2):
            got = piece(g, c, zk[k], y)
            arrived(got, r.s_zr.at[gi, k - 1])
            send(got, got, r.s_ys.at[gi, k], r.s_yr.at[gi, k], yn)
            send(got, got, r.s_cs.at[gi, k, 0], r.s_cr.at[gi, k, 0], sib)

    def spread_y(g):
        gi = GROUPS.index(g)
        for k in (0, 1, 3, 2):
            got = piece(g, c, zk[k], 1 - y)
            arrived(got, r.s_yr.at[gi, k])
            send(got, got, r.s_cs.at[gi, k, 1], r.s_cr.at[gi, k, 1], sib)

    def whole(g):
        gi = GROUPS.index(g)
        for k in range(4):
            for j in range(2):
                arrived(piece(g, 1 - c, zk[k], y if j == 0 else 1 - y), r.s_cr.at[gi, k, j])

    def swap(i, src, dst):
        send(src, dst, r.s_es.at[i], r.s_er.at[i], xn)

    def swapped(i, dst):
        arrived(dst, r.s_er.at[i])

    def sum_small(which, first):
        base = 4 * which
        r.gs[base] = first

        def exchange(step, to, slot):
            send(r.gs.at[base + step], r.gr.at[6 * which + slot], r.s_gs.at[which, slot], r.s_gr.at[which, slot], to)

        def got(slot):
            ref = r.gr.at[6 * which + slot]
            arrived(ref, r.s_gr.at[which, slot])
            return ref[...]

        exchange(0, xn, 0)
        total = first + got(0)
        r.gs[base + 1] = total
        exchange(1, yn, 1)
        total = total + got(1)
        r.gs[base + 2] = total
        exchange(2, sib, 2)
        total = total + got(2)
        r.gs[base + 3] = total
        for k in (1, 2, 3):
            send(r.gs.at[base + 3], r.gr.at[6 * which + 2 + 4 - k], r.s_gs.at[which, 2 + k], r.s_gr.at[which, 6 - k], zp[k])
        for k in (1, 2, 3):
            total = total + got(2 + k)
        return total

    loads = [local(r.tokens, r.tok.at[pl.ds(0, OWN)], r.s_loc.at[0]), local(r.cot_in, r.cot.at[pl.ds(0, OWN)], r.s_loc.at[1])]
    gain_load = local(r.gains, r.gr.at[12], r.s_loc.at[2])
    start_cols("a")
    swap(0, r.tokens, r.tok.at[pl.ds(OWN, OWN)])
    start_rows("o")
    start_cols("f")
    start_cols("s")
    start_rows("d")
    swap(1, r.cot_in, r.cot.at[pl.ds(OWN, OWN)])

    spread_own("a")
    spread_own("o")
    gain_load.wait()
    gains = sum_small(0, r.gr[12])
    r.gr[12] = gains
    loads[0].wait()

    def norm_rows(start):
        rows = pl.ds(start, 64)
        v = r.tok[rows, :].astype(F32)
        scale = lax.rsqrt(jnp.mean(v * v, axis=-1, keepdims=True) + EPS)
        r.nrm[rows, :] = (v * scale * r.gr[12, 0:1, :]).astype(BF16)

    row_loop(OWN, 64, norm_rows)
    swapped(0, r.tok.at[pl.ds(OWN, OWN)])
    row_loop(OWN, 64, lambda s: norm_rows(s + OWN))
    spread_z("a")
    spread_own("f")
    spread_y("a")
    spread_z("o")
    whole("a")

    def proj(at, width):
        r.qkv[:, pl.ds(at, width)] = dot(r.nrm[...], r.wa[:, pl.ds(at, width)]).astype(BF16)

    def proj_gate(at, width):
        r.gp[:, pl.ds(at, width)] = dot(r.nrm[...], r.wa[:, pl.ds(3 * HALF + at, width)])

    tile_loop(3 * HALF, 256, proj)
    tile_loop(HALF, 256, proj_gate)
    spread_z("f")
    spread_own("s")
    spread_y("o")

    lane = lax.broadcasted_iota(jnp.int32, (64, 128), 1)
    row = lax.broadcasted_iota(jnp.int32, (64, 128), 0)
    left = lane < 64
    causal = (lane % 64) <= row

    def pair(v):
        zero = jnp.zeros_like(v)
        return jnp.concatenate([jnp.where(left, v, zero), jnp.where(left, zero, v)], axis=0)

    def half_sum(v):
        zero = jnp.zeros_like(v)
        a = jnp.sum(jnp.where(left, v, zero), axis=-1, keepdims=True)
        b = jnp.sum(jnp.where(left, zero, v), axis=-1, keepdims=True)
        return jnp.where(left, a, b)

    def half_max(v):
        low = jnp.full_like(v, -3e38)
        a = jnp.max(jnp.where(left, v, low), axis=-1, keepdims=True)
        b = jnp.max(jnp.where(left, low, v), axis=-1, keepdims=True)
        return jnp.where(left, a, b)

    def attend(start):
        rows = pl.ds(start, 64)
        for h in range(4):
            cols = pl.ds(128 * h, 128)
            q = r.qkv[rows, cols]
            k = r.qkv[rows, pl.ds(HALF + 128 * h, 128)]
            v = r.qkv[rows, pl.ds(2 * HALF + 128 * h, 128)]
            s = jnp.where(causal, dot_t(q, pair(k)) * HDIM ** (-0.5), -1e30)
            e = jnp.exp(s - half_max(s))
            prob = e / half_sum(e)
            r.prob[rows, cols] = prob
            att = dot(prob.astype(BF16), pair(v))
            r.att[rows, cols] = att
            g = r.gp[rows, cols]
            r.mix[rows, cols] = (att * (g * jax.nn.sigmoid(g))).astype(BF16)

    row_loop(ROWS, 64, attend)
    whole("o")

    def split_store(acc, e, at, width):
        r.po[:, pl.ds(at, width)] = acc[:OWN]
        r.es[e, :, pl.ds(at, width)] = acc[OWN:].astype(BF16)

    tile_loop(D, 256, lambda at, w: split_store(dot(r.mix[...], r.wo[:, pl.ds(at, w)]), 0, at, w))
    swap(2, r.es.at[0], r.er.at[0])
    spread_z("s")
    spread_own("d")
    spread_y("f")
    swapped(2, r.er.at[0])

    def resid_rows(start):
        rows = pl.ds(start, 64)
        v = r.tok[rows, :].astype(F32) + r.po[rows, :] + r.er[0, rows, :].astype(F32)
        r.res[rows, :] = v
        scale = lax.rsqrt(jnp.mean(v * v, axis=-1, keepdims=True) + EPS)
        r.nt[rows, :] = (v * scale * r.gr[12, 1:2, :]).astype(BF16)

    row_loop(OWN, 64, resid_rows)
    swap(3, r.nt.at[pl.ds(0, OWN)], r.nt.at[pl.ds(OWN, OWN)])
    spread_y("s")
    spread_z("d")
    whole("f")
    whole("s")
    swapped(3, r.nt.at[pl.ds(OWN, OWN)])

    def hidden(at, width):
        a = dot(r.nt[...], r.wf[:, pl.ds(at, width)]).astype(BF16)
        b = dot(r.nt[...], r.wf[:, pl.ds(FH + at, width)]).astype(BF16)
        r.fs[:, pl.ds(at, width)] = a
        r.fs[:, pl.ds(FH + at, width)] = b
        r.pr[:, pl.ds(at, width)] = (a.astype(F32) * b.astype(F32)).astype(BF16)

    tile_loop(FH, 256, hidden)
    loads[1].wait()
    swapped(1, r.cot.at[pl.ds(OWN, OWN)])

    def chunk_dot(i, cc):
        kind, at, cols = CHUNKS[i]
        if kind == "d":
            out = t_dot(r.pr[...], r.cot[:, lanes_of(512 * cc + at, cols)])
        elif kind == "f":
            out = t_dot(r.nt[:, lanes_of(512 * cc, 512)], r.fs[:, pl.ds(at, cols)])
        elif kind == "o":
            out = t_dot(r.mix[...], r.bg[:, lanes_of(512 * cc, cols)])
        else:
            out = t_dot(r.nrm[:, lanes_of(512 * cc, 512)], r.g4[:, pl.ds(at, cols)])
        return out.reshape(4, 2, piece_rows(kind), cols)

    buf = lambda name, i: getattr(r, f"{name}{i}")
    chunk_sends = {}

    def give(i):
        kind, _, cols = CHUNKS[i]
        if i >= 4 and i - 2 in chunk_sends:
            chunk_sends.pop(i - 2).wait_send()
        stage = r.sbd.at[i % 2] if kind == "d" else r.sbf.at[i % 2, :, :, :, pl.ds(0, cols)]
        stage[...] = chunk_dot(i, 1 - c).astype(BF16)
        chunk_sends[i] = send(stage, buf("rb", i), r.r_cs.at[i], r.r_cr.at[i], sib, later=False)

    def take(i):
        arrived(buf("rb", i), r.r_cr.at[i])
        own = buf("ow", i)
        own[...] = (chunk_dot(i, c) + buf("rb", i)[...].astype(F32)).astype(BF16)
        send(own.at[:, 1 - y], buf("yr", i), r.r_ys.at[i], r.r_yr.at[i], yn)

    def take_y(i):
        arrived(buf("yr", i), r.r_yr.at[i])
        own, part = buf("ow", i), buf("yr", i)
        for k in (1, 3, 2, 0):
            slot = own.at[zk[k], y]
            slot[...] = (slot[...].astype(F32) + part[zk[k]].astype(F32)).astype(BF16)
            if k:
                send(slot, buf("zr", i).at[3 - k], r.r_zs.at[i, k - 1], r.r_zr.at[i, 3 - k], zp[k])

    finals = []

    def take_z(i):
        kind, at, cols = CHUNKS[i]
        own, part, fin = buf("ow", i), buf("zr", i), buf("fin", i)
        total = own[z, y].astype(F32)
        for k in range(3):
            arrived(part.at[k], r.r_zr.at[i, k])
            total = total + part[k].astype(F32)
        fin[...] = total
        if kind in ("f", "a"):
            if kind == "f":
                out, place = (r.g1, FH * x + at) if at < FH else (r.g2, FH * x + at - FH)
            else:
                out, place = (r.gq, r.gk, r.gv, r.gg)[at // 512], HALF * x
            dst = out.at[:, lanes_of(place, cols)]
            finals.append(local(fin.at[rows_of(32 * x, 32, 32)], dst, r.r_fs.at[i, 0]))
            send(fin.at[rows_of(32 * (1 - x), 32, 32)], dst, r.r_fs.at[i, 1], r.r_fr.at[i, 0], xn)
            return
        out = r.gd if kind == "d" else r.go
        n = 88 if kind == "d" else 32
        dst = out.at[:, lanes_of(512 * c + at, cols)]
        for xx in range(2):
            src = fin.at[pl.ds(n * xx, n)]
            itself = jnp.logical_and(x == c, x == xx)

            @pl.when(itself)
            def _():
                local(src, dst, r.r_fr.at[i, c])

            @pl.when(jnp.logical_not(itself))
            def _():
                send(src, dst, r.r_fs.at[i, xx], r.r_fr.at[i, c], dev(x, z, y, xx), later=False)

    def finish(i):
        kind, at, cols = CHUNKS[i]
        if kind in ("f", "a"):
            if kind == "f":
                out, place = (r.g1, FH * (1 - x) + at) if at < FH else (r.g2, FH * (1 - x) + at - FH)
            else:
                out, place = (r.gq, r.gk, r.gv, r.gg)[at // 512], HALF * (1 - x)
            arrived(out.at[:, lanes_of(place, cols)], r.r_fr.at[i, 0])
            return
        out = r.gd if kind == "d" else r.go
        n = 88 if kind == "d" else 32
        for cc in range(2):
            arrived(out.at[:, pl.ds(512 * cc + at, cols)], r.r_fr.at[i, cc])
        for xx in range(2):
            itself = jnp.logical_and(x == c, x == xx)

            @pl.when(jnp.logical_not(itself))
            def _():
                src = buf("fin", i).at[pl.ds(n * xx, n)]
                remote(src, src, r.r_fs.at[i, xx], r.r_fs.at[i, xx], xn).wait_send()

    give(0)
    spread_y("d")
    give(1)
    take(0)
    whole("d")

    def hidden_grad(at, width):
        pg = dot_t(r.cot[...], r.wd[pl.ds(at, width), :]).astype(BF16).astype(F32)
        a = r.fs[:, pl.ds(at, width)].astype(F32)
        b = r.fs[:, pl.ds(FH + at, width)].astype(F32)
        r.fs[:, pl.ds(at, width)] = (pg * b).astype(BF16)
        r.fs[:, pl.ds(FH + at, width)] = (pg * a).astype(BF16)

    tile_loop(FH, 256, hidden_grad)
    tile_loop(D, 256, lambda at, w: split_store(dot_t(r.fs[...], r.wf[pl.ds(at, w), :]), 1, at, w))
    swap(4, r.es.at[1], r.er.at[1])
    take(1)
    give(2)
    take_y(0)
    give(3)
    take(2)
    swapped(4, r.er.at[1])
    r.gacc[...] = jnp.zeros((2, 8, D), F32)

    def resid_grad_rows(start):
        rows = pl.ds(start, 64)
        ng = r.po[rows, :] + r.er[1, rows, :].astype(F32)
        v = r.res[rows, :]
        scale = lax.rsqrt(jnp.mean(v * v, axis=-1, keepdims=True) + EPS)
        n = ng * r.gr[12, 1:2, :]
        grad = r.cot[rows, :].astype(F32) + scale * n - v * (scale * scale * scale * jnp.mean(n * v, axis=-1, keepdims=True))
        r.rg[rows, :] = grad
        r.bg[rows, :] = grad.astype(BF16)
        r.gacc[1] += jnp.sum((ng * v * scale).reshape(8, 8, D), axis=0)

    row_loop(OWN, 64, resid_grad_rows)
    swap(5, r.bg.at[pl.ds(0, OWN)], r.bg.at[pl.ds(OWN, OWN)])
    tile_loop(D, 256, lambda at, w: split_store(dot(r.pr[...], r.wd[:, pl.ds(at, w)]), 3, at, w))
    swap(6, r.es.at[3], r.er.at[3])
    take_y(1)
    give(4)
    take(3)
    take_z(0)
    swapped(5, r.bg.at[pl.ds(OWN, OWN)])

    def mixed_grad(at, width):
        cols = pl.ds(at, width)
        mg = dot_t(r.bg[...], r.wo[pl.ds(at, width), :]).astype(BF16).astype(F32)
        g = r.gp[:, cols]
        s = jax.nn.sigmoid(g)
        r.dout[:, cols] = (mg * (g * s)).astype(BF16)
        r.g4[:, pl.ds(3 * HALF + at, width)] = (mg * r.att[:, cols] * (s * (1.0 + g * (1.0 - s)))).astype(BF16)

    tile_loop(HALF, 256, mixed_grad)

    def attend_grad(start):
        rows = pl.ds(start, 64)
        for h in range(4):
            cols = pl.ds(128 * h, 128)
            q = r.qkv[rows, cols]
            k = r.qkv[rows, pl.ds(HALF + 128 * h, 128)]
            v = r.qkv[rows, pl.ds(2 * HALF + 128 * h, 128)]
            do = r.dout[rows, cols]
            prob = r.prob[rows, cols]
            vg = t_dot(prob.astype(BF16), do)
            r.g4[rows, pl.ds(2 * HALF + 128 * h, 128)] = jnp.where(left, vg[:64], vg[64:]).astype(BF16)
            pg = dot_t(do, pair(v))
            sg = (prob * (pg - half_sum(prob * pg))).astype(BF16)
            r.g4[rows, cols] = (dot(sg, pair(k)) * HDIM ** (-0.5)).astype(BF16)
            kg = t_dot(sg, q)
            r.g4[rows, pl.ds(HALF + 128 * h, 128)] = (jnp.where(left, kg[:64], kg[64:]) * HDIM ** (-0.5)).astype(BF16)

    row_loop(ROWS, 64, attend_grad)
    swapped(6, r.er.at[3])

    def block_out_rows(start):
        rows = pl.ds(start, 64)
        r.bo[rows, :] = (r.res[rows, :] + r.po[rows, :] + r.er[3, rows, :].astype(F32)).astype(BF16)

    row_loop(OWN, 64, block_out_rows)
    outs = [local(r.bo, r.block_out, r.s_out.at[0])]
    tile_loop(D, 256, lambda at, w: split_store(dot_t(r.g4[...], r.wa[pl.ds(at, w), :]), 2, at, w))
    swap(7, r.es.at[2], r.er.at[2])
    take_y(2)
    give(5)
    take(4)
    take_z(1)
    swapped(7, r.er.at[2])

    def tokens_grad_rows(start):
        rows = pl.ds(start, 64)
        ng = r.po[rows, :] + r.er[2, rows, :].astype(F32)
        v = r.tok[rows, :].astype(F32)
        scale = lax.rsqrt(jnp.mean(v * v, axis=-1, keepdims=True) + EPS)
        n = ng * r.gr[12, 0:1, :]
        r.rg[rows, :] = r.rg[rows, :] + scale * n - v * (scale * scale * scale * jnp.mean(n * v, axis=-1, keepdims=True))
        r.gacc[0] += jnp.sum((ng * v * scale).reshape(8, 8, D), axis=0)

    row_loop(OWN, 64, tokens_grad_rows)
    outs.append(local(r.rg, r.tokens_grad, r.s_out.at[1]))
    take_y(3)
    give(6)
    take(5)
    for i in range(7, NCH + 4):
        if i < NCH:
            give(i)
        if i - 1 < NCH:
            take(i - 1)
        if 0 <= i - 3 < NCH:
            take_y(i - 3)
        if 0 <= i - 5 < NCH:
            take_z(i - 5)
        if i == NCH:
            which = lax.broadcasted_iota(jnp.int32, (8, D), 0)
            a = jnp.sum(r.gacc[0], axis=0, keepdims=True)
            b = jnp.sum(r.gacc[1], axis=0, keepdims=True)
            zero = jnp.zeros((8, D), F32)
            total = sum_small(1, jnp.where(which == 0, a, zero) + jnp.where(which == 1, b, zero))
            r.gacc[0] = total
            outs.append(local(r.gacc.at[0], r.gain_grads, r.s_out.at[2]))
    take_z(NCH - 1)
    for i in range(NCH):
        finish(i)
    for copy in list(chunk_sends.values()) + sends:
        copy.wait_send()
    for copy in finals + outs:
        copy.wait()
    for g in ("a", "f", "s"):
        gi = GROUPS.index(g)
        own = col_shard(g, x)
        remote(own, own, r.s_xs.at[gi, 0], r.s_xs.at[gi, 0], xn).wait_send()
    for g in ("o", "d"):
        gi = GROUPS.index(g)
        block = r.wo.at[pl.ds(0, 32), pl.ds(0, 512)] if g == "o" else r.wds.at[0]

        @pl.when(x != c)
        def _():
            remote(block, block, r.s_xs.at[gi, 0], r.s_xs.at[gi, 0], xn).wait_send()

        remote(block, block, r.s_xs.at[gi, 1], r.s_xs.at[gi, 1], xn).wait_send()


def fused_layer(
    tokens, attn_gain, w_query, w_key, w_value, w_gate, w_output, ffn_gain, w_first, w_second, w_down, cotangent
):
    me = lax.axis_index("dp") * 16 + lax.axis_index("fsdp")
    lane = lax.broadcasted_iota(jnp.int32, (8, D), 1)
    row = lax.broadcasted_iota(jnp.int32, (8, D), 0)
    mine = lane // 32 == me
    spread = lambda gain: jnp.tile(gain.astype(F32), 32)[None, :]
    gains = jnp.where(mine & (row == 0), spread(attn_gain), 0.0) + jnp.where(mine & (row == 1), spread(ffn_gain), 0.0)
    items = scratch_list()
    names = IN_NAMES + OUT_NAMES + tuple(name for name, _ in items)
    shape = jax.ShapeDtypeStruct
    outs = pl.pallas_call(
        functools.partial(layer_kernel, names),
        out_shape=[
            shape((OWN, D), BF16), shape((OWN, D), F32), shape((8, D), F32),
            shape((32, D), F32), shape((32, D), F32), shape((32, D), F32), shape((32, D), F32), shape((32, D), F32),
            shape((32, FF), F32), shape((32, FF), F32), shape((88, D), F32),
        ],
        in_specs=[pl.BlockSpec(memory_space=pl.ANY)] * len(IN_NAMES),
        out_specs=[pl.BlockSpec(memory_space=pl.ANY)] * len(OUT_NAMES),
        scratch_shapes=[spec for _, spec in items],
        compiler_params=pltpu.CompilerParams(collective_id=0, has_side_effects=True, vmem_limit_bytes=66 * 2**20 - 2**21),
        name="layer",
    )(tokens, gains, w_query, w_key, w_value, w_gate, w_output, w_first, w_second, w_down, cotangent)
    block_out, tokens_grad, gain_grads, gq, gk, gv, gg, go, g1, g2, gd = outs
    own = lax.dynamic_slice(gain_grads, (0, me * 32), (8, 32))
    return block_out, tokens_grad, own[0], gq, gk, gv, gg, go, own[1], g1, g2, gd


def rms_scale(values, gain):
    return values * lax.rsqrt(jnp.mean(values * values, axis=-1, keepdims=True) + EPS) * gain


def gated(attended, gate_pre):
    return attended * jax.nn.silu(gate_pre)


def contract_rows(left, right):
    return lax.dot_general(
        left, right, (((0,), (0,)), ((), ())), preferred_element_type=jnp.float32
    )


def contract_cols(left, right):
    return lax.dot_general(
        left, right, (((1,), (1,)), ((), ())), preferred_element_type=jnp.float32
    )


def project(left, right):
    return jnp.dot(left, right, preferred_element_type=jnp.float32)


def flatten_rows(matrix):
    return matrix.reshape(-1, 128)


def restore_rows(flat, columns):
    return flat.reshape(-1, columns)


def split_heads(matrix):
    return matrix.reshape(matrix.shape[0] // BLK, BLK, HEADS, HDIM)


def block_scores(queries, keys):
    raw = jnp.einsum(
        "bqhd,bkhd->bhqk",
        split_heads(queries),
        split_heads(keys),
        preferred_element_type=jnp.float32,
    )
    causal = jnp.arange(BLK)[:, None] >= jnp.arange(BLK)[None, :]
    return jnp.where(causal, raw * HDIM ** (-0.5), -1e30)


def attend_forward(queries, keys, values):
    scores = block_scores(queries, keys)
    highest = jnp.max(scores, axis=-1, keepdims=True)
    weights = jnp.exp(scores - highest)
    total = jnp.sum(weights, axis=-1, keepdims=True)
    probs = (weights / total).astype(jnp.bfloat16)
    attended = jnp.einsum(
        "bhqk,bkhd->bqhd", probs, split_heads(values), preferred_element_type=jnp.float32
    )
    return (attended.reshape(queries.shape[0], D), highest + jnp.log(total))


def attend_backward(queries, keys, values, log_total, attended_grad):
    scores = block_scores(queries, keys)
    probs = jnp.exp(scores - log_total)
    grad_heads = split_heads(attended_grad)
    value_grad = jnp.einsum(
        "bhqk,bqhd->bkhd",
        probs.astype(jnp.bfloat16),
        grad_heads,
        preferred_element_type=jnp.float32,
    )
    prob_grad = jnp.einsum(
        "bqhd,bkhd->bhqk", grad_heads, split_heads(values), preferred_element_type=jnp.float32
    )
    score_grad = (probs * (prob_grad - jnp.sum(probs * prob_grad, axis=-1, keepdims=True))).astype(
        jnp.bfloat16
    )
    factor = HDIM ** (-0.5)
    query_grad = (
        jnp.einsum(
            "bhqk,bkhd->bqhd", score_grad, split_heads(keys), preferred_element_type=jnp.float32
        )
        * factor
    )
    key_grad = (
        jnp.einsum(
            "bhqk,bqhd->bkhd", score_grad, split_heads(queries), preferred_element_type=jnp.float32
        )
        * factor
    )
    length = queries.shape[0]
    return (
        query_grad.reshape(length, D).astype(jnp.bfloat16),
        key_grad.reshape(length, D).astype(jnp.bfloat16),
        value_grad.reshape(length, D).astype(jnp.bfloat16),
    )


def on_device(
    tokens,
    attn_gain,
    w_query,
    w_key,
    w_value,
    w_gate,
    w_output,
    ffn_gain,
    w_first,
    w_second,
    w_down,
    cotangent,
):
    attn_whole = (
        lax.all_gather(attn_gain, ("dp", "fsdp"), axis=0, tiled=True),
        lax.all_gather(w_query, ("dp", "fsdp"), axis=0, tiled=True),
        lax.all_gather(w_key, ("dp", "fsdp"), axis=0, tiled=True),
        lax.all_gather(w_value, ("dp", "fsdp"), axis=0, tiled=True),
        lax.all_gather(w_gate, ("dp", "fsdp"), axis=0, tiled=True),
        lax.all_gather(w_output, ("dp", "fsdp"), axis=0, tiled=True),
    )
    gain_one, query_full, key_full, value_full, gate_full, output_full = attn_whole
    inputs = tokens.astype(jnp.float32)
    normed_pre, norm_pull = jax.vjp(rms_scale, inputs, gain_one.astype(jnp.float32))
    normed = normed_pre.astype(jnp.bfloat16)
    queries = project(normed, query_full).astype(jnp.bfloat16)
    keys = project(normed, key_full).astype(jnp.bfloat16)
    values = project(normed, value_full).astype(jnp.bfloat16)
    gate_pre = project(normed, gate_full)
    attended, log_total = attend_forward(queries, keys, values)
    mixed_pre, gate_pull = jax.vjp(gated, attended, gate_pre)
    mixed = mixed_pre.astype(jnp.bfloat16)
    resid = inputs + project(mixed, output_full)
    ffn_whole = (
        lax.all_gather(ffn_gain, ("dp", "fsdp"), axis=0, tiled=True),
        lax.all_gather(w_first, ("dp", "fsdp"), axis=0, tiled=True),
        lax.all_gather(w_second, ("dp", "fsdp"), axis=0, tiled=True),
        lax.all_gather(w_down, ("dp", "fsdp"), axis=0, tiled=True),
    )
    gain_two, first_full, second_full, down_full = ffn_whole
    normed_two_pre, norm_two_pull = jax.vjp(rms_scale, resid, gain_two.astype(jnp.float32))
    normed_two = normed_two_pre.astype(jnp.bfloat16)
    first = project(normed_two, first_full).astype(jnp.bfloat16)
    second = project(normed_two, second_full).astype(jnp.bfloat16)
    product = (first.astype(jnp.float32) * second.astype(jnp.float32)).astype(jnp.bfloat16)
    block_out = (resid + project(product, down_full)).astype(jnp.bfloat16)
    gain_two, first_full, second_full, down_full = (
        lax.all_gather(ffn_gain, ("dp", "fsdp"), axis=0, tiled=True),
        lax.all_gather(w_first, ("dp", "fsdp"), axis=0, tiled=True),
        lax.all_gather(w_second, ("dp", "fsdp"), axis=0, tiled=True),
        lax.all_gather(w_down, ("dp", "fsdp"), axis=0, tiled=True),
    )
    product_grad = contract_cols(cotangent, down_full).astype(jnp.bfloat16)
    product_wide = product_grad.astype(jnp.float32)
    first_grad = (product_wide * second.astype(jnp.float32)).astype(jnp.bfloat16)
    second_grad = (product_wide * first.astype(jnp.float32)).astype(jnp.bfloat16)
    normed_two_grad = contract_cols(first_grad, first_full) + contract_cols(
        second_grad, second_full
    )
    resid_part, gain_two_grad = norm_two_pull(normed_two_grad)
    resid_grad = cotangent.astype(jnp.float32) + resid_part
    down_grad = contract_rows(product, cotangent)
    first_w_grad = contract_rows(normed_two, first_grad)
    second_w_grad = contract_rows(normed_two, second_grad)
    ffn_sums = (
        lax.psum_scatter(gain_two_grad, ("dp", "fsdp"), scatter_dimension=0, tiled=True),
        lax.psum_scatter(
            flatten_rows(first_w_grad), ("dp", "fsdp"), scatter_dimension=0, tiled=True
        ),
        lax.psum_scatter(
            flatten_rows(second_w_grad), ("dp", "fsdp"), scatter_dimension=0, tiled=True
        ),
        lax.psum_scatter(flatten_rows(down_grad), ("dp", "fsdp"), scatter_dimension=0, tiled=True),
    )
    gain_one, query_full, key_full, value_full, gate_full, output_full = (
        lax.all_gather(attn_gain, ("dp", "fsdp"), axis=0, tiled=True),
        lax.all_gather(w_query, ("dp", "fsdp"), axis=0, tiled=True),
        lax.all_gather(w_key, ("dp", "fsdp"), axis=0, tiled=True),
        lax.all_gather(w_value, ("dp", "fsdp"), axis=0, tiled=True),
        lax.all_gather(w_gate, ("dp", "fsdp"), axis=0, tiled=True),
        lax.all_gather(w_output, ("dp", "fsdp"), axis=0, tiled=True),
    )
    branch_grad = resid_grad.astype(jnp.bfloat16)
    mixed_grad = contract_cols(branch_grad, output_full).astype(jnp.bfloat16)
    attended_part, gate_part = gate_pull(mixed_grad.astype(jnp.float32))
    attended_grad = attended_part.astype(jnp.bfloat16)
    gate_grad = gate_part.astype(jnp.bfloat16)
    query_grad, key_grad, value_grad = attend_backward(
        queries, keys, values, log_total, attended_grad
    )
    normed_grad = contract_cols(query_grad, query_full) + contract_cols(key_grad, key_full)
    normed_grad = (
        normed_grad + contract_cols(value_grad, value_full) + contract_cols(gate_grad, gate_full)
    )
    input_part, gain_one_grad = norm_pull(normed_grad)
    tokens_grad = resid_grad + input_part
    output_w_grad = contract_rows(mixed, branch_grad)
    query_w_grad = contract_rows(normed, query_grad)
    key_w_grad = contract_rows(normed, key_grad)
    value_w_grad = contract_rows(normed, value_grad)
    gate_w_grad = contract_rows(normed, gate_grad)
    attn_sums = (
        lax.psum_scatter(gain_one_grad, ("dp", "fsdp"), scatter_dimension=0, tiled=True),
        lax.psum_scatter(
            flatten_rows(query_w_grad), ("dp", "fsdp"), scatter_dimension=0, tiled=True
        ),
        lax.psum_scatter(flatten_rows(key_w_grad), ("dp", "fsdp"), scatter_dimension=0, tiled=True),
        lax.psum_scatter(
            flatten_rows(value_w_grad), ("dp", "fsdp"), scatter_dimension=0, tiled=True
        ),
        lax.psum_scatter(
            flatten_rows(gate_w_grad), ("dp", "fsdp"), scatter_dimension=0, tiled=True
        ),
        lax.psum_scatter(
            flatten_rows(output_w_grad), ("dp", "fsdp"), scatter_dimension=0, tiled=True
        ),
    )
    gain_two_sum, first_flat, second_flat, down_flat = ffn_sums
    gain_one_sum, query_flat, key_flat, value_flat, gate_flat, output_flat = attn_sums
    query_sum = restore_rows(query_flat, D)
    key_sum = restore_rows(key_flat, D)
    value_sum = restore_rows(value_flat, D)
    gate_sum = restore_rows(gate_flat, D)
    output_sum = restore_rows(output_flat, D)
    first_sum = restore_rows(first_flat, FF)
    second_sum = restore_rows(second_flat, FF)
    down_sum = restore_rows(down_flat, D)
    return (
        block_out,
        tokens_grad,
        gain_one_sum,
        query_sum,
        key_sum,
        value_sum,
        gate_sum,
        output_sum,
        gain_two_sum,
        first_sum,
        second_sum,
        down_sum,
    )


def solution(mesh):
    fits = dict(mesh.shape) == {"dp": 2, "fsdp": 16}
    return jax.shard_map(
        fused_layer if fits else on_device,
        mesh=mesh,
        in_specs=(
            P(("dp", "fsdp"), None),
            P(("dp", "fsdp")),
            P(("dp", "fsdp"), None),
            P(("dp", "fsdp"), None),
            P(("dp", "fsdp"), None),
            P(("dp", "fsdp"), None),
            P(("dp", "fsdp"), None),
            P(("dp", "fsdp")),
            P(("dp", "fsdp"), None),
            P(("dp", "fsdp"), None),
            P(("dp", "fsdp"), None),
            P(("dp", "fsdp"), None),
        ),
        out_specs=(
            P(("dp", "fsdp"), None),
            P(("dp", "fsdp"), None),
            P(("dp", "fsdp")),
            P(("dp", "fsdp"), None),
            P(("dp", "fsdp"), None),
            P(("dp", "fsdp"), None),
            P(("dp", "fsdp"), None),
            P(("dp", "fsdp"), None),
            P(("dp", "fsdp")),
            P(("dp", "fsdp"), None),
            P(("dp", "fsdp"), None),
            P(("dp", "fsdp"), None),
        ),
        check_vma=False,
    )
```

```python
import functools

import jax
import jax.numpy as jnp
from jax import lax
from jax.experimental import pallas as pl
from jax.experimental.pallas import tpu as pltpu
from jax.sharding import PartitionSpec as P

D = 1024
HEADS = 16
HDIM = 64
FF = 2816
BLK = 64


EPS = 1e-06


MESH = pl.DeviceIdType.MESH
F32, BF16 = jnp.float32, jnp.bfloat16

OWN = 256
ROWS = 512
HALF = 512
FH = 1408
CHUNKS = (
    ("d", 0, 256), ("d", 256, 256),
    ("f", 0, 768), ("f", 768, 640), ("f", 1408, 768), ("f", 2176, 640),
    ("o", 0, 512),
    ("a", 1536, 512), ("a", 1024, 512), ("a", 512, 512), ("a", 0, 512),
)
NCH = len(CHUNKS)
Z_FIRST = tuple(i in (1, 7,) for i in range(NCH))
Y_FIRST = ("d",)
GROUPS = ("a", "b", "o", "f", "s", "d")
GA, GB, GO, GF, GS, GD = GROUPS


def piece_rows(kind):
    return 176 if kind == "d" else 64


def scratch_list():
    vm, dma = pltpu.VMEM, pltpu.SemaphoreType.DMA
    items = [
        ("wa", vm((D, 4 * HALF + 128), BF16)), ("wf", vm((D, 2 * FH), BF16)),
        ("wo", vm((HALF, D), BF16)), ("wd", vm((FH, D), BF16)), ("wds", vm((2, 88, 512), BF16)),
        ("tok", vm((ROWS, D), BF16)), ("cot", vm((ROWS, D), BF16)), ("nrm", vm((ROWS, D), BF16)),
        ("qkv", vm((ROWS, 3 * HALF), BF16)), ("gp", vm((ROWS, HALF), F32)), ("att", vm((ROWS, HALF), F32)),
        ("prob", vm((ROWS, HALF), F32)), ("mix", vm((ROWS, HALF), BF16)), ("dout", vm((ROWS, HALF), BF16)),
        ("res", vm((OWN, D), F32)), ("nt", vm((ROWS, D), BF16)), ("fs", vm((ROWS, 2 * FH), BF16)),
        ("pr", vm((ROWS, FH), BF16)), ("g4", vm((ROWS, 4 * HALF), BF16)), ("bg", vm((ROWS, D), BF16)),
        ("rg", vm((OWN, D), F32)), ("po", vm((OWN, D), F32)), ("bo", vm((OWN, D), BF16)),
        ("es", vm((3, OWN, D), BF16)), ("er", vm((3, OWN, D), BF16)),
        ("gs", vm((4, 8, D), F32)), ("gr", vm((6, 8, D), F32)), ("gain", vm((8, D), F32)), ("gacc", vm((2, 8, D), F32)),
        ("sbd", vm((2, 4, 2, 176, 256), BF16)), ("sbf", vm((2, 4, 2, 64, 768), BF16)),
    ]
    for i, (kind, _, cols) in enumerate(CHUNKS):
        r = piece_rows(kind)
        items += [
            (f"rb{i}", vm((4, 2, r, cols), BF16)), (f"ow{i}", vm((4, 2, r, cols), BF16)),
            (f"yr{i}", vm((r, cols) if Z_FIRST[i] else (4, r, cols), BF16)),
            (f"zr{i}", vm((3, 2, r, cols) if Z_FIRST[i] else (3, r, cols), BF16)),
            (f"zx{i}", vm((2, r, cols) if Z_FIRST[i] else (r, cols), BF16)),
            (f"fin{i}", vm((r, cols), F32)),
        ]
    n = len(GROUPS)
    items += [
        ("s_loc", dma((4,))), ("s_wl", dma((n,))), ("s_xs", dma((n, 2))), ("s_xr", dma((n,))),
        ("s_es", dma((16,))), ("s_er", dma((16,))),
        ("s_zs", dma((n, 2, 5))), ("s_zr", dma((n, 2, 3))), ("s_ys", dma((n, 4))), ("s_yr", dma((n, 4))),
        ("s_cs", dma((n, 4, 2))), ("s_cr", dma((n, 4, 2))),
        ("s_gs", dma((6,))), ("s_gr", dma((6,))),
        ("r_cs", dma((NCH,))), ("r_cr", dma((NCH,))), ("r_ys", dma((NCH,))), ("r_yr", dma((NCH,))),
        ("r_zs", dma((NCH, 3))), ("r_zr", dma((NCH, 3))), ("r_zx", dma((NCH,))), ("r_zt", dma((NCH,))), ("r_fs", dma((NCH, 2))), ("r_fr", dma((NCH, 2))),
        ("s_out", dma((4,))),
    ]
    return items


IN_NAMES = ("tokens", "gains", "wq", "wk", "wv", "wg", "wo_in", "w1", "w2", "wd_in", "cot_in")
OUT_NAMES = ("block_out", "tokens_grad", "gain_grads", "gq", "gk", "gv", "gg", "go", "g1", "g2", "gd")


class Refs:
    def __init__(self, names, refs):
        self.__dict__.update(zip(names, refs))


def rows_of(start, count, unit=8):
    return pl.ds(pl.multiple_of(start, unit), count)


def lanes_of(start, count):
    return pl.ds(pl.multiple_of(start, 128), count)


def dot(a, b):
    return jnp.dot(a, b, preferred_element_type=F32)


def dot_t(a, b):
    return lax.dot_general(a, b, (((1,), (1,)), ((), ())), preferred_element_type=F32)


def t_dot(a, b):
    return lax.dot_general(a, b, (((0,), (0,)), ((), ())), preferred_element_type=F32)


def tile_loop(total, width, fn):
    count = total // width
    if count == 1:
        fn(0, width)
    else:
        lax.fori_loop(0, count, lambda i, u: (fn(pl.multiple_of(i * width, width), width), u)[1], 0)
    if total % width:
        fn(count * width, total % width)


def row_loop(total, step, fn):
    lax.fori_loop(0, total // step, lambda i, u: (fn(pl.multiple_of(i * step, step)), u)[1], 0)


def layer_kernel(names, *refs):
    r = Refs(names, refs)
    c = lax.axis_index("dp")
    f = lax.axis_index("fsdp")
    z, y, x = f // 4, (f // 2) % 2, f % 2

    def dev(cc, zz, yy, xx):
        return (cc, zz * 4 + yy * 2 + xx)

    xn, yn, sib, diag = dev(c, z, y, 1 - x), dev(c, z, 1 - y, x), dev(1 - c, z, y, x), dev(1 - c, z, y, 1 - x)
    zk = [(z + k) % 4 for k in range(4)]
    zp = [dev(c, zk[k], y, x) for k in range(4)]

    barrier = pltpu.get_barrier_semaphore()
    for peer in (xn, yn, sib, diag, zp[1], zp[2], zp[3]):
        pl.semaphore_signal(barrier, inc=1, device_id=peer, device_id_type=MESH)
    pl.semaphore_wait(barrier, 7)

    sends, guarded = [], []
    inner = jnp.logical_and(z != 0, z != 3)

    def remote(src, dst, ss, rs, to):
        return pltpu.make_async_remote_copy(
            src_ref=src, dst_ref=dst, send_sem=ss, recv_sem=rs, device_id=to, device_id_type=MESH
        )

    def send(src, dst, ss, rs, to, later=True):
        copy = remote(src, dst, ss, rs, to)
        copy.start()
        if later:
            sends.append(copy)
        return copy

    def send_if(pred, src, dst, ss, rs, to):
        copy = remote(src, dst, ss, rs, to)
        pl.when(pred)(copy.start)
        guarded.append((pred, copy))

    def arrived(ref, sem):
        remote(ref, ref, sem, sem, xn).wait_recv()

    def local(src, dst, sem):
        copy = pltpu.make_async_copy(src, dst, sem)
        copy.start()
        return copy

    mine = x
    p = c * 8 + z * 2 + y
    m = z * 2 + y

    def piece(g, cc, zz, yy):
        if g in "ab":
            cols = pl.ds(0, 1024) if g == "a" else pl.ds(1024, 1024 + 128)
            return r.wa.at[rows_of(64 * (cc * 8 + zz * 2 + yy), 64, 64), cols]
        if g == "f":
            return r.wf.at[rows_of(64 * (cc * 8 + zz * 2 + yy), 64, 64), pl.ds(0, FH)]
        if g == "s":
            return r.wf.at[rows_of(64 * (cc * 8 + zz * 2 + yy), 64, 64), pl.ds(FH, FH)]
        if g == "o":
            return r.wo.at[rows_of(64 * (zz * 2 + yy), 64, 64), lanes_of(512 * cc, 512)]
        return r.wd.at[rows_of(176 * (zz * 2 + yy), 176, 16), lanes_of(512 * cc, 512)]

    def col_shard(g, who):
        row = rows_of(64 * p + 32 * who, 32, 32)
        if g in "ab":
            return r.wa.at[row, pl.ds(0, 1024) if g == "a" else pl.ds(1024, 1024 + 128)]
        return r.wf.at[row, pl.ds(0 if g == "f" else FH, FH)]

    def start_cols(g):
        gi = GROUPS.index(g)
        if g in "ab":
            first = 0 if g == "a" else 2
            parts = [(w, HALF, HALF * j) for j, w in enumerate((r.wq, r.wk, r.wv, r.wg))][first : first + 2]
            full = r.wa
        else:
            parts = [(r.w1, FH, 0)] if g == "f" else [(r.w2, FH, FH)]
            full = r.wf
        row = rows_of(64 * p + 32 * x, 32, 32)
        if g == "b":
            local(r.gains, full.at[row, pl.ds(4 * HALF, 128)], r.s_wl.at[gi])
            send(r.gains, full.at[row, pl.ds(4 * HALF, 128)], r.s_xs.at[gi, 0], r.s_xr.at[gi], xn, later=False)
        for w, width, at in parts:
            local(w.at[:, lanes_of(width * x, width)], full.at[row, pl.ds(at, width)], r.s_wl.at[gi])
            send(
                w.at[:, lanes_of(width * (1 - x), width)], full.at[row, pl.ds(at, width)],
                r.s_xs.at[gi, 0], r.s_xr.at[gi], xn, later=False,
            )

    def start_rows(g):
        gi = GROUPS.index(g)
        w = r.wo_in if g == "o" else r.wd_in

        def place(h):
            if g == "o":
                return r.wo.at[rows_of(64 * m + 32 * x, 32, 32), lanes_of(512 * h, 512)]
            return r.wds.at[x]

        @pl.when(x == c)
        def _():
            local(w.at[:, lanes_of(512 * c, 512)], place(c), r.s_xr.at[gi])

        @pl.when(x != c)
        def _():
            send(w.at[:, lanes_of(512 * c, 512)], place(c), r.s_xs.at[gi, 0], r.s_xr.at[gi], xn, later=False)

        send(
            w.at[:, lanes_of(512 * (1 - c), 512)], place(1 - c), r.s_xs.at[gi, 1], r.s_xr.at[gi], dev(1 - c, z, y, c),
            later=False,
        )

    def piece_ready(g):
        gi = GROUPS.index(g)
        if g in "abfs":
            own = col_shard(g, x)
            pltpu.make_async_copy(own, own, r.s_wl.at[gi]).wait()
            arrived(col_shard(g, 1 - x), r.s_xr.at[gi])
        elif g == "o":
            arrived(piece("o", c, z, y), r.s_xr.at[gi])
        else:
            arrived(r.wds, r.s_xr.at[gi])
            both = jnp.concatenate([r.wds[0].astype(F32), r.wds[1].astype(F32)], axis=0)
            r.wd[rows_of(176 * m, 176, 16), lanes_of(512 * c, 512)] = both.astype(BF16)

    near = [
        jnp.where(z < 2, 1, 3),
        jnp.where(z == 1, 3, jnp.where(z == 2, 1, 2)),
        jnp.where(z == 0, 3, jnp.where(z == 3, 1, 2)),
    ]

    def near_z(n):
        return z if n == 0 else lax.rem(z + near[n - 1], 4)

    def up_down(g, yy, j):
        gi = GROUPS.index(g)
        own = piece(g, c, z, yy)
        send_if(z < 3, own, own, r.s_zs.at[gi, j, 0], r.s_zr.at[gi, j, 2], zp[1])
        send_if(z > 0, own, own, r.s_zs.at[gi, j, 1], r.s_zr.at[gi, j, 0], zp[3])

    def across(g, n):
        gi = GROUPS.index(g)
        ref = piece(g, c, near_z(n), y)
        send(ref, ref, r.s_ys.at[gi, n], r.s_yr.at[gi, n], yn)

    def to_core(g, n, j):
        gi = GROUPS.index(g)
        ref = piece(g, c, near_z(n), y if j == 0 else 1 - y)
        send(ref, ref, r.s_cs.at[gi, n, j], r.s_cr.at[gi, n, j], sib)

    def own(g):
        piece_ready(g)
        if g in Y_FIRST:
            across(g, 0)
            up_down(g, y, 0)
        else:
            up_down(g, y, 0)
            across(g, 0)
        to_core(g, 0, 0)

    def got_z(g, n, j=0):
        gi = GROUPS.index(g)
        got = piece(g, c, near_z(n), y if j == 0 else 1 - y)
        arrived(got, r.s_zr.at[gi, j, near[n - 1] - 1])
        src = near_z(n)
        to = jnp.where(src > z, z - 1, z + 1)
        slot = lax.rem(src - to + 4, 4) - 1
        send_if(inner, got, got, r.s_zs.at[gi, j, 1 + n], r.s_zr.at[gi, j, slot], dev(c, to, y, x))
        if g not in Y_FIRST:
            across(g, n)
        to_core(g, n, j)

    def got_y(g, n):
        gi = GROUPS.index(g)
        arrived(piece(g, c, near_z(n), 1 - y), r.s_yr.at[gi, n])
        if g in Y_FIRST:
            up_down(g, 1 - y, 1)
        to_core(g, n, 1)

    def spread_z(g):
        for j in range(2 if g in Y_FIRST else 1):
            for n in (1, 2, 3):
                got_z(g, n, j)

    def spread_y(g):
        for n in range(1 if g in Y_FIRST else 4):
            got_y(g, n)

    def whole(g):
        gi = GROUPS.index(g)
        for k in range(4):
            for j in range(2):
                arrived(piece(g, 1 - c, near_z(k), y if j == 0 else 1 - y), r.s_cr.at[gi, k, j])

    swaps = {}

    def swap(i, src, dst):
        swaps[i] = send(src, dst, r.s_es.at[i], r.s_er.at[i], xn, later=False)

    def swapped(i, dst):
        arrived(dst, r.s_er.at[i])

    def grad_sum(n, value=None):
        def out(slot, to):
            send(r.gs.at[min(slot, 3)], r.gr.at[slot], r.s_gs.at[slot], r.s_gr.at[slot], to)

        def got(slot):
            arrived(r.gr.at[slot], r.s_gr.at[slot])
            return r.gr[slot]

        if n == 0:
            r.gs[0] = value
            out(0, xn)
        elif n < 3:
            r.gs[n] = r.gs[n - 1] + got(n - 1)
            out(n, yn if n == 1 else sib)
        elif n == 3:
            r.gs[3] = r.gs[2] + got(2)
            for k in (1, 2, 3):
                send(r.gs.at[3], r.gr.at[6 - k], r.s_gs.at[2 + k], r.s_gr.at[6 - k], zp[k])
        else:
            return r.gs[3] + (got(3) + got(4) + got(5))

    def norm_rows(start, at, out):
        v = r.tok[pl.ds(start + at, 64), :].astype(F32)
        scale = lax.rsqrt(jnp.mean(v * v, axis=-1, keepdims=True) + EPS)
        out[pl.ds(start, 64), :] = v * scale

    def gain_rows(start):
        rows = pl.ds(start, 64)
        r.nrm[rows, :] = (r.po[rows, :] * r.gain[0:1, :]).astype(BF16)
        r.nrm[pl.ds(start + OWN, 64), :] = (r.rg[rows, :] * r.gain[0:1, :]).astype(BF16)

    def proj(at, width):
        r.qkv[:, pl.ds(at, width)] = dot(r.nrm[...], r.wa[:, pl.ds(at, width)]).astype(BF16)

    def proj_gate(at, width):
        r.gp[:, pl.ds(at, width)] = dot(r.nrm[...], r.wa[:, pl.ds(3 * HALF + at, width)])

    lane = lax.broadcasted_iota(jnp.int32, (64, 128), 1)
    row = lax.broadcasted_iota(jnp.int32, (64, 128), 0)
    left = lane < 64
    causal = (lane % 64) <= row

    def pair(v):
        zero = jnp.zeros_like(v)
        return jnp.concatenate([jnp.where(left, v, zero), jnp.where(left, zero, v)], axis=0)

    def half_sum(v):
        zero = jnp.zeros_like(v)
        a = jnp.sum(jnp.where(left, v, zero), axis=-1, keepdims=True)
        b = jnp.sum(jnp.where(left, zero, v), axis=-1, keepdims=True)
        return jnp.where(left, a, b)

    def half_max(v):
        low = jnp.full_like(v, -3e38)
        a = jnp.max(jnp.where(left, v, low), axis=-1, keepdims=True)
        b = jnp.max(jnp.where(left, low, v), axis=-1, keepdims=True)
        return jnp.where(left, a, b)

    def attend(start):
        rows = pl.ds(start, 64)
        for h in range(4):
            cols = pl.ds(128 * h, 128)
            q = r.qkv[rows, cols]
            k = r.qkv[rows, pl.ds(HALF + 128 * h, 128)]
            v = r.qkv[rows, pl.ds(2 * HALF + 128 * h, 128)]
            s = jnp.where(causal, dot_t(q, pair(k)) * HDIM ** (-0.5), -1e30)
            e = jnp.exp(s - half_max(s))
            prob = e / half_sum(e)
            r.prob[rows, cols] = prob
            att = dot(prob.astype(BF16), pair(v))
            r.att[rows, cols] = att
            g = r.gp[rows, cols]
            r.mix[rows, cols] = (att * (g * jax.nn.sigmoid(g))).astype(BF16)

    def partial_rows(left, right, slot, start, count):
        rows = pl.ds(start, count)

        def tile(at, width):
            acc = right(left[rows, :], at, width)
            if start < OWN:
                r.po[rows, pl.ds(at, width)] = acc
            else:
                r.es[slot, pl.ds(start - OWN, count), pl.ds(at, width)] = acc.astype(BF16)

        tile_loop(D, 256, tile)

    def out_product(v, at, width):
        return dot(v, r.wo[:, pl.ds(at, width)])

    def hidden_back(v, at, width):
        return dot_t(v, r.wf[pl.ds(at, width), :])

    def heads_back(v, at, width):
        return dot_t(v, r.wa[pl.ds(at, width), pl.ds(0, 4 * HALF)])

    def resid_rows(start):
        rows = pl.ds(start, 64)
        v = r.tok[rows, :].astype(F32) + r.po[rows, :] + r.er[0, rows, :].astype(F32)
        r.res[rows, :] = v
        scale = lax.rsqrt(jnp.mean(v * v, axis=-1, keepdims=True) + EPS)
        r.nt[rows, :] = (v * scale * r.gain[1:2, :]).astype(BF16)

    def hidden(at, width):
        a = dot(r.nt[...], r.wf[:, pl.ds(at, width)]).astype(BF16)
        b = dot(r.nt[...], r.wf[:, pl.ds(FH + at, width)]).astype(BF16)
        r.fs[:, pl.ds(at, width)] = a
        r.fs[:, pl.ds(FH + at, width)] = b
        r.pr[:, pl.ds(at, width)] = (a.astype(F32) * b.astype(F32)).astype(BF16)

    def hidden_grad(at, width):
        pg = dot_t(r.cot[...], r.wd[pl.ds(at, width), :]).astype(BF16).astype(F32)
        a = r.fs[:, pl.ds(at, width)].astype(F32)
        b = r.fs[:, pl.ds(FH + at, width)].astype(F32)
        r.fs[:, pl.ds(at, width)] = (pg * b).astype(BF16)
        r.fs[:, pl.ds(FH + at, width)] = (pg * a).astype(BF16)

    def resid_grad_rows(start):
        rows = pl.ds(start, 64)
        ng = r.po[rows, :] + r.er[1, rows, :].astype(F32)
        v = r.res[rows, :]
        scale = lax.rsqrt(jnp.mean(v * v, axis=-1, keepdims=True) + EPS)
        n = ng * r.gain[1:2, :]
        grad = r.cot[rows, :].astype(F32) + scale * n - v * (scale * scale * scale * jnp.mean(n * v, axis=-1, keepdims=True))
        r.rg[rows, :] = grad
        r.bg[rows, :] = grad.astype(BF16)
        r.gacc[1] += jnp.sum((ng * v * scale).reshape(8, 8, D), axis=0)

    def mixed_grad(start, count):
        rows = pl.ds(start, count)

        def tile(at, width):
            cols = pl.ds(at, width)
            mg = dot_t(r.bg[rows, :], r.wo[pl.ds(at, width), :]).astype(BF16).astype(F32)
            g = r.gp[rows, cols]
            s = jax.nn.sigmoid(g)
            r.dout[rows, cols] = (mg * (g * s)).astype(BF16)
            r.g4[rows, pl.ds(3 * HALF + at, width)] = (mg * r.att[rows, cols] * (s * (1.0 + g * (1.0 - s)))).astype(BF16)

        tile_loop(HALF, 256, tile)

    def attend_grad(start):
        rows = pl.ds(start, 64)
        for h in range(4):
            cols = pl.ds(128 * h, 128)
            q = r.qkv[rows, cols]
            k = r.qkv[rows, pl.ds(HALF + 128 * h, 128)]
            v = r.qkv[rows, pl.ds(2 * HALF + 128 * h, 128)]
            do = r.dout[rows, cols]
            prob = r.prob[rows, cols]
            vg = t_dot(prob.astype(BF16), do)
            r.g4[rows, pl.ds(2 * HALF + 128 * h, 128)] = jnp.where(left, vg[:64], vg[64:]).astype(BF16)
            pg = dot_t(do, pair(v))
            sg = (prob * (pg - half_sum(prob * pg))).astype(BF16)
            r.g4[rows, cols] = (dot(sg, pair(k)) * HDIM ** (-0.5)).astype(BF16)
            kg = t_dot(sg, q)
            r.g4[rows, pl.ds(HALF + 128 * h, 128)] = (jnp.where(left, kg[:64], kg[64:]) * HDIM ** (-0.5)).astype(BF16)

    def block_out_rows(start):
        rows = pl.ds(start, 64)
        r.bo[rows, :] = (r.res[rows, :] + r.er[0, rows, :].astype(F32)).astype(BF16)

    def block_out_part(at, width):
        acc = dot(r.pr[...], r.wd[:, pl.ds(at, width)])
        r.res[:, pl.ds(at, width)] += acc[:OWN]
        r.es[0, :, pl.ds(at, width)] = acc[OWN:].astype(BF16)

    def tokens_grad_rows(start):
        rows = pl.ds(start, 64)
        ng = r.po[rows, :] + r.er[2, rows, :].astype(F32)
        v = r.tok[rows, :].astype(F32)
        scale = lax.rsqrt(jnp.mean(v * v, axis=-1, keepdims=True) + EPS)
        n = ng * r.gain[0:1, :]
        r.rg[rows, :] = r.rg[rows, :] + scale * n - v * (scale * scale * scale * jnp.mean(n * v, axis=-1, keepdims=True))
        r.gacc[0] += jnp.sum((ng * v * scale).reshape(8, 8, D), axis=0)

    def chunk_dot(i, cc):
        kind, at, cols = CHUNKS[i]
        if kind == "d":
            out = t_dot(r.pr[...], r.cot[:, lanes_of(512 * cc + at, cols)])
        elif kind == "f":
            out = t_dot(r.nt[:, lanes_of(512 * cc, 512)], r.fs[:, pl.ds(at, cols)])
        elif kind == "o":
            out = t_dot(r.mix[...], r.bg[:, lanes_of(512 * cc, cols)])
        else:
            out = t_dot(r.nrm[:, lanes_of(512 * cc, 512)], r.g4[:, pl.ds(at, cols)])
        return out.reshape(4, 2, piece_rows(kind), cols)

    buf = lambda name, i: getattr(r, f"{name}{i}")
    chunk_sends = {}

    def give(i):
        kind, _, cols = CHUNKS[i]
        if i >= 4 and i - 2 in chunk_sends:
            chunk_sends.pop(i - 2).wait_send()
        stage = r.sbd.at[i % 2] if kind == "d" else r.sbf.at[i % 2, :, :, :, pl.ds(0, cols)]
        stage[...] = chunk_dot(i, 1 - c).astype(BF16)
        chunk_sends[i] = send(stage, buf("rb", i), r.r_cs.at[i], r.r_cr.at[i], sib, later=False)

    def take(i):
        arrived(buf("rb", i), r.r_cr.at[i])
        own = buf("ow", i)
        own[...] = (chunk_dot(i, c) + buf("rb", i)[...].astype(F32)).astype(BF16)
        if Z_FIRST[i]:
            to_owners(i)
        else:
            send(own.at[:, 1 - y], buf("yr", i), r.r_ys.at[i], r.r_yr.at[i], yn)

    def z_slot(i, zz):
        own = buf("ow", i)
        return own.at[zz] if Z_FIRST[i] else own.at[zz, y]

    def to_owners(i):
        beside = dev(c, jnp.where(z == 3, 2, 1), y, x)
        far = jnp.where(z == 3, 0, 3)
        send_if(jnp.logical_not(inner), z_slot(i, far), buf("zx", i), r.r_zs.at[i, 2], r.r_zx.at[i], beside)
        for k in (1, 3):
            slot = z_slot(i, zk[k])
            send_if(z != (3 if k == 1 else 0), slot, buf("zr", i).at[3 - k], r.r_zs.at[i, 1 if k == 3 else 0], r.r_zr.at[i, 3 - k], zp[k])
        two = z_slot(i, zk[2])
        send_if(jnp.logical_not(inner), two, buf("zr", i).at[1], r.r_zt.at[i], r.r_zr.at[i, 1], zp[2])

    def pass_far(i):
        two = z_slot(i, zk[2])

        @pl.when(inner)
        def _():
            arrived(buf("zx", i), r.r_zx.at[i])
            two[...] = (two[...].astype(F32) + buf("zx", i)[...].astype(F32)).astype(BF16)

        send_if(inner, two, buf("zr", i).at[1], r.r_zs.at[i, 2], r.r_zr.at[i, 1], zp[2])

    def take_y(i):
        own, part = buf("ow", i), buf("yr", i)
        arrived(part, r.r_yr.at[i])
        if Z_FIRST[i]:
            return
        for k in range(4):
            slot = own.at[zk[k], y]
            slot[...] = (slot[...].astype(F32) + part[zk[k]].astype(F32)).astype(BF16)
        to_owners(i)

    finals = []

    def add_z(i, dst, first, half=None):
        part = buf("zr", i)
        take_part = (lambda j: part[j]) if half is None else (lambda j: part[j, half])
        if not half:
            arrived(part.at[1], r.r_zr.at[i, 1])
        dst[...] = first + take_part(1).astype(F32)
        for j, end in ((0, 3), (2, 0)):

            @pl.when(z != end)
            def _():
                if not half:
                    arrived(part.at[j], r.r_zr.at[i, j])
                dst[...] += take_part(j).astype(F32)

    def owner_sum(i):
        own, fin = buf("ow", i), buf("fin", i)
        for half in range(2):
            add_z(i, fin, own[z, half].astype(F32), half)
            own[z, half] = fin[...].astype(BF16)
        send(own.at[z, 1 - y], buf("yr", i), r.r_ys.at[i], r.r_yr.at[i], yn)

    def take_z(i):
        kind, at, cols = CHUNKS[i]
        own, fin = buf("ow", i), buf("fin", i)
        if Z_FIRST[i]:
            fin[...] = own[z, y].astype(F32) + buf("yr", i)[...].astype(F32)
        else:
            add_z(i, fin, own[z, y].astype(F32))
        if kind in ("f", "a"):
            if kind == "f":
                out, place = (r.g1, FH * x + at) if at < FH else (r.g2, FH * x + at - FH)
            else:
                out, place = (r.gq, r.gk, r.gv, r.gg)[at // 512], HALF * x
            dst = out.at[:, lanes_of(place, cols)]
            finals.append(local(fin.at[rows_of(32 * x, 32, 32)], dst, r.r_fs.at[i, 0]))
            send(fin.at[rows_of(32 * (1 - x), 32, 32)], dst, r.r_fs.at[i, 1], r.r_fr.at[i, 0], xn)
            return
        out = r.gd if kind == "d" else r.go
        n = 88 if kind == "d" else 32
        dst = out.at[:, lanes_of(512 * c + at, cols)]
        for xx in range(2):
            src = fin.at[pl.ds(n * xx, n)]
            itself = jnp.logical_and(x == c, x == xx)

            @pl.when(itself)
            def _():
                local(src, dst, r.r_fr.at[i, c])

            @pl.when(jnp.logical_not(itself))
            def _():
                send(src, dst, r.r_fs.at[i, xx], r.r_fr.at[i, c], dev(x, z, y, xx), later=False)

    def finish(i):
        kind, at, cols = CHUNKS[i]
        if kind in ("f", "a"):
            if kind == "f":
                out, place = (r.g1, FH * (1 - x) + at) if at < FH else (r.g2, FH * (1 - x) + at - FH)
            else:
                out, place = (r.gq, r.gk, r.gv, r.gg)[at // 512], HALF * (1 - x)
            arrived(out.at[:, lanes_of(place, cols)], r.r_fr.at[i, 0])
            return
        out = r.gd if kind == "d" else r.go
        n = 88 if kind == "d" else 32
        for cc in range(2):
            arrived(out.at[:, pl.ds(512 * cc + at, cols)], r.r_fr.at[i, cc])
        for xx in range(2):
            itself = jnp.logical_and(x == c, x == xx)

            @pl.when(jnp.logical_not(itself))
            def _():
                src = buf("fin", i).at[pl.ds(n * xx, n)]
                remote(src, src, r.r_fs.at[i, xx], r.r_fs.at[i, xx], xn).wait_send()

    def over(start, count, fn):
        row_loop(count, 64, lambda at: fn(at + start))

    def swap_rows(i, src, dst, start, count):
        swap(i, src.at[pl.ds(start, count)], dst.at[pl.ds(start, count)])

    def swapped_rows(i, dst, start, count):
        swapped(i, dst.at[pl.ds(start, count)])

    load_tok = local(r.tokens, r.tok.at[pl.ds(0, OWN)], r.s_loc.at[0])
    load_cot = local(r.cot_in, r.cot.at[pl.ds(0, OWN)], r.s_loc.at[1])
    outs = []

    def do_start():
        start_cols("a")
        start_cols("b")
        r.gacc[...] = jnp.zeros((2, 8, D), F32)

    def do_start2():
        start_rows("o")
        start_cols("s")
        start_cols("f")
        start_rows("d")
        swap(0, r.tokens, r.tok.at[pl.ds(OWN, OWN)])
        swap(1, r.cot_in, r.cot.at[pl.ds(OWN, OWN)])

    def do_norm_own():
        load_tok.wait()
        over(0, OWN, lambda start: norm_rows(start, 0, r.po))

    def do_norm_partner():
        swapped(0, r.tok.at[pl.ds(OWN, OWN)])
        over(0, OWN, lambda start: norm_rows(start, OWN, r.rg))

    def do_proj():
        unit_row = lax.broadcasted_iota(jnp.int32, (8, 128), 0)
        unit = jnp.where(unit_row == lax.broadcasted_iota(jnp.int32, (8, 128), 1), 1.0, 0.0).astype(BF16)
        r.gain[...] = dot_t(unit, r.wa[:, pl.ds(4 * HALF, 128)])
        row_loop(OWN, 64, gain_rows)
        tile_loop(3 * HALF, 256, proj)
        tile_loop(HALF, 256, proj_gate)

    def do_out(start):
        if start == 0:
            partial_rows(r.mix, out_product, 0, 0, 256)
            return
        partial_rows(r.mix, out_product, 0, start, 128)
        swap_rows(2 if start == 256 else 3, r.es.at[0], r.er.at[0], start - OWN, 128)

    def do_resid(start):
        swapped_rows(2 + start // 128, r.er.at[0], start, 128)
        over(start, 128, resid_rows)
        swap(4 + start // 128, r.nt.at[pl.ds(start, 128)], r.nt.at[pl.ds(OWN + start, 128)])

    def do_hidden():
        swapped(4, r.nt.at[pl.ds(OWN, 128)])
        swapped(5, r.nt.at[pl.ds(OWN + 128, 128)])
        tile_loop(FH, 256, hidden)

    def do_cot():
        load_cot.wait()
        swapped(1, r.cot.at[pl.ds(OWN, OWN)])

    def do_back(start):
        if start == 0:
            partial_rows(r.fs, hidden_back, 1, 0, 256)
            return
        partial_rows(r.fs, hidden_back, 1, start, 128)
        swap_rows(6 if start == 256 else 7, r.es.at[1], r.er.at[1], start - OWN, 128)

    def do_resid_grad(start):
        swapped_rows(6 + start // 128, r.er.at[1], start, 128)
        over(start, 128, resid_grad_rows)
        swap(8 + start // 128, r.bg.at[pl.ds(start, 128)], r.bg.at[pl.ds(OWN + start, 128)])

    def do_mixed_grad(start):
        if start == 0:
            mixed_grad(0, 256)
            return
        swapped(8 if start == 256 else 9, r.bg.at[pl.ds(start, 128)])
        mixed_grad(start, 128)

    def do_heads_back(start):
        partial_rows(r.g4, heads_back, 2, start, 256)
        if start:
            swap(11, r.es.at[2], r.er.at[2])

    def do_block_out():
        swaps.pop(2).wait_send()
        swaps.pop(3).wait_send()
        tile_loop(D, 256, block_out_part)
        swap(10, r.es.at[0], r.er.at[0])

    def do_tokens_grad():
        swapped(11, r.er.at[2])
        over(0, OWN, tokens_grad_rows)
        outs.append(local(r.rg, r.tokens_grad, r.s_out.at[1]))

    def do_block_rows():
        swapped(10, r.er.at[0])
        over(0, OWN, block_out_rows)
        outs.append(local(r.bo, r.block_out, r.s_out.at[0]))

    def do_gsum(n):
        if n == 0:
            which = lax.broadcasted_iota(jnp.int32, (8, D), 0)
            zero = jnp.zeros((8, D), F32)
            sums = [jnp.sum(r.gacc[i], axis=0, keepdims=True) for i in range(2)]
            grad_sum(0, jnp.where(which == 0, sums[0], zero) + jnp.where(which == 1, sums[1], zero))
        elif n < 4:
            grad_sum(n)
        else:
            r.gacc[0] = grad_sum(4)
            outs.append(local(r.gacc.at[0], r.gain_grads, r.s_out.at[2]))

    def do_take_z(i):
        if Z_FIRST[i]:
            take_y(i)
        take_z(i)

    def do_attend(start):
        over(start, 64, attend)

    def do_hidden_grad():
        tile_loop(FH, 256, hidden_grad)

    def do_attend_grad(start):
        over(start, 64, attend_grad)

    work = (
        (do_start,), (own, GA), (own, GB), (do_start2,), (got_y, GA, 0), (own, GO), (got_z, GA, 1, 0),
        (got_z, GA, 2, 0), (got_y, GB, 0), (got_z, GO, 1, 0), (got_z, GB, 1, 0), (got_z, GO, 2, 0), (do_norm_own,),
        (got_z, GO, 3, 0), (got_z, GB, 2, 0), (got_z, GA, 3, 0), (got_z, GB, 3, 0), (got_y, GO, 1), (got_y, GO, 0),
        (got_y, GO, 3), (own, GF), (do_norm_partner,), (got_y, GB, 2), (got_y, GA, 1), (got_y, GB, 1), (own, GD),
        (own, GS), (got_z, GF, 1, 0), (got_y, GA, 3), (got_y, GA, 2), (got_y, GO, 2), (got_y, GB, 3), (whole, GB),
        (whole, GA), (do_proj,), (got_z, GS, 1, 0), (do_attend, 0), (do_attend, 320), (got_y, GD, 0),
        (do_attend, 256), (whole, GO), (got_z, GS, 2, 0), (do_attend, 448), (do_out, 256), (do_attend, 384),
        (got_y, GF, 0), (got_z, GF, 2, 0), (got_z, GD, 1, 0), (do_attend, 64), (do_attend, 192), (got_z, GD, 2, 0),
        (got_y, GS, 0), (got_y, GF, 1), (do_out, 384), (got_z, GS, 3, 0), (got_z, GD, 1, 1), (got_y, GS, 1),
        (do_attend, 128), (got_y, GS, 2), (do_out, 0), (do_resid, 0), (got_z, GF, 3, 0), (do_resid, 128),
        (got_y, GF, 2), (got_z, GD, 3, 0), (got_z, GD, 2, 1), (got_y, GS, 3), (got_y, GF, 3), (whole, GS),
        (got_z, GD, 3, 1), (whole, GF), (do_hidden,), (do_cot,), (give, 0), (give, 1), (whole, GD), (do_hidden_grad,),
        (take, 0), (do_back, 256), (take, 1), (give, 2), (do_back, 384), (take, 2), (do_back, 0), (give, 3),
        (do_resid_grad, 0), (pass_far, 1), (give, 4), (take_y, 0), (do_resid_grad, 128), (take, 3),
        (do_mixed_grad, 0), (owner_sum, 1), (do_attend_grad, 0), (take_y, 2), (pass_far, 0), (do_attend_grad, 64),
        (give, 5), (take, 4), (do_attend_grad, 192), (do_attend_grad, 128), (do_mixed_grad, 256),
        (do_mixed_grad, 384), (give, 6), (take_y, 3), (pass_far, 2), (do_attend_grad, 448), (take, 5), (give, 7),
        (do_attend_grad, 256), (do_take_z, 0), (do_attend_grad, 384), (take, 7), (do_attend_grad, 320),
        (do_heads_back, 256), (pass_far, 3), (do_take_z, 1), (pass_far, 7), (do_heads_back, 0), (take, 6),
        (take_y, 4), (give, 8), (do_block_out,), (take_y, 5), (take, 8), (give, 9), (give, 10), (pass_far, 4),
        (do_tokens_grad,), (do_gsum, 0), (take, 9), (do_take_z, 2), (owner_sum, 7), (take_y, 6), (take_y, 8),
        (pass_far, 5), (do_take_z, 4), (do_take_z, 3), (finish, 0), (take, 10), (pass_far, 8), (do_gsum, 1),
        (pass_far, 6), (take_y, 9), (pass_far, 9), (finish, 2), (do_take_z, 6), (do_take_z, 7), (do_take_z, 5),
        (take_y, 10), (finish, 1), (finish, 4), (pass_far, 10), (do_take_z, 9), (do_gsum, 2), (finish, 6),
        (do_take_z, 8), (do_gsum, 3), (do_take_z, 10), (finish, 7), (finish, 8), (finish, 5), (finish, 3),
        (finish, 9), (do_block_rows,), (finish, 10), (do_gsum, 4),
    )
    for step, *args in work:
        step(*args)
    for copy in list(chunk_sends.values()) + list(swaps.values()) + sends:
        copy.wait_send()
    for pred, copy in guarded:
        pl.when(pred)(copy.wait_send)
    for copy in finals + outs:
        copy.wait()
    for g in "abfs":
        gi = GROUPS.index(g)
        own = col_shard(g, x)
        remote(own, own, r.s_xs.at[gi, 0], r.s_xs.at[gi, 0], xn).wait_send()
    for g in ("o", "d"):
        gi = GROUPS.index(g)
        block = r.wo.at[pl.ds(0, 32), pl.ds(0, 512)] if g == "o" else r.wds.at[0]

        @pl.when(x != c)
        def _():
            remote(block, block, r.s_xs.at[gi, 0], r.s_xs.at[gi, 0], xn).wait_send()

        remote(block, block, r.s_xs.at[gi, 1], r.s_xs.at[gi, 1], xn).wait_send()


def hand_over(gain_ref, *refs):
    count = (len(refs) - 4) // 3
    ins, (one, two), outs = refs[:count], refs[count : count + 2], refs[count + 2 : 2 * count + 2]
    held, (in_sems, out_sems) = refs[2 * count + 2 : -2], refs[-2:]
    loads = [pltpu.make_async_copy(a, b, in_sems.at[i]) for i, (a, b) in enumerate(zip(ins, held))]
    stores = [pltpu.make_async_copy(a, b, out_sems.at[i]) for i, (a, b) in enumerate(zip(held, outs))]
    for load in loads:
        load.start()
    me = lax.axis_index("dp") * 16 + lax.axis_index("fsdp")
    block = gain_ref[:, lanes_of(128 * (me // 4), 128)]
    block = pltpu.roll(block, lax.rem(128 - 32 * lax.rem(me, 4), 128), 1)
    one[...] = block[0, :32]
    two[...] = block[1, :32]
    for load, store in zip(loads, stores):
        load.wait()
        store.start()
    for store in stores:
        store.wait()


def fused_layer(
    tokens, attn_gain, w_query, w_key, w_value, w_gate, w_output, ffn_gain, w_first, w_second, w_down, cotangent
):
    gains = jnp.pad(jnp.stack([attn_gain, ffn_gain], axis=1), ((0, 0), (0, 126)))
    items = scratch_list()
    names = IN_NAMES + OUT_NAMES + tuple(name for name, _ in items)
    shape = jax.ShapeDtypeStruct
    outs = pl.pallas_call(
        functools.partial(layer_kernel, names),
        out_shape=[
            shape((OWN, D), BF16), shape((OWN, D), F32), shape((8, D), F32),
            shape((32, D), F32), shape((32, D), F32), shape((32, D), F32), shape((32, D), F32), shape((32, D), F32),
            shape((32, FF), F32), shape((32, FF), F32), shape((88, D), F32),
        ],
        in_specs=[pl.BlockSpec(memory_space=pl.ANY)] * len(IN_NAMES),
        out_specs=[pl.BlockSpec(memory_space=pl.ANY)] * len(OUT_NAMES),
        scratch_shapes=[spec for _, spec in items],
        compiler_params=pltpu.CompilerParams(collective_id=0, has_side_effects=True, vmem_limit_bytes=66 * 2**20 - 2**21),
        name="layer",
    )(tokens, gains, w_query, w_key, w_value, w_gate, w_output, w_first, w_second, w_down, cotangent)
    block_out, tokens_grad, gain_grads, gq, gk, gv, gg, go, g1, g2, gd = outs
    kept = (block_out, tokens_grad, gq, gk, gv, gg, go, g1, g2, gd)
    anywhere = pl.BlockSpec(memory_space=pl.ANY)
    in_vmem = pl.BlockSpec(memory_space=pltpu.VMEM)
    gain_one, gain_two, *rest = pl.pallas_call(
        hand_over,
        out_shape=[shape((32,), F32)] * 2 + [shape(v.shape, v.dtype) for v in kept],
        in_specs=[in_vmem] + [anywhere] * len(kept),
        out_specs=[in_vmem] * 2 + [anywhere] * len(kept),
        scratch_shapes=[pltpu.VMEM(v.shape, v.dtype) for v in kept] + [pltpu.SemaphoreType.DMA((len(kept),))] * 2,
        compiler_params=pltpu.CompilerParams(vmem_limit_bytes=63 * 2**20),
        name="hand_over",
    )(gain_grads, *kept)
    block_out, tokens_grad, gq, gk, gv, gg, go, g1, g2, gd = rest
    return block_out, tokens_grad, gain_one, gq, gk, gv, gg, go, gain_two, g1, g2, gd


def rms_scale(values, gain):
    return values * lax.rsqrt(jnp.mean(values * values, axis=-1, keepdims=True) + EPS) * gain


def gated(attended, gate_pre):
    return attended * jax.nn.silu(gate_pre)


def contract_rows(left, right):
    return lax.dot_general(
        left, right, (((0,), (0,)), ((), ())), preferred_element_type=jnp.float32
    )


def contract_cols(left, right):
    return lax.dot_general(
        left, right, (((1,), (1,)), ((), ())), preferred_element_type=jnp.float32
    )


def project(left, right):
    return jnp.dot(left, right, preferred_element_type=jnp.float32)


def flatten_rows(matrix):
    return matrix.reshape(-1, 128)


def restore_rows(flat, columns):
    return flat.reshape(-1, columns)


def split_heads(matrix):
    return matrix.reshape(matrix.shape[0] // BLK, BLK, HEADS, HDIM)


def block_scores(queries, keys):
    raw = jnp.einsum(
        "bqhd,bkhd->bhqk",
        split_heads(queries),
        split_heads(keys),
        preferred_element_type=jnp.float32,
    )
    causal = jnp.arange(BLK)[:, None] >= jnp.arange(BLK)[None, :]
    return jnp.where(causal, raw * HDIM ** (-0.5), -1e30)


def attend_forward(queries, keys, values):
    scores = block_scores(queries, keys)
    highest = jnp.max(scores, axis=-1, keepdims=True)
    weights = jnp.exp(scores - highest)
    total = jnp.sum(weights, axis=-1, keepdims=True)
    probs = (weights / total).astype(jnp.bfloat16)
    attended = jnp.einsum(
        "bhqk,bkhd->bqhd", probs, split_heads(values), preferred_element_type=jnp.float32
    )
    return (attended.reshape(queries.shape[0], D), highest + jnp.log(total))


def attend_backward(queries, keys, values, log_total, attended_grad):
    scores = block_scores(queries, keys)
    probs = jnp.exp(scores - log_total)
    grad_heads = split_heads(attended_grad)
    value_grad = jnp.einsum(
        "bhqk,bqhd->bkhd",
        probs.astype(jnp.bfloat16),
        grad_heads,
        preferred_element_type=jnp.float32,
    )
    prob_grad = jnp.einsum(
        "bqhd,bkhd->bhqk", grad_heads, split_heads(values), preferred_element_type=jnp.float32
    )
    score_grad = (probs * (prob_grad - jnp.sum(probs * prob_grad, axis=-1, keepdims=True))).astype(
        jnp.bfloat16
    )
    factor = HDIM ** (-0.5)
    query_grad = (
        jnp.einsum(
            "bhqk,bkhd->bqhd", score_grad, split_heads(keys), preferred_element_type=jnp.float32
        )
        * factor
    )
    key_grad = (
        jnp.einsum(
            "bhqk,bqhd->bkhd", score_grad, split_heads(queries), preferred_element_type=jnp.float32
        )
        * factor
    )
    length = queries.shape[0]
    return (
        query_grad.reshape(length, D).astype(jnp.bfloat16),
        key_grad.reshape(length, D).astype(jnp.bfloat16),
        value_grad.reshape(length, D).astype(jnp.bfloat16),
    )


def on_device(
    tokens,
    attn_gain,
    w_query,
    w_key,
    w_value,
    w_gate,
    w_output,
    ffn_gain,
    w_first,
    w_second,
    w_down,
    cotangent,
):
    attn_whole = (
        lax.all_gather(attn_gain, ("dp", "fsdp"), axis=0, tiled=True),
        lax.all_gather(w_query, ("dp", "fsdp"), axis=0, tiled=True),
        lax.all_gather(w_key, ("dp", "fsdp"), axis=0, tiled=True),
        lax.all_gather(w_value, ("dp", "fsdp"), axis=0, tiled=True),
        lax.all_gather(w_gate, ("dp", "fsdp"), axis=0, tiled=True),
        lax.all_gather(w_output, ("dp", "fsdp"), axis=0, tiled=True),
    )
    gain_one, query_full, key_full, value_full, gate_full, output_full = attn_whole
    inputs = tokens.astype(jnp.float32)
    normed_pre, norm_pull = jax.vjp(rms_scale, inputs, gain_one.astype(jnp.float32))
    normed = normed_pre.astype(jnp.bfloat16)
    queries = project(normed, query_full).astype(jnp.bfloat16)
    keys = project(normed, key_full).astype(jnp.bfloat16)
    values = project(normed, value_full).astype(jnp.bfloat16)
    gate_pre = project(normed, gate_full)
    attended, log_total = attend_forward(queries, keys, values)
    mixed_pre, gate_pull = jax.vjp(gated, attended, gate_pre)
    mixed = mixed_pre.astype(jnp.bfloat16)
    resid = inputs + project(mixed, output_full)
    ffn_whole = (
        lax.all_gather(ffn_gain, ("dp", "fsdp"), axis=0, tiled=True),
        lax.all_gather(w_first, ("dp", "fsdp"), axis=0, tiled=True),
        lax.all_gather(w_second, ("dp", "fsdp"), axis=0, tiled=True),
        lax.all_gather(w_down, ("dp", "fsdp"), axis=0, tiled=True),
    )
    gain_two, first_full, second_full, down_full = ffn_whole
    normed_two_pre, norm_two_pull = jax.vjp(rms_scale, resid, gain_two.astype(jnp.float32))
    normed_two = normed_two_pre.astype(jnp.bfloat16)
    first = project(normed_two, first_full).astype(jnp.bfloat16)
    second = project(normed_two, second_full).astype(jnp.bfloat16)
    product = (first.astype(jnp.float32) * second.astype(jnp.float32)).astype(jnp.bfloat16)
    block_out = (resid + project(product, down_full)).astype(jnp.bfloat16)
    gain_two, first_full, second_full, down_full = (
        lax.all_gather(ffn_gain, ("dp", "fsdp"), axis=0, tiled=True),
        lax.all_gather(w_first, ("dp", "fsdp"), axis=0, tiled=True),
        lax.all_gather(w_second, ("dp", "fsdp"), axis=0, tiled=True),
        lax.all_gather(w_down, ("dp", "fsdp"), axis=0, tiled=True),
    )
    product_grad = contract_cols(cotangent, down_full).astype(jnp.bfloat16)
    product_wide = product_grad.astype(jnp.float32)
    first_grad = (product_wide * second.astype(jnp.float32)).astype(jnp.bfloat16)
    second_grad = (product_wide * first.astype(jnp.float32)).astype(jnp.bfloat16)
    normed_two_grad = contract_cols(first_grad, first_full) + contract_cols(
        second_grad, second_full
    )
    resid_part, gain_two_grad = norm_two_pull(normed_two_grad)
    resid_grad = cotangent.astype(jnp.float32) + resid_part
    down_grad = contract_rows(product, cotangent)
    first_w_grad = contract_rows(normed_two, first_grad)
    second_w_grad = contract_rows(normed_two, second_grad)
    ffn_sums = (
        lax.psum_scatter(gain_two_grad, ("dp", "fsdp"), scatter_dimension=0, tiled=True),
        lax.psum_scatter(
            flatten_rows(first_w_grad), ("dp", "fsdp"), scatter_dimension=0, tiled=True
        ),
        lax.psum_scatter(
            flatten_rows(second_w_grad), ("dp", "fsdp"), scatter_dimension=0, tiled=True
        ),
        lax.psum_scatter(flatten_rows(down_grad), ("dp", "fsdp"), scatter_dimension=0, tiled=True),
    )
    gain_one, query_full, key_full, value_full, gate_full, output_full = (
        lax.all_gather(attn_gain, ("dp", "fsdp"), axis=0, tiled=True),
        lax.all_gather(w_query, ("dp", "fsdp"), axis=0, tiled=True),
        lax.all_gather(w_key, ("dp", "fsdp"), axis=0, tiled=True),
        lax.all_gather(w_value, ("dp", "fsdp"), axis=0, tiled=True),
        lax.all_gather(w_gate, ("dp", "fsdp"), axis=0, tiled=True),
        lax.all_gather(w_output, ("dp", "fsdp"), axis=0, tiled=True),
    )
    branch_grad = resid_grad.astype(jnp.bfloat16)
    mixed_grad = contract_cols(branch_grad, output_full).astype(jnp.bfloat16)
    attended_part, gate_part = gate_pull(mixed_grad.astype(jnp.float32))
    attended_grad = attended_part.astype(jnp.bfloat16)
    gate_grad = gate_part.astype(jnp.bfloat16)
    query_grad, key_grad, value_grad = attend_backward(
        queries, keys, values, log_total, attended_grad
    )
    normed_grad = contract_cols(query_grad, query_full) + contract_cols(key_grad, key_full)
    normed_grad = (
        normed_grad + contract_cols(value_grad, value_full) + contract_cols(gate_grad, gate_full)
    )
    input_part, gain_one_grad = norm_pull(normed_grad)
    tokens_grad = resid_grad + input_part
    output_w_grad = contract_rows(mixed, branch_grad)
    query_w_grad = contract_rows(normed, query_grad)
    key_w_grad = contract_rows(normed, key_grad)
    value_w_grad = contract_rows(normed, value_grad)
    gate_w_grad = contract_rows(normed, gate_grad)
    attn_sums = (
        lax.psum_scatter(gain_one_grad, ("dp", "fsdp"), scatter_dimension=0, tiled=True),
        lax.psum_scatter(
            flatten_rows(query_w_grad), ("dp", "fsdp"), scatter_dimension=0, tiled=True
        ),
        lax.psum_scatter(flatten_rows(key_w_grad), ("dp", "fsdp"), scatter_dimension=0, tiled=True),
        lax.psum_scatter(
            flatten_rows(value_w_grad), ("dp", "fsdp"), scatter_dimension=0, tiled=True
        ),
        lax.psum_scatter(
            flatten_rows(gate_w_grad), ("dp", "fsdp"), scatter_dimension=0, tiled=True
        ),
        lax.psum_scatter(
            flatten_rows(output_w_grad), ("dp", "fsdp"), scatter_dimension=0, tiled=True
        ),
    )
    gain_two_sum, first_flat, second_flat, down_flat = ffn_sums
    gain_one_sum, query_flat, key_flat, value_flat, gate_flat, output_flat = attn_sums
    query_sum = restore_rows(query_flat, D)
    key_sum = restore_rows(key_flat, D)
    value_sum = restore_rows(value_flat, D)
    gate_sum = restore_rows(gate_flat, D)
    output_sum = restore_rows(output_flat, D)
    first_sum = restore_rows(first_flat, FF)
    second_sum = restore_rows(second_flat, FF)
    down_sum = restore_rows(down_flat, D)
    return (
        block_out,
        tokens_grad,
        gain_one_sum,
        query_sum,
        key_sum,
        value_sum,
        gate_sum,
        output_sum,
        gain_two_sum,
        first_sum,
        second_sum,
        down_sum,
    )


def solution(mesh):
    fits = dict(mesh.shape) == {"dp": 2, "fsdp": 16}
    return jax.shard_map(
        fused_layer if fits else on_device,
        mesh=mesh,
        in_specs=(
            P(("dp", "fsdp"), None),
            P(("dp", "fsdp")),
            P(("dp", "fsdp"), None),
            P(("dp", "fsdp"), None),
            P(("dp", "fsdp"), None),
            P(("dp", "fsdp"), None),
            P(("dp", "fsdp"), None),
            P(("dp", "fsdp")),
            P(("dp", "fsdp"), None),
            P(("dp", "fsdp"), None),
            P(("dp", "fsdp"), None),
            P(("dp", "fsdp"), None),
        ),
        out_specs=(
            P(("dp", "fsdp"), None),
            P(("dp", "fsdp"), None),
            P(("dp", "fsdp")),
            P(("dp", "fsdp"), None),
            P(("dp", "fsdp"), None),
            P(("dp", "fsdp"), None),
            P(("dp", "fsdp"), None),
            P(("dp", "fsdp"), None),
            P(("dp", "fsdp")),
            P(("dp", "fsdp"), None),
            P(("dp", "fsdp"), None),
            P(("dp", "fsdp"), None),
        ),
        check_vma=False,
    )
```

```python
import functools

import jax
import jax.numpy as jnp
from jax import lax
from jax.experimental import pallas as pl
from jax.experimental.pallas import tpu as pltpu
from jax.sharding import PartitionSpec as P

D = 1024
HEADS = 16
HDIM = 64
FF = 2816
BLK = 64


EPS = 1e-06


MESH = pl.DeviceIdType.MESH
F32, BF16 = jnp.float32, jnp.bfloat16

OWN = 256
ROWS = 512
HALF = 512
FH = 1408
CHUNKS = (
    ("d", 0, 256), ("d", 256, 256),
    ("f", 0, 768), ("f", 768, 640), ("f", 1408, 768), ("f", 2176, 640),
    ("o", 0, 512),
    ("a", 1536, 512), ("a", 1024, 512), ("a", 512, 512), ("a", 0, 512),
)
NCH = len(CHUNKS)
Z_FIRST = tuple(i in (1, 7,) for i in range(NCH))
Y_FIRST = ("s",)
GROUPS = ("a", "b", "o", "f", "s", "g", "t", "d")
GA, GB, GO, GF, GS, GG, GT, GD = GROUPS
SPANS = {"a": (0, 1152), "b": (1152, 1024), "f": (0, 768), "g": (768, 640), "s": (FH, 768), "t": (FH + 768, 640)}


def piece_rows(kind):
    return 176 if kind == "d" else 64


def scratch_list():
    vm, dma = pltpu.VMEM, pltpu.SemaphoreType.DMA
    items = [
        ("wa", vm((D, 4 * HALF + 128), BF16)), ("wf", vm((D, 2 * FH), BF16)),
        ("wo", vm((HALF, D), BF16)), ("wd", vm((FH, D), BF16)), ("wds", vm((2, 88, 512), BF16)),
        ("tok", vm((ROWS, D), BF16)), ("cot", vm((ROWS, D), BF16)), ("nrm", vm((ROWS, D), BF16)),
        ("qkv", vm((ROWS, 3 * HALF), BF16)), ("gp", vm((ROWS, HALF), F32)), ("att", vm((ROWS, HALF), F32)),
        ("prob", vm((ROWS, HALF), F32)), ("mix", vm((ROWS, HALF), BF16)), ("dout", vm((ROWS, HALF), BF16)),
        ("res", vm((OWN, D), F32)), ("nt", vm((ROWS, D), BF16)), ("fs", vm((ROWS, 2 * FH), BF16)),
        ("pr", vm((ROWS, FH), BF16)), ("g4", vm((ROWS, 4 * HALF), BF16)), ("bg", vm((ROWS, D), BF16)),
        ("rg", vm((OWN, D), F32)), ("po", vm((OWN, D), F32)), ("bo", vm((OWN, D), BF16)),
        ("es", vm((3, OWN, D), BF16)), ("er", vm((3, OWN, D), BF16)),
        ("gs", vm((4, 8, D), F32)), ("gr", vm((6, 8, D), F32)), ("gain", vm((8, D), F32)), ("gains", vm((32, 128), BF16)), ("gacc", vm((2, 8, D), F32)),
        ("sbd", vm((2, 4, 2, 176, 256), BF16)), ("sbf", vm((2, 4, 2, 64, 768), BF16)),
    ]
    for i, (kind, _, cols) in enumerate(CHUNKS):
        r = piece_rows(kind)
        items += [
            (f"rb{i}", vm((4, 2, r, cols), BF16)), (f"ow{i}", vm((4, 2, r, cols), BF16)),
            (f"yr{i}", vm((r, cols) if Z_FIRST[i] else (4, r, cols), BF16)),
            (f"zr{i}", vm((3, 2, r, cols) if Z_FIRST[i] else (3, r, cols), BF16)),
            (f"zx{i}", vm((2, r, cols) if Z_FIRST[i] else (r, cols), BF16)),
            (f"fin{i}", vm((r, cols), F32)),
        ]
    n = len(GROUPS)
    items += [
        ("s_loc", dma((4,))), ("s_wl", dma((n,))), ("s_xs", dma((n, 2))), ("s_xr", dma((n,))),
        ("s_es", dma((16,))), ("s_er", dma((16,))),
        ("s_zs", dma((n, 2, 5))), ("s_zr", dma((n, 2, 3))), ("s_ys", dma((n, 4))), ("s_yr", dma((n, 4))),
        ("s_cs", dma((n, 4, 2))), ("s_cr", dma((n, 4, 2))),
        ("s_gs", dma((6,))), ("s_gr", dma((6,))),
        ("r_cs", dma((NCH,))), ("r_cr", dma((NCH,))), ("r_ys", dma((NCH,))), ("r_yr", dma((NCH,))),
        ("r_zs", dma((NCH, 3))), ("r_zr", dma((NCH, 3))), ("r_zx", dma((NCH,))), ("r_zt", dma((NCH,))), ("r_fs", dma((NCH, 2))), ("r_fr", dma((NCH, 2))),
        ("s_out", dma((4,))),
    ]
    return items


IN_NAMES = ("tokens", "gain_a", "gain_f", "wq", "wk", "wv", "wg", "wo_in", "w1", "w2", "wd_in", "cot_in")
OUT_NAMES = ("block_out", "tokens_grad", "gain_grads", "gq", "gk", "gv", "gg", "go", "g1", "g2", "gd")


class Refs:
    def __init__(self, names, refs):
        self.__dict__.update(zip(names, refs))


def rows_of(start, count, unit=8):
    return pl.ds(pl.multiple_of(start, unit), count)


def lanes_of(start, count):
    return pl.ds(pl.multiple_of(start, 128), count)


def dot(a, b):
    return jnp.dot(a, b, preferred_element_type=F32)


def dot_t(a, b):
    return lax.dot_general(a, b, (((1,), (1,)), ((), ())), preferred_element_type=F32)


def t_dot(a, b):
    return lax.dot_general(a, b, (((0,), (0,)), ((), ())), preferred_element_type=F32)


def tile_loop(total, width, fn):
    count = total // width
    if count == 1:
        fn(0, width)
    else:
        lax.fori_loop(0, count, lambda i, u: (fn(pl.multiple_of(i * width, width), width), u)[1], 0)
    if total % width:
        fn(count * width, total % width)


def row_loop(total, step, fn):
    lax.fori_loop(0, total // step, lambda i, u: (fn(pl.multiple_of(i * step, step)), u)[1], 0)


def layer_kernel(names, *refs):
    r = Refs(names, refs)
    c = lax.axis_index("dp")
    f = lax.axis_index("fsdp")
    z, y, x = f // 4, (f // 2) % 2, f % 2

    def dev(cc, zz, yy, xx):
        return (cc, zz * 4 + yy * 2 + xx)

    xn, yn, sib, diag = dev(c, z, y, 1 - x), dev(c, z, 1 - y, x), dev(1 - c, z, y, x), dev(1 - c, z, y, 1 - x)
    zk = [(z + k) % 4 for k in range(4)]
    zp = [dev(c, zk[k], y, x) for k in range(4)]

    barrier = pltpu.get_barrier_semaphore()
    for peer in (xn, yn, sib, diag, zp[1], zp[2], zp[3]):
        pl.semaphore_signal(barrier, inc=1, device_id=peer, device_id_type=MESH)
    pl.semaphore_wait(barrier, 7)

    sends, guarded = [], []
    inner = jnp.logical_and(z != 0, z != 3)

    def remote(src, dst, ss, rs, to):
        return pltpu.make_async_remote_copy(
            src_ref=src, dst_ref=dst, send_sem=ss, recv_sem=rs, device_id=to, device_id_type=MESH
        )

    def send(src, dst, ss, rs, to, later=True):
        copy = remote(src, dst, ss, rs, to)
        copy.start()
        if later:
            sends.append(copy)
        return copy

    def send_if(pred, src, dst, ss, rs, to):
        copy = remote(src, dst, ss, rs, to)
        pl.when(pred)(copy.start)
        guarded.append((pred, copy))

    def arrived(ref, sem):
        remote(ref, ref, sem, sem, xn).wait_recv()

    def local(src, dst, sem):
        copy = pltpu.make_async_copy(src, dst, sem)
        copy.start()
        return copy

    mine = x
    p = c * 8 + z * 2 + y
    m = z * 2 + y

    def piece(g, cc, zz, yy):
        if g in SPANS:
            full = r.wa if g in "ab" else r.wf
            return full.at[rows_of(64 * (cc * 8 + zz * 2 + yy), 64, 64), pl.ds(*SPANS[g])]
        if g == "o":
            return r.wo.at[rows_of(64 * (zz * 2 + yy), 64, 64), lanes_of(512 * cc, 512)]
        return r.wd.at[rows_of(176 * (zz * 2 + yy), 176, 16), lanes_of(512 * cc, 512)]

    def col_shard(g, who):
        row = rows_of(64 * p + 32 * who, 32, 32)
        return (r.wa if g in "ab" else r.wf).at[row, pl.ds(*SPANS[g])]

    def start_cols(g):
        gi = GROUPS.index(g)
        if g == "a":
            parts = [(r.wq, HALF, 0, HALF, 0), (r.wk, HALF, 0, HALF, HALF)]
        elif g == "b":
            parts = [(r.wv, HALF, 0, HALF, 1152), (r.wg, HALF, 0, HALF, 1152 + HALF)]
        else:
            at, cols = SPANS[g]
            parts = [(r.w1 if g in "fg" else r.w2, FH, at % FH, cols, at)]
        full = r.wa if g in "ab" else r.wf
        row = rows_of(64 * p + 32 * x, 32, 32)
        if g == "a":
            local(r.gains, full.at[row, pl.ds(1024, 128)], r.s_wl.at[gi])
            send(r.gains, full.at[row, pl.ds(1024, 128)], r.s_xs.at[gi, 0], r.s_xr.at[gi], xn, later=False)
        for w, half, first, cols, at in parts:
            dst = full.at[row, pl.ds(at, cols)]
            local(w.at[:, lanes_of(half * x + first, cols)], dst, r.s_wl.at[gi])
            send(
                w.at[:, lanes_of(half * (1 - x) + first, cols)], dst,
                r.s_xs.at[gi, 0], r.s_xr.at[gi], xn, later=False,
            )

    def start_rows(g):
        gi = GROUPS.index(g)
        w = r.wo_in if g == "o" else r.wd_in

        def place(h):
            if g == "o":
                return r.wo.at[rows_of(64 * m + 32 * x, 32, 32), lanes_of(512 * h, 512)]
            return r.wds.at[x]

        @pl.when(x == c)
        def _():
            local(w.at[:, lanes_of(512 * c, 512)], place(c), r.s_xr.at[gi])

        @pl.when(x != c)
        def _():
            send(w.at[:, lanes_of(512 * c, 512)], place(c), r.s_xs.at[gi, 0], r.s_xr.at[gi], xn, later=False)

        send(
            w.at[:, lanes_of(512 * (1 - c), 512)], place(1 - c), r.s_xs.at[gi, 1], r.s_xr.at[gi], dev(1 - c, z, y, c),
            later=False,
        )

    def piece_ready(g):
        gi = GROUPS.index(g)
        if g in SPANS:
            own = col_shard(g, x)
            pltpu.make_async_copy(own, own, r.s_wl.at[gi]).wait()
            arrived(col_shard(g, 1 - x), r.s_xr.at[gi])
        elif g == "o":
            arrived(piece("o", c, z, y), r.s_xr.at[gi])
        else:
            arrived(r.wds, r.s_xr.at[gi])
            both = jnp.concatenate([r.wds[0].astype(F32), r.wds[1].astype(F32)], axis=0)
            r.wd[rows_of(176 * m, 176, 16), lanes_of(512 * c, 512)] = both.astype(BF16)

    near = [
        jnp.where(z < 2, 1, 3),
        jnp.where(z == 1, 3, jnp.where(z == 2, 1, 2)),
        jnp.where(z == 0, 3, jnp.where(z == 3, 1, 2)),
    ]

    def near_z(n):
        return z if n == 0 else lax.rem(z + near[n - 1], 4)

    def up_down(g, yy, j):
        gi = GROUPS.index(g)
        own = piece(g, c, z, yy)
        send_if(z < 3, own, own, r.s_zs.at[gi, j, 0], r.s_zr.at[gi, j, 2], zp[1])
        send_if(z > 0, own, own, r.s_zs.at[gi, j, 1], r.s_zr.at[gi, j, 0], zp[3])

    def across(g, n):
        gi = GROUPS.index(g)
        ref = piece(g, c, near_z(n), y)
        send(ref, ref, r.s_ys.at[gi, n], r.s_yr.at[gi, n], yn)

    def to_core(g, n, j):
        gi = GROUPS.index(g)
        ref = piece(g, c, near_z(n), y if j == 0 else 1 - y)
        send(ref, ref, r.s_cs.at[gi, n, j], r.s_cr.at[gi, n, j], sib)

    def own(g):
        piece_ready(g)
        if g in Y_FIRST:
            across(g, 0)
            up_down(g, y, 0)
        else:
            up_down(g, y, 0)
            across(g, 0)
        to_core(g, 0, 0)

    def got_z(g, n, j=0):
        gi = GROUPS.index(g)
        got = piece(g, c, near_z(n), y if j == 0 else 1 - y)
        arrived(got, r.s_zr.at[gi, j, near[n - 1] - 1])
        src = near_z(n)
        to = jnp.where(src > z, z - 1, z + 1)
        slot = lax.rem(src - to + 4, 4) - 1
        send_if(inner, got, got, r.s_zs.at[gi, j, 1 + n], r.s_zr.at[gi, j, slot], dev(c, to, y, x))
        if g not in Y_FIRST:
            across(g, n)
        to_core(g, n, j)

    def got_y(g, n):
        gi = GROUPS.index(g)
        arrived(piece(g, c, near_z(n), 1 - y), r.s_yr.at[gi, n])
        if g in Y_FIRST:
            up_down(g, 1 - y, 1)
        to_core(g, n, 1)

    def spread_z(g):
        for j in range(2 if g in Y_FIRST else 1):
            for n in (1, 2, 3):
                got_z(g, n, j)

    def spread_y(g):
        for n in range(1 if g in Y_FIRST else 4):
            got_y(g, n)

    def whole(g):
        gi = GROUPS.index(g)
        for k in range(4):
            for j in range(2):
                arrived(piece(g, 1 - c, near_z(k), y if j == 0 else 1 - y), r.s_cr.at[gi, k, j])

    swaps = {}

    def swap(i, src, dst):
        swaps[i] = send(src, dst, r.s_es.at[i], r.s_er.at[i], xn, later=False)

    def swapped(i, dst):
        arrived(dst, r.s_er.at[i])

    def grad_sum(n, value=None):
        def out(slot, to):
            send(r.gs.at[min(slot, 3)], r.gr.at[slot], r.s_gs.at[slot], r.s_gr.at[slot], to)

        def got(slot):
            arrived(r.gr.at[slot], r.s_gr.at[slot])
            return r.gr[slot]

        if n == 0:
            r.gs[0] = value
            out(0, xn)
        elif n < 3:
            r.gs[n] = r.gs[n - 1] + got(n - 1)
            out(n, yn if n == 1 else sib)
        elif n == 3:
            r.gs[3] = r.gs[2] + got(2)
            for k in (1, 2, 3):
                send(r.gs.at[3], r.gr.at[6 - k], r.s_gs.at[2 + k], r.s_gr.at[6 - k], zp[k])
        else:
            return r.gs[3] + (got(3) + got(4) + got(5))

    def norm_rows(start, at, out):
        v = r.tok[pl.ds(start + at, 64), :].astype(F32)
        scale = lax.rsqrt(jnp.mean(v * v, axis=-1, keepdims=True) + EPS)
        out[pl.ds(start, 64), :] = v * scale

    def gain_rows(start):
        rows = pl.ds(start, 64)
        r.nrm[rows, :] = (r.po[rows, :] * r.gain[0:1, :]).astype(BF16)
        r.nrm[pl.ds(start + OWN, 64), :] = (r.rg[rows, :] * r.gain[0:1, :]).astype(BF16)

    def proj(at, width, shift=0):
        r.qkv[:, pl.ds(at + shift, width)] = dot(r.nrm[...], r.wa[:, pl.ds(at + shift + shift // 8, width)]).astype(BF16)

    def proj_gate(at, width):
        r.gp[:, pl.ds(at, width)] = dot(r.nrm[...], r.wa[:, pl.ds(1152 + HALF + at, width)])

    lane = lax.broadcasted_iota(jnp.int32, (64, 128), 1)
    row = lax.broadcasted_iota(jnp.int32, (64, 128), 0)
    left = lane < 64
    causal = (lane % 64) <= row

    def pair(v):
        zero = jnp.zeros_like(v)
        return jnp.concatenate([jnp.where(left, v, zero), jnp.where(left, zero, v)], axis=0)

    def half_sum(v):
        zero = jnp.zeros_like(v)
        a = jnp.sum(jnp.where(left, v, zero), axis=-1, keepdims=True)
        b = jnp.sum(jnp.where(left, zero, v), axis=-1, keepdims=True)
        return jnp.where(left, a, b)

    def half_max(v):
        low = jnp.full_like(v, -3e38)
        a = jnp.max(jnp.where(left, v, low), axis=-1, keepdims=True)
        b = jnp.max(jnp.where(left, low, v), axis=-1, keepdims=True)
        return jnp.where(left, a, b)

    def head_cols(base, h):
        return pl.ds(base + 128 * h, 128)

    def attend(start):
        rows, heads = pl.ds(start, 64), range(4)
        q = [r.qkv[rows, head_cols(0, h)] for h in heads]
        k = [r.qkv[rows, head_cols(HALF, h)] for h in heads]
        v = [r.qkv[rows, head_cols(2 * HALF, h)] for h in heads]
        g = [r.gp[rows, head_cols(0, h)] for h in heads]
        s = [jnp.where(causal, dot_t(a, pair(b)) * HDIM ** (-0.5), -1e30) for a, b in zip(q, k)]
        e = [jnp.exp(a - half_max(a)) for a in s]
        prob = [a / half_sum(a) for a in e]
        att = [dot(a.astype(BF16), pair(b)) for a, b in zip(prob, v)]
        mix = [(a * (b * jax.nn.sigmoid(b))).astype(BF16) for a, b in zip(att, g)]
        for h in heads:
            r.prob[rows, head_cols(0, h)] = prob[h]
            r.att[rows, head_cols(0, h)] = att[h]
            r.mix[rows, head_cols(0, h)] = mix[h]

    def partial_rows(left, right, slot, start, count):
        rows = pl.ds(start, count)

        def tile(at, width):
            acc = right(left[rows, :], at, width)
            if start < OWN:
                r.po[rows, pl.ds(at, width)] = acc
            else:
                r.es[slot, pl.ds(start - OWN, count), pl.ds(at, width)] = acc.astype(BF16)

        tile_loop(D, 256, tile)

    def out_product(v, at, width):
        return dot(v, r.wo[:, pl.ds(at, width)])

    def hidden_back(v, at, width):
        return dot_t(v, r.wf[pl.ds(at, width), :])

    def heads_back(v, at, width):
        left, right = v[:, : 2 * HALF], v[:, 2 * HALF :]
        return dot_t(left, r.wa[pl.ds(at, width), pl.ds(0, 1024)]) + dot_t(right, r.wa[pl.ds(at, width), pl.ds(1152, 1024)])

    def resid_rows(start):
        rows = pl.ds(start, 64)
        v = r.tok[rows, :].astype(F32) + r.po[rows, :] + r.er[0, rows, :].astype(F32)
        r.res[rows, :] = v
        scale = lax.rsqrt(jnp.mean(v * v, axis=-1, keepdims=True) + EPS)
        r.nt[rows, :] = (v * scale * r.gain[1:2, :]).astype(BF16)

    def hidden(at, width):
        a = dot(r.nt[...], r.wf[:, pl.ds(at, width)]).astype(BF16)
        b = dot(r.nt[...], r.wf[:, pl.ds(FH + at, width)]).astype(BF16)
        r.fs[:, pl.ds(at, width)] = a
        r.fs[:, pl.ds(FH + at, width)] = b
        r.pr[:, pl.ds(at, width)] = (a.astype(F32) * b.astype(F32)).astype(BF16)

    def hidden_grad(at, width):
        pg = dot_t(r.cot[...], r.wd[pl.ds(at, width), :]).astype(BF16).astype(F32)
        a = r.fs[:, pl.ds(at, width)].astype(F32)
        b = r.fs[:, pl.ds(FH + at, width)].astype(F32)
        r.fs[:, pl.ds(at, width)] = (pg * b).astype(BF16)
        r.fs[:, pl.ds(FH + at, width)] = (pg * a).astype(BF16)

    def resid_grad_rows(start):
        rows = pl.ds(start, 64)
        ng = r.po[rows, :] + r.er[1, rows, :].astype(F32)
        v = r.res[rows, :]
        scale = lax.rsqrt(jnp.mean(v * v, axis=-1, keepdims=True) + EPS)
        n = ng * r.gain[1:2, :]
        grad = r.cot[rows, :].astype(F32) + scale * n - v * (scale * scale * scale * jnp.mean(n * v, axis=-1, keepdims=True))
        r.rg[rows, :] = grad
        r.bg[rows, :] = grad.astype(BF16)
        r.gacc[1] += jnp.sum((ng * v * scale).reshape(8, 8, D), axis=0)

    def mixed_grad(start, count):
        rows = pl.ds(start, count)

        def tile(at, width):
            cols = pl.ds(at, width)
            mg = dot_t(r.bg[rows, :], r.wo[pl.ds(at, width), :]).astype(BF16).astype(F32)
            g = r.gp[rows, cols]
            s = jax.nn.sigmoid(g)
            r.dout[rows, cols] = (mg * (g * s)).astype(BF16)
            r.g4[rows, pl.ds(3 * HALF + at, width)] = (mg * r.att[rows, cols] * (s * (1.0 + g * (1.0 - s)))).astype(BF16)

        tile_loop(HALF, 256, tile)

    def attend_grad(start):
        rows, heads = pl.ds(start, 64), range(4)
        q = [r.qkv[rows, head_cols(0, h)] for h in heads]
        k = [r.qkv[rows, head_cols(HALF, h)] for h in heads]
        v = [r.qkv[rows, head_cols(2 * HALF, h)] for h in heads]
        do = [r.dout[rows, head_cols(0, h)] for h in heads]
        prob = [r.prob[rows, head_cols(0, h)] for h in heads]
        pg = [dot_t(a, pair(b)) for a, b in zip(do, v)]
        vg = [t_dot(a.astype(BF16), b) for a, b in zip(prob, do)]
        sg = [(a * (b - half_sum(a * b))).astype(BF16) for a, b in zip(prob, pg)]
        qg = [dot(a, pair(b)) * HDIM ** (-0.5) for a, b in zip(sg, k)]
        kg = [t_dot(a, b) for a, b in zip(sg, q)]
        for h in heads:
            r.g4[rows, head_cols(0, h)] = qg[h].astype(BF16)
            r.g4[rows, head_cols(HALF, h)] = (jnp.where(left, kg[h][:64], kg[h][64:]) * HDIM ** (-0.5)).astype(BF16)
            r.g4[rows, head_cols(2 * HALF, h)] = jnp.where(left, vg[h][:64], vg[h][64:]).astype(BF16)

    def block_out_rows(start):
        rows = pl.ds(start, 64)
        r.bo[rows, :] = (r.res[rows, :] + r.er[0, rows, :].astype(F32)).astype(BF16)

    def block_out_part(at, width):
        acc = dot(r.pr[...], r.wd[:, pl.ds(at, width)])
        r.res[:, pl.ds(at, width)] += acc[:OWN]
        r.es[0, :, pl.ds(at, width)] = acc[OWN:].astype(BF16)

    def tokens_grad_rows(start):
        rows = pl.ds(start, 64)
        ng = r.po[rows, :] + r.er[2, rows, :].astype(F32)
        v = r.tok[rows, :].astype(F32)
        scale = lax.rsqrt(jnp.mean(v * v, axis=-1, keepdims=True) + EPS)
        n = ng * r.gain[0:1, :]
        r.rg[rows, :] = r.rg[rows, :] + scale * n - v * (scale * scale * scale * jnp.mean(n * v, axis=-1, keepdims=True))
        r.gacc[0] += jnp.sum((ng * v * scale).reshape(8, 8, D), axis=0)

    def chunk_dot(i, cc):
        kind, at, cols = CHUNKS[i]
        if kind == "d":
            out = t_dot(r.pr[...], r.cot[:, lanes_of(512 * cc + at, cols)])
        elif kind == "f":
            out = t_dot(r.nt[:, lanes_of(512 * cc, 512)], r.fs[:, pl.ds(at, cols)])
        elif kind == "o":
            out = t_dot(r.mix[...], r.bg[:, lanes_of(512 * cc, cols)])
        else:
            out = t_dot(r.nrm[:, lanes_of(512 * cc, 512)], r.g4[:, pl.ds(at, cols)])
        return out.reshape(4, 2, piece_rows(kind), cols)

    buf = lambda name, i: getattr(r, f"{name}{i}")
    chunk_sends = {}

    def give(i):
        kind, _, cols = CHUNKS[i]
        if i >= 4 and i - 2 in chunk_sends:
            chunk_sends.pop(i - 2).wait_send()
        stage = r.sbd.at[i % 2] if kind == "d" else r.sbf.at[i % 2, :, :, :, pl.ds(0, cols)]
        stage[...] = chunk_dot(i, 1 - c).astype(BF16)
        chunk_sends[i] = send(stage, buf("rb", i), r.r_cs.at[i], r.r_cr.at[i], sib, later=False)

    def take(i):
        arrived(buf("rb", i), r.r_cr.at[i])
        own = buf("ow", i)
        own[...] = (chunk_dot(i, c) + buf("rb", i)[...].astype(F32)).astype(BF16)
        if Z_FIRST[i]:
            to_owners(i)
        else:
            send(own.at[:, 1 - y], buf("yr", i), r.r_ys.at[i], r.r_yr.at[i], yn)

    def z_slot(i, zz):
        own = buf("ow", i)
        return own.at[zz] if Z_FIRST[i] else own.at[zz, y]

    def to_owners(i):
        beside = dev(c, jnp.where(z == 3, 2, 1), y, x)
        far = jnp.where(z == 3, 0, 3)
        send_if(jnp.logical_not(inner), z_slot(i, far), buf("zx", i), r.r_zs.at[i, 2], r.r_zx.at[i], beside)
        for k in (1, 3):
            slot = z_slot(i, zk[k])
            send_if(z != (3 if k == 1 else 0), slot, buf("zr", i).at[3 - k], r.r_zs.at[i, 1 if k == 3 else 0], r.r_zr.at[i, 3 - k], zp[k])
        two = z_slot(i, zk[2])
        send_if(jnp.logical_not(inner), two, buf("zr", i).at[1], r.r_zt.at[i], r.r_zr.at[i, 1], zp[2])

    def pass_far(i):
        two = z_slot(i, zk[2])

        @pl.when(inner)
        def _():
            arrived(buf("zx", i), r.r_zx.at[i])
            two[...] = (two[...].astype(F32) + buf("zx", i)[...].astype(F32)).astype(BF16)

        send_if(inner, two, buf("zr", i).at[1], r.r_zs.at[i, 2], r.r_zr.at[i, 1], zp[2])

    def take_y(i):
        own, part = buf("ow", i), buf("yr", i)
        arrived(part, r.r_yr.at[i])
        if Z_FIRST[i]:
            return
        for k in range(4):
            slot = own.at[zk[k], y]
            slot[...] = (slot[...].astype(F32) + part[zk[k]].astype(F32)).astype(BF16)
        to_owners(i)

    finals = []

    def add_z(i, dst, first, half=None):
        part = buf("zr", i)
        take_part = (lambda j: part[j]) if half is None else (lambda j: part[j, half])
        if not half:
            arrived(part.at[1], r.r_zr.at[i, 1])
        dst[...] = first + take_part(1).astype(F32)
        for j, end in ((0, 3), (2, 0)):

            @pl.when(z != end)
            def _():
                if not half:
                    arrived(part.at[j], r.r_zr.at[i, j])
                dst[...] += take_part(j).astype(F32)

    def owner_sum(i):
        own, fin = buf("ow", i), buf("fin", i)
        for half in range(2):
            add_z(i, fin, own[z, half].astype(F32), half)
            own[z, half] = fin[...].astype(BF16)
        send(own.at[z, 1 - y], buf("yr", i), r.r_ys.at[i], r.r_yr.at[i], yn)

    def take_z(i):
        kind, at, cols = CHUNKS[i]
        own, fin = buf("ow", i), buf("fin", i)
        if Z_FIRST[i]:
            fin[...] = own[z, y].astype(F32) + buf("yr", i)[...].astype(F32)
        else:
            add_z(i, fin, own[z, y].astype(F32))
        if kind in ("f", "a"):
            if kind == "f":
                out, place = (r.g1, FH * x + at) if at < FH else (r.g2, FH * x + at - FH)
            else:
                out, place = (r.gq, r.gk, r.gv, r.gg)[at // 512], HALF * x
            dst = out.at[:, lanes_of(place, cols)]
            finals.append(local(fin.at[rows_of(32 * x, 32, 32)], dst, r.r_fs.at[i, 0]))
            send(fin.at[rows_of(32 * (1 - x), 32, 32)], dst, r.r_fs.at[i, 1], r.r_fr.at[i, 0], xn)
            return
        out = r.gd if kind == "d" else r.go
        n = 88 if kind == "d" else 32
        dst = out.at[:, lanes_of(512 * c + at, cols)]
        for xx in range(2):
            src = fin.at[pl.ds(n * xx, n)]
            itself = jnp.logical_and(x == c, x == xx)

            @pl.when(itself)
            def _():
                local(src, dst, r.r_fr.at[i, c])

            @pl.when(jnp.logical_not(itself))
            def _():
                send(src, dst, r.r_fs.at[i, xx], r.r_fr.at[i, c], dev(x, z, y, xx), later=False)

    def finish(i):
        kind, at, cols = CHUNKS[i]
        if kind in ("f", "a"):
            if kind == "f":
                out, place = (r.g1, FH * (1 - x) + at) if at < FH else (r.g2, FH * (1 - x) + at - FH)
            else:
                out, place = (r.gq, r.gk, r.gv, r.gg)[at // 512], HALF * (1 - x)
            arrived(out.at[:, lanes_of(place, cols)], r.r_fr.at[i, 0])
            return
        out = r.gd if kind == "d" else r.go
        n = 88 if kind == "d" else 32
        for cc in range(2):
            arrived(out.at[:, pl.ds(512 * cc + at, cols)], r.r_fr.at[i, cc])
        for xx in range(2):
            itself = jnp.logical_and(x == c, x == xx)

            @pl.when(jnp.logical_not(itself))
            def _():
                src = buf("fin", i).at[pl.ds(n * xx, n)]
                remote(src, src, r.r_fs.at[i, xx], r.r_fs.at[i, xx], xn).wait_send()

    def over(start, count, fn):
        row_loop(count, 64, lambda at: fn(at + start))

    def swap_rows(i, src, dst, start, count):
        swap(i, src.at[pl.ds(start, count)], dst.at[pl.ds(start, count)])

    def swapped_rows(i, dst, start, count):
        swapped(i, dst.at[pl.ds(start, count)])

    load_tok = local(r.tokens, r.tok.at[pl.ds(0, OWN)], r.s_loc.at[0])
    load_cot = local(r.cot_in, r.cot.at[pl.ds(0, OWN)], r.s_loc.at[1])
    outs = []

    def do_start():
        eye = lax.broadcasted_iota(jnp.int32, (32, 32), 0) == lax.broadcasted_iota(jnp.int32, (32, 32), 1)
        column = lax.broadcasted_iota(jnp.int32, (32, 128), 1)
        total = jnp.zeros((32, 128), F32)
        for i, ref in enumerate((r.gain_a, r.gain_f)):
            values = jnp.broadcast_to(ref[...].astype(F32)[None, :], (32, 32))
            upright = jnp.sum(jnp.where(eye, values, 0.0), axis=1, keepdims=True)
            total = total + jnp.where(column == i, upright, 0.0)
        r.gains[...] = total.astype(BF16)
        start_cols("a")
        start_cols("b")
        r.gacc[...] = jnp.zeros((2, 8, D), F32)

    def do_start2():
        start_rows("o")
        for g in "fsgt":
            start_cols(g)
        start_rows("d")
        swap(0, r.tokens, r.tok.at[pl.ds(OWN, OWN)])
        swap(1, r.cot_in, r.cot.at[pl.ds(OWN, OWN)])

    def do_norm_own():
        load_tok.wait()
        over(0, OWN, lambda start: norm_rows(start, 0, r.po))

    def do_norm_partner():
        swapped(0, r.tok.at[pl.ds(OWN, OWN)])
        over(0, OWN, lambda start: norm_rows(start, OWN, r.rg))

    def do_proj(part):
        if part:
            tile_loop(HALF, 256, lambda at, width: proj(at, width, 2 * HALF))
            tile_loop(HALF, 256, proj_gate)
            return
        unit_row = lax.broadcasted_iota(jnp.int32, (8, 128), 0)
        unit = jnp.where(unit_row == lax.broadcasted_iota(jnp.int32, (8, 128), 1), 1.0, 0.0).astype(BF16)
        r.gain[...] = dot_t(unit, r.wa[:, pl.ds(1024, 128)])
        row_loop(OWN, 64, gain_rows)
        tile_loop(2 * HALF, 256, proj)

    def do_out(start):
        partial_rows(r.mix, out_product, 0, start, 128)
        if start >= OWN:
            swap_rows(2 if start == 256 else 3, r.es.at[0], r.er.at[0], start - OWN, 128)

    def do_resid(start):
        swapped_rows(2 + start // 128, r.er.at[0], start, 128)
        over(start, 128, resid_rows)
        swap(4 + start // 128, r.nt.at[pl.ds(start, 128)], r.nt.at[pl.ds(OWN + start, 128)])

    def do_hidden(part):
        if part:
            tile_loop(640, 256, lambda at, width: hidden(at + 768, width))
            return
        swapped(4, r.nt.at[pl.ds(OWN, 128)])
        swapped(5, r.nt.at[pl.ds(OWN + 128, 128)])
        tile_loop(768, 256, hidden)

    def do_cot():
        load_cot.wait()
        swapped(1, r.cot.at[pl.ds(OWN, OWN)])

    def do_back(start):
        if start == 0:
            partial_rows(r.fs, hidden_back, 1, 0, 256)
            return
        partial_rows(r.fs, hidden_back, 1, start, 128)
        swap_rows(6 if start == 256 else 7, r.es.at[1], r.er.at[1], start - OWN, 128)

    def do_resid_grad(start):
        swapped_rows(6 + start // 128, r.er.at[1], start, 128)
        over(start, 128, resid_grad_rows)
        swap(8 + start // 128, r.bg.at[pl.ds(start, 128)], r.bg.at[pl.ds(OWN + start, 128)])

    def do_mixed_grad(start):
        if start == 0:
            mixed_grad(0, 256)
            return
        swapped(8 if start == 256 else 9, r.bg.at[pl.ds(start, 128)])
        mixed_grad(start, 128)

    def do_heads_back(start):
        partial_rows(r.g4, heads_back, 2, start, 256)
        if start:
            swap(11, r.es.at[2], r.er.at[2])

    def do_block_out():
        swaps.pop(2).wait_send()
        swaps.pop(3).wait_send()
        tile_loop(D, 256, block_out_part)
        swap(10, r.es.at[0], r.er.at[0])

    def do_tokens_grad():
        swapped(11, r.er.at[2])
        over(0, OWN, tokens_grad_rows)
        outs.append(local(r.rg, r.tokens_grad, r.s_out.at[1]))

    def do_block_rows():
        swapped(10, r.er.at[0])
        over(0, OWN, block_out_rows)
        outs.append(local(r.bo, r.block_out, r.s_out.at[0]))

    def do_gsum(n):
        if n == 0:
            which = lax.broadcasted_iota(jnp.int32, (8, D), 0)
            zero = jnp.zeros((8, D), F32)
            sums = [jnp.sum(r.gacc[i], axis=0, keepdims=True) for i in range(2)]
            grad_sum(0, jnp.where(which == 0, sums[0], zero) + jnp.where(which == 1, sums[1], zero))
        elif n < 4:
            grad_sum(n)
        else:
            r.gacc[0] = grad_sum(4)
            outs.append(local(r.gacc.at[0], r.gain_grads, r.s_out.at[2]))

    def do_take_z(i):
        if Z_FIRST[i]:
            take_y(i)
        take_z(i)

    def do_attend(start):
        over(start, 64, attend)

    def do_hidden_grad():
        tile_loop(FH, 256, hidden_grad)

    def do_attend_grad(start):
        over(start, 64, attend_grad)

    work = (
        (do_start,), (own, GA), (own, GB), (do_start2,), (got_z, GA, 1, 0), (own, GO), (got_z, GA, 2, 0),
        (got_z, GB, 1, 0), (do_norm_own,), (got_z, GB, 2, 0), (got_z, GA, 3, 0), (got_y, GO, 0), (got_z, GB, 3, 0),
        (got_y, GA, 0), (got_z, GO, 1, 0), (got_z, GO, 2, 0), (got_z, GO, 3, 0), (got_y, GB, 0), (got_y, GA, 2),
        (own, GS), (got_y, GB, 1), (own, GG), (own, GT), (got_y, GA, 3), (got_y, GB, 2), (own, GD), (got_y, GA, 1),
        (own, GF), (do_norm_partner,), (got_z, GS, 1, 0), (whole, GA), (got_y, GB, 3), (do_proj, 0), (whole, GB),
        (do_proj, 1), (got_y, GO, 1), (got_y, GO, 2), (got_y, GO, 3), (got_z, GG, 1, 0), (do_attend, 256),
        (got_y, GS, 0), (whole, GO), (do_attend, 320), (do_out, 256), (got_z, GG, 2, 0), (got_z, GF, 1, 0),
        (do_attend, 384), (do_attend, 448), (do_out, 384), (got_z, GF, 2, 0), (do_attend, 128), (got_z, GS, 1, 1),
        (got_z, GS, 2, 1), (do_attend, 192), (got_z, GG, 3, 0), (do_attend, 64), (do_attend, 0), (do_out, 0),
        (do_out, 128), (got_z, GF, 3, 0), (do_resid, 0), (got_y, GD, 0), (got_z, GS, 3, 1), (got_z, GT, 1, 0),
        (got_z, GT, 2, 0), (got_z, GT, 3, 0), (got_y, GT, 0), (got_z, GS, 2, 0), (got_y, GG, 0), (got_z, GD, 1, 0),
        (do_resid, 128), (got_z, GD, 2, 0), (got_y, GG, 2), (got_z, GS, 3, 0), (whole, GS), (got_y, GF, 3),
        (got_y, GG, 3), (got_y, GG, 1), (got_y, GF, 2), (got_y, GT, 1), (got_y, GF, 0), (got_y, GF, 1), (whole, GG),
        (whole, GF), (got_y, GT, 2), (got_z, GD, 3, 0), (got_y, GT, 3), (do_hidden, 0), (whole, GT), (do_hidden, 1),
        (do_cot,), (give, 0), (give, 1), (got_y, GD, 1), (got_y, GD, 2), (take, 0), (got_y, GD, 3), (take, 1),
        (whole, GD), (do_hidden_grad,), (give, 2), (do_back, 256), (give, 3), (take, 2), (give, 4), (take, 3),
        (give, 5), (do_back, 384), (take_y, 0), (take, 5), (pass_far, 1), (do_back, 0), (do_resid_grad, 0),
        (take_y, 2), (do_resid_grad, 128), (pass_far, 0), (do_mixed_grad, 0), (do_attend_grad, 64), (owner_sum, 1),
        (do_attend_grad, 128), (do_attend_grad, 0), (do_attend_grad, 192), (take, 4), (do_mixed_grad, 256),
        (pass_far, 2), (do_attend_grad, 320), (do_take_z, 0), (take_y, 3), (do_take_z, 2), (do_attend_grad, 256),
        (do_mixed_grad, 384), (do_attend_grad, 384), (do_attend_grad, 448), (give, 6), (pass_far, 3), (take_y, 5),
        (do_heads_back, 256), (give, 7), (take, 6), (give, 8), (do_take_z, 1), (take, 7), (give, 9), (take, 8),
        (pass_far, 5), (give, 10), (take, 10), (pass_far, 7), (do_take_z, 5), (take_y, 4), (do_take_z, 3),
        (do_heads_back, 0), (do_tokens_grad,), (do_gsum, 0), (take, 9), (do_block_out,), (take_y, 6), (pass_far, 4),
        (do_take_z, 4), (take_y, 8), (finish, 1), (pass_far, 6), (do_take_z, 6), (take_y, 10), (pass_far, 8),
        (owner_sum, 7), (take_y, 9), (do_gsum, 1), (pass_far, 10), (finish, 4), (do_take_z, 8), (pass_far, 9),
        (do_gsum, 2), (do_take_z, 10), (do_take_z, 7), (finish, 0), (finish, 2), (do_gsum, 3), (do_take_z, 9),
        (finish, 10), (do_block_rows,), (finish, 6), (finish, 3), (finish, 5), (finish, 8), (finish, 7), (do_gsum, 4),
        (finish, 9),
    )
    for step, *args in work:
        step(*args)
    for copy in list(chunk_sends.values()) + list(swaps.values()) + sends:
        copy.wait_send()
    for pred, copy in guarded:
        pl.when(pred)(copy.wait_send)
    for copy in finals + outs:
        copy.wait()
    for g in SPANS:
        gi = GROUPS.index(g)
        own = col_shard(g, x)
        remote(own, own, r.s_xs.at[gi, 0], r.s_xs.at[gi, 0], xn).wait_send()
    for g in ("o", "d"):
        gi = GROUPS.index(g)
        block = r.wo.at[pl.ds(0, 32), pl.ds(0, 512)] if g == "o" else r.wds.at[0]

        @pl.when(x != c)
        def _():
            remote(block, block, r.s_xs.at[gi, 0], r.s_xs.at[gi, 0], xn).wait_send()

        remote(block, block, r.s_xs.at[gi, 1], r.s_xs.at[gi, 1], xn).wait_send()


def hand_over(gain_ref, *refs):
    count = (len(refs) - 4) // 3
    ins, (one, two), outs = refs[:count], refs[count : count + 2], refs[count + 2 : 2 * count + 2]
    held, (in_sems, out_sems) = refs[2 * count + 2 : -2], refs[-2:]
    loads = [pltpu.make_async_copy(a, b, in_sems.at[i]) for i, (a, b) in enumerate(zip(ins, held))]
    stores = [pltpu.make_async_copy(a, b, out_sems.at[i]) for i, (a, b) in enumerate(zip(held, outs))]
    for load in loads:
        load.start()
    me = lax.axis_index("dp") * 16 + lax.axis_index("fsdp")
    block = gain_ref[:, lanes_of(128 * (me // 4), 128)]
    block = pltpu.roll(block, lax.rem(128 - 32 * lax.rem(me, 4), 128), 1)
    one[...] = block[0, :32]
    two[...] = block[1, :32]
    for load, store in zip(loads, stores):
        load.wait()
        store.start()
    for store in stores:
        store.wait()


def fused_layer(
    tokens, attn_gain, w_query, w_key, w_value, w_gate, w_output, ffn_gain, w_first, w_second, w_down, cotangent
):
    items = scratch_list()
    names = IN_NAMES + OUT_NAMES + tuple(name for name, _ in items)
    shape = jax.ShapeDtypeStruct
    outs = pl.pallas_call(
        functools.partial(layer_kernel, names),
        out_shape=[
            shape((OWN, D), BF16), shape((OWN, D), F32), shape((8, D), F32),
            shape((32, D), F32), shape((32, D), F32), shape((32, D), F32), shape((32, D), F32), shape((32, D), F32),
            shape((32, FF), F32), shape((32, FF), F32), shape((88, D), F32),
        ],
        in_specs=[pl.BlockSpec(memory_space=pltpu.VMEM if n.startswith("gain") else pl.ANY) for n in IN_NAMES],
        out_specs=[pl.BlockSpec(memory_space=pl.ANY)] * len(OUT_NAMES),
        scratch_shapes=[spec for _, spec in items],
        compiler_params=pltpu.CompilerParams(collective_id=0, has_side_effects=True, vmem_limit_bytes=66 * 2**20 - 2**21),
        name="layer",
    )(tokens, attn_gain, ffn_gain, w_query, w_key, w_value, w_gate, w_output, w_first, w_second, w_down, cotangent)
    block_out, tokens_grad, gain_grads, gq, gk, gv, gg, go, g1, g2, gd = outs
    kept = (block_out, tokens_grad, gq, gk, gv, gg, go, g1, g2, gd)
    anywhere = pl.BlockSpec(memory_space=pl.ANY)
    in_vmem = pl.BlockSpec(memory_space=pltpu.VMEM)
    gain_one, gain_two, *rest = pl.pallas_call(
        hand_over,
        out_shape=[shape((32,), F32)] * 2 + [shape(v.shape, v.dtype) for v in kept],
        in_specs=[in_vmem] + [anywhere] * len(kept),
        out_specs=[in_vmem] * 2 + [anywhere] * len(kept),
        scratch_shapes=[pltpu.VMEM(v.shape, v.dtype) for v in kept] + [pltpu.SemaphoreType.DMA((len(kept),))] * 2,
        compiler_params=pltpu.CompilerParams(vmem_limit_bytes=63 * 2**20),
        name="hand_over",
    )(gain_grads, *kept)
    block_out, tokens_grad, gq, gk, gv, gg, go, g1, g2, gd = rest
    return block_out, tokens_grad, gain_one, gq, gk, gv, gg, go, gain_two, g1, g2, gd


def rms_scale(values, gain):
    return values * lax.rsqrt(jnp.mean(values * values, axis=-1, keepdims=True) + EPS) * gain


def gated(attended, gate_pre):
    return attended * jax.nn.silu(gate_pre)


def contract_rows(left, right):
    return lax.dot_general(
        left, right, (((0,), (0,)), ((), ())), preferred_element_type=jnp.float32
    )


def contract_cols(left, right):
    return lax.dot_general(
        left, right, (((1,), (1,)), ((), ())), preferred_element_type=jnp.float32
    )


def project(left, right):
    return jnp.dot(left, right, preferred_element_type=jnp.float32)


def flatten_rows(matrix):
    return matrix.reshape(-1, 128)


def restore_rows(flat, columns):
    return flat.reshape(-1, columns)


def split_heads(matrix):
    return matrix.reshape(matrix.shape[0] // BLK, BLK, HEADS, HDIM)


def block_scores(queries, keys):
    raw = jnp.einsum(
        "bqhd,bkhd->bhqk",
        split_heads(queries),
        split_heads(keys),
        preferred_element_type=jnp.float32,
    )
    causal = jnp.arange(BLK)[:, None] >= jnp.arange(BLK)[None, :]
    return jnp.where(causal, raw * HDIM ** (-0.5), -1e30)


def attend_forward(queries, keys, values):
    scores = block_scores(queries, keys)
    highest = jnp.max(scores, axis=-1, keepdims=True)
    weights = jnp.exp(scores - highest)
    total = jnp.sum(weights, axis=-1, keepdims=True)
    probs = (weights / total).astype(jnp.bfloat16)
    attended = jnp.einsum(
        "bhqk,bkhd->bqhd", probs, split_heads(values), preferred_element_type=jnp.float32
    )
    return (attended.reshape(queries.shape[0], D), highest + jnp.log(total))


def attend_backward(queries, keys, values, log_total, attended_grad):
    scores = block_scores(queries, keys)
    probs = jnp.exp(scores - log_total)
    grad_heads = split_heads(attended_grad)
    value_grad = jnp.einsum(
        "bhqk,bqhd->bkhd",
        probs.astype(jnp.bfloat16),
        grad_heads,
        preferred_element_type=jnp.float32,
    )
    prob_grad = jnp.einsum(
        "bqhd,bkhd->bhqk", grad_heads, split_heads(values), preferred_element_type=jnp.float32
    )
    score_grad = (probs * (prob_grad - jnp.sum(probs * prob_grad, axis=-1, keepdims=True))).astype(
        jnp.bfloat16
    )
    factor = HDIM ** (-0.5)
    query_grad = (
        jnp.einsum(
            "bhqk,bkhd->bqhd", score_grad, split_heads(keys), preferred_element_type=jnp.float32
        )
        * factor
    )
    key_grad = (
        jnp.einsum(
            "bhqk,bqhd->bkhd", score_grad, split_heads(queries), preferred_element_type=jnp.float32
        )
        * factor
    )
    length = queries.shape[0]
    return (
        query_grad.reshape(length, D).astype(jnp.bfloat16),
        key_grad.reshape(length, D).astype(jnp.bfloat16),
        value_grad.reshape(length, D).astype(jnp.bfloat16),
    )


def on_device(
    tokens,
    attn_gain,
    w_query,
    w_key,
    w_value,
    w_gate,
    w_output,
    ffn_gain,
    w_first,
    w_second,
    w_down,
    cotangent,
):
    attn_whole = (
        lax.all_gather(attn_gain, ("dp", "fsdp"), axis=0, tiled=True),
        lax.all_gather(w_query, ("dp", "fsdp"), axis=0, tiled=True),
        lax.all_gather(w_key, ("dp", "fsdp"), axis=0, tiled=True),
        lax.all_gather(w_value, ("dp", "fsdp"), axis=0, tiled=True),
        lax.all_gather(w_gate, ("dp", "fsdp"), axis=0, tiled=True),
        lax.all_gather(w_output, ("dp", "fsdp"), axis=0, tiled=True),
    )
    gain_one, query_full, key_full, value_full, gate_full, output_full = attn_whole
    inputs = tokens.astype(jnp.float32)
    normed_pre, norm_pull = jax.vjp(rms_scale, inputs, gain_one.astype(jnp.float32))
    normed = normed_pre.astype(jnp.bfloat16)
    queries = project(normed, query_full).astype(jnp.bfloat16)
    keys = project(normed, key_full).astype(jnp.bfloat16)
    values = project(normed, value_full).astype(jnp.bfloat16)
    gate_pre = project(normed, gate_full)
    attended, log_total = attend_forward(queries, keys, values)
    mixed_pre, gate_pull = jax.vjp(gated, attended, gate_pre)
    mixed = mixed_pre.astype(jnp.bfloat16)
    resid = inputs + project(mixed, output_full)
    ffn_whole = (
        lax.all_gather(ffn_gain, ("dp", "fsdp"), axis=0, tiled=True),
        lax.all_gather(w_first, ("dp", "fsdp"), axis=0, tiled=True),
        lax.all_gather(w_second, ("dp", "fsdp"), axis=0, tiled=True),
        lax.all_gather(w_down, ("dp", "fsdp"), axis=0, tiled=True),
    )
    gain_two, first_full, second_full, down_full = ffn_whole
    normed_two_pre, norm_two_pull = jax.vjp(rms_scale, resid, gain_two.astype(jnp.float32))
    normed_two = normed_two_pre.astype(jnp.bfloat16)
    first = project(normed_two, first_full).astype(jnp.bfloat16)
    second = project(normed_two, second_full).astype(jnp.bfloat16)
    product = (first.astype(jnp.float32) * second.astype(jnp.float32)).astype(jnp.bfloat16)
    block_out = (resid + project(product, down_full)).astype(jnp.bfloat16)
    gain_two, first_full, second_full, down_full = (
        lax.all_gather(ffn_gain, ("dp", "fsdp"), axis=0, tiled=True),
        lax.all_gather(w_first, ("dp", "fsdp"), axis=0, tiled=True),
        lax.all_gather(w_second, ("dp", "fsdp"), axis=0, tiled=True),
        lax.all_gather(w_down, ("dp", "fsdp"), axis=0, tiled=True),
    )
    product_grad = contract_cols(cotangent, down_full).astype(jnp.bfloat16)
    product_wide = product_grad.astype(jnp.float32)
    first_grad = (product_wide * second.astype(jnp.float32)).astype(jnp.bfloat16)
    second_grad = (product_wide * first.astype(jnp.float32)).astype(jnp.bfloat16)
    normed_two_grad = contract_cols(first_grad, first_full) + contract_cols(
        second_grad, second_full
    )
    resid_part, gain_two_grad = norm_two_pull(normed_two_grad)
    resid_grad = cotangent.astype(jnp.float32) + resid_part
    down_grad = contract_rows(product, cotangent)
    first_w_grad = contract_rows(normed_two, first_grad)
    second_w_grad = contract_rows(normed_two, second_grad)
    ffn_sums = (
        lax.psum_scatter(gain_two_grad, ("dp", "fsdp"), scatter_dimension=0, tiled=True),
        lax.psum_scatter(
            flatten_rows(first_w_grad), ("dp", "fsdp"), scatter_dimension=0, tiled=True
        ),
        lax.psum_scatter(
            flatten_rows(second_w_grad), ("dp", "fsdp"), scatter_dimension=0, tiled=True
        ),
        lax.psum_scatter(flatten_rows(down_grad), ("dp", "fsdp"), scatter_dimension=0, tiled=True),
    )
    gain_one, query_full, key_full, value_full, gate_full, output_full = (
        lax.all_gather(attn_gain, ("dp", "fsdp"), axis=0, tiled=True),
        lax.all_gather(w_query, ("dp", "fsdp"), axis=0, tiled=True),
        lax.all_gather(w_key, ("dp", "fsdp"), axis=0, tiled=True),
        lax.all_gather(w_value, ("dp", "fsdp"), axis=0, tiled=True),
        lax.all_gather(w_gate, ("dp", "fsdp"), axis=0, tiled=True),
        lax.all_gather(w_output, ("dp", "fsdp"), axis=0, tiled=True),
    )
    branch_grad = resid_grad.astype(jnp.bfloat16)
    mixed_grad = contract_cols(branch_grad, output_full).astype(jnp.bfloat16)
    attended_part, gate_part = gate_pull(mixed_grad.astype(jnp.float32))
    attended_grad = attended_part.astype(jnp.bfloat16)
    gate_grad = gate_part.astype(jnp.bfloat16)
    query_grad, key_grad, value_grad = attend_backward(
        queries, keys, values, log_total, attended_grad
    )
    normed_grad = contract_cols(query_grad, query_full) + contract_cols(key_grad, key_full)
    normed_grad = (
        normed_grad + contract_cols(value_grad, value_full) + contract_cols(gate_grad, gate_full)
    )
    input_part, gain_one_grad = norm_pull(normed_grad)
    tokens_grad = resid_grad + input_part
    output_w_grad = contract_rows(mixed, branch_grad)
    query_w_grad = contract_rows(normed, query_grad)
    key_w_grad = contract_rows(normed, key_grad)
    value_w_grad = contract_rows(normed, value_grad)
    gate_w_grad = contract_rows(normed, gate_grad)
    attn_sums = (
        lax.psum_scatter(gain_one_grad, ("dp", "fsdp"), scatter_dimension=0, tiled=True),
        lax.psum_scatter(
            flatten_rows(query_w_grad), ("dp", "fsdp"), scatter_dimension=0, tiled=True
        ),
        lax.psum_scatter(flatten_rows(key_w_grad), ("dp", "fsdp"), scatter_dimension=0, tiled=True),
        lax.psum_scatter(
            flatten_rows(value_w_grad), ("dp", "fsdp"), scatter_dimension=0, tiled=True
        ),
        lax.psum_scatter(
            flatten_rows(gate_w_grad), ("dp", "fsdp"), scatter_dimension=0, tiled=True
        ),
        lax.psum_scatter(
            flatten_rows(output_w_grad), ("dp", "fsdp"), scatter_dimension=0, tiled=True
        ),
    )
    gain_two_sum, first_flat, second_flat, down_flat = ffn_sums
    gain_one_sum, query_flat, key_flat, value_flat, gate_flat, output_flat = attn_sums
    query_sum = restore_rows(query_flat, D)
    key_sum = restore_rows(key_flat, D)
    value_sum = restore_rows(value_flat, D)
    gate_sum = restore_rows(gate_flat, D)
    output_sum = restore_rows(output_flat, D)
    first_sum = restore_rows(first_flat, FF)
    second_sum = restore_rows(second_flat, FF)
    down_sum = restore_rows(down_flat, D)
    return (
        block_out,
        tokens_grad,
        gain_one_sum,
        query_sum,
        key_sum,
        value_sum,
        gate_sum,
        output_sum,
        gain_two_sum,
        first_sum,
        second_sum,
        down_sum,
    )


def solution(mesh):
    fits = dict(mesh.shape) == {"dp": 2, "fsdp": 16}
    return jax.shard_map(
        fused_layer if fits else on_device,
        mesh=mesh,
        in_specs=(
            P(("dp", "fsdp"), None),
            P(("dp", "fsdp")),
            P(("dp", "fsdp"), None),
            P(("dp", "fsdp"), None),
            P(("dp", "fsdp"), None),
            P(("dp", "fsdp"), None),
            P(("dp", "fsdp"), None),
            P(("dp", "fsdp")),
            P(("dp", "fsdp"), None),
            P(("dp", "fsdp"), None),
            P(("dp", "fsdp"), None),
            P(("dp", "fsdp"), None),
        ),
        out_specs=(
            P(("dp", "fsdp"), None),
            P(("dp", "fsdp"), None),
            P(("dp", "fsdp")),
            P(("dp", "fsdp"), None),
            P(("dp", "fsdp"), None),
            P(("dp", "fsdp"), None),
            P(("dp", "fsdp"), None),
            P(("dp", "fsdp"), None),
            P(("dp", "fsdp")),
            P(("dp", "fsdp"), None),
            P(("dp", "fsdp"), None),
            P(("dp", "fsdp"), None),
        ),
        check_vma=False,
    )
```

```python
import functools

import jax
import jax.numpy as jnp
from jax import lax
from jax.experimental import pallas as pl
from jax.experimental.pallas import tpu as pltpu
from jax.sharding import PartitionSpec as P

D = 1024
HEADS = 16
HDIM = 64
FF = 2816
BLK = 64


EPS = 1e-06


MESH = pl.DeviceIdType.MESH
F32, BF16 = jnp.float32, jnp.bfloat16

OWN = 256
ROWS = 512
HALF = 512
FH = 1408
CHUNKS = (
    ("d", 0, 256), ("d", 256, 256),
    ("f", 0, 768), ("f", 768, 640), ("f", 1408, 768), ("f", 2176, 640),
    ("o", 0, 512),
    ("a", 1536, 512), ("a", 1024, 512), ("a", 512, 512), ("a", 0, 256), ("a", 256, 256),
)
NCH = len(CHUNKS)
Z_FIRST = tuple(i in (1, 7,) for i in range(NCH))
Y_FIRST = ("s",)
GROUPS = ("h", "a", "b", "o", "f", "s", "g", "t", "d")
GH, GA, GB, GO, GF, GS, GG, GT, GD = GROUPS
SPANS = {"h": (0, 1152), "a": (0, 1152), "b": (1152, 1024), "f": (0, 768), "g": (768, 640), "s": (FH, 768), "t": (FH + 768, 640)}


def piece_rows(kind):
    return 176 if kind == "d" else 64


def scratch_list():
    vm, dma = pltpu.VMEM, pltpu.SemaphoreType.DMA
    items = [
        ("wa", vm((D, 4 * HALF + 128), BF16)), ("wf", vm((D, 2 * FH), BF16)),
        ("wo", vm((HALF, D), BF16)), ("wd", vm((FH, D), BF16)), ("wds", vm((2, 88, 512), BF16)),
        ("tok", vm((ROWS, D), BF16)), ("cot", vm((ROWS, D), BF16)), ("nrm", vm((ROWS, D), BF16)),
        ("qkv", vm((ROWS, 3 * HALF), BF16)), ("gp", vm((ROWS, HALF), F32)), ("att", vm((ROWS, HALF), F32)),
        ("prob", vm((ROWS, HALF), F32)), ("mix", vm((ROWS, HALF), BF16)), ("dout", vm((ROWS, HALF), BF16)),
        ("res", vm((OWN, D), F32)), ("nt", vm((ROWS, D), BF16)), ("fs", vm((ROWS, 2 * FH), BF16)),
        ("pr", vm((ROWS, FH), BF16)), ("g4", vm((ROWS, 4 * HALF), BF16)), ("bg", vm((ROWS, D), BF16)),
        ("rg", vm((OWN, D), F32)), ("po", vm((OWN, D), F32)), ("bo", vm((OWN, D), BF16)),
        ("es", vm((3, OWN, D), BF16)), ("er", vm((3, OWN, D), BF16)),
        ("gs", vm((4, 8, D), F32)), ("gr", vm((6, 8, D), F32)), ("gain", vm((8, D), F32)), ("gains", vm((32, 128), BF16)), ("gacc", vm((2, 8, D), F32)),
        ("sbd", vm((2, 4, 2, 176, 256), BF16)), ("sbf", vm((2, 4, 2, 64, 768), BF16)),
    ]
    for i, (kind, _, cols) in enumerate(CHUNKS):
        r = piece_rows(kind)
        items += [
            (f"rb{i}", vm((4, 2, r, cols), BF16)), (f"ow{i}", vm((4, 2, r, cols), BF16)),
            (f"yr{i}", vm((r, cols) if Z_FIRST[i] else (4, r, cols), BF16)),
            (f"zr{i}", vm((3, 2, r, cols) if Z_FIRST[i] else (3, r, cols), BF16)),
            (f"zx{i}", vm((2, r, cols) if Z_FIRST[i] else (r, cols), BF16)),
            (f"fin{i}", vm((r, cols), F32)),
        ]
    n = len(GROUPS)
    items += [
        ("s_loc", dma((4,))), ("s_wl", dma((n,))), ("s_xs", dma((n, 2))), ("s_xr", dma((n,))),
        ("s_es", dma((16,))), ("s_er", dma((16,))),
        ("s_zs", dma((n, 2, 5))), ("s_zr", dma((n, 2, 3))), ("s_ys", dma((n, 4))), ("s_yr", dma((n, 4))),
        ("s_cs", dma((n, 4, 2))), ("s_cr", dma((n, 4, 2))),
        ("s_gs", dma((6,))), ("s_gr", dma((6,))),
        ("r_cs", dma((NCH,))), ("r_cr", dma((NCH,))), ("r_ys", dma((NCH,))), ("r_yr", dma((NCH,))),
        ("r_zs", dma((NCH, 3))), ("r_zr", dma((NCH, 3))), ("r_zx", dma((NCH,))), ("r_zt", dma((NCH,))), ("r_fs", dma((NCH, 2))), ("r_fr", dma((NCH, 2))),
        ("s_out", dma((4,))),
    ]
    return items


IN_NAMES = ("tokens", "gain_a", "gain_f", "wq", "wk", "wv", "wg", "wo_in", "w1", "w2", "wd_in", "cot_in")
OUT_NAMES = ("block_out", "tokens_grad", "gain_grads", "gq", "gk", "gv", "gg", "go", "g1", "g2", "gd")


class Refs:
    def __init__(self, names, refs):
        self.__dict__.update(zip(names, refs))


def rows_of(start, count, unit=8):
    return pl.ds(pl.multiple_of(start, unit), count)


def lanes_of(start, count):
    return pl.ds(pl.multiple_of(start, 128), count)


def dot(a, b):
    return jnp.dot(a, b, preferred_element_type=F32)


def dot_t(a, b):
    return lax.dot_general(a, b, (((1,), (1,)), ((), ())), preferred_element_type=F32)


def t_dot(a, b):
    return lax.dot_general(a, b, (((0,), (0,)), ((), ())), preferred_element_type=F32)


def tile_loop(total, width, fn):
    count = total // width
    if count == 1:
        fn(0, width)
    else:
        lax.fori_loop(0, count, lambda i, u: (fn(pl.multiple_of(i * width, width), width), u)[1], 0)
    if total % width:
        fn(count * width, total % width)


def row_loop(total, step, fn):
    lax.fori_loop(0, total // step, lambda i, u: (fn(pl.multiple_of(i * step, step)), u)[1], 0)


def layer_kernel(names, *refs):
    r = Refs(names, refs)
    c = lax.axis_index("dp")
    f = lax.axis_index("fsdp")
    z, y, x = f // 4, (f // 2) % 2, f % 2

    def dev(cc, zz, yy, xx):
        return (cc, zz * 4 + yy * 2 + xx)

    xn, yn, sib, diag = dev(c, z, y, 1 - x), dev(c, z, 1 - y, x), dev(1 - c, z, y, x), dev(1 - c, z, y, 1 - x)
    zk = [(z + k) % 4 for k in range(4)]
    zp = [dev(c, zk[k], y, x) for k in range(4)]

    barrier = pltpu.get_barrier_semaphore()
    for peer in (xn, yn, sib, diag, zp[1], zp[2], zp[3]):
        pl.semaphore_signal(barrier, inc=1, device_id=peer, device_id_type=MESH)
    pl.semaphore_wait(barrier, 7)

    sends, guarded = [], []
    inner = jnp.logical_and(z != 0, z != 3)

    def remote(src, dst, ss, rs, to):
        return pltpu.make_async_remote_copy(
            src_ref=src, dst_ref=dst, send_sem=ss, recv_sem=rs, device_id=to, device_id_type=MESH
        )

    def send(src, dst, ss, rs, to, later=True):
        copy = remote(src, dst, ss, rs, to)
        copy.start()
        if later:
            sends.append(copy)
        return copy

    def send_if(pred, src, dst, ss, rs, to):
        copy = remote(src, dst, ss, rs, to)
        pl.when(pred)(copy.start)
        guarded.append((pred, copy))

    def arrived(ref, sem):
        remote(ref, ref, sem, sem, xn).wait_recv()

    def local(src, dst, sem):
        copy = pltpu.make_async_copy(src, dst, sem)
        copy.start()
        return copy

    mine = x
    p = c * 8 + z * 2 + y
    m = z * 2 + y

    def piece(g, cc, zz, yy):
        if g in "ha":
            part = x if g == "h" else 1 - x
            return r.wa.at[rows_of(64 * (cc * 8 + zz * 2 + yy) + 32 * part, 32, 32), pl.ds(*SPANS[g])]
        if g in SPANS:
            full = r.wa if g == "b" else r.wf
            return full.at[rows_of(64 * (cc * 8 + zz * 2 + yy), 64, 64), pl.ds(*SPANS[g])]
        if g == "o":
            return r.wo.at[rows_of(64 * (zz * 2 + yy), 64, 64), lanes_of(512 * cc, 512)]
        return r.wd.at[rows_of(176 * (zz * 2 + yy), 176, 16), lanes_of(512 * cc, 512)]

    def col_shard(g, who):
        row = rows_of(64 * p + 32 * who, 32, 32)
        return (r.wa if g in "hab" else r.wf).at[row, pl.ds(*SPANS[g])]

    def start_cols(g):
        gi = GROUPS.index(g)
        if g == "a":
            parts = [(r.wq, HALF, 0, HALF, 0), (r.wk, HALF, 0, HALF, HALF)]
        elif g == "b":
            parts = [(r.wv, HALF, 0, HALF, 1152), (r.wg, HALF, 0, HALF, 1152 + HALF)]
        else:
            at, cols = SPANS[g]
            parts = [(r.w1 if g in "fg" else r.w2, FH, at % FH, cols, at)]
        full = r.wa if g in "ab" else r.wf
        row = rows_of(64 * p + 32 * x, 32, 32)
        if g == "a":
            local(r.gains, full.at[row, pl.ds(1024, 128)], r.s_wl.at[gi])
            send(r.gains, full.at[row, pl.ds(1024, 128)], r.s_xs.at[gi, 0], r.s_xr.at[gi], xn, later=False)
        for w, half, first, cols, at in parts:
            dst = full.at[row, pl.ds(at, cols)]
            local(w.at[:, lanes_of(half * x + first, cols)], dst, r.s_wl.at[gi])
            send(
                w.at[:, lanes_of(half * (1 - x) + first, cols)], dst,
                r.s_xs.at[gi, 0], r.s_xr.at[gi], xn, later=False,
            )

    def start_rows(g):
        gi = GROUPS.index(g)
        w = r.wo_in if g == "o" else r.wd_in

        def place(h):
            if g == "o":
                return r.wo.at[rows_of(64 * m + 32 * x, 32, 32), lanes_of(512 * h, 512)]
            return r.wds.at[x]

        @pl.when(x == c)
        def _():
            local(w.at[:, lanes_of(512 * c, 512)], place(c), r.s_xr.at[gi])

        @pl.when(x != c)
        def _():
            send(w.at[:, lanes_of(512 * c, 512)], place(c), r.s_xs.at[gi, 0], r.s_xr.at[gi], xn, later=False)

        send(
            w.at[:, lanes_of(512 * (1 - c), 512)], place(1 - c), r.s_xs.at[gi, 1], r.s_xr.at[gi], dev(1 - c, z, y, c),
            later=False,
        )

    def piece_ready(g):
        gi = GROUPS.index(g)
        if g == "a":
            arrived(col_shard(g, 1 - x), r.s_xr.at[gi])
        elif g in SPANS:
            own = col_shard(g, x)
            pltpu.make_async_copy(own, own, r.s_wl.at[GROUPS.index("a") if g == "h" else gi]).wait()
            if g != "h":
                arrived(col_shard(g, 1 - x), r.s_xr.at[gi])
        elif g == "o":
            arrived(piece("o", c, z, y), r.s_xr.at[gi])
        else:
            arrived(r.wds, r.s_xr.at[gi])
            both = jnp.concatenate([r.wds[0].astype(F32), r.wds[1].astype(F32)], axis=0)
            r.wd[rows_of(176 * m, 176, 16), lanes_of(512 * c, 512)] = both.astype(BF16)

    near = [
        jnp.where(z < 2, 1, 3),
        jnp.where(z == 1, 3, jnp.where(z == 2, 1, 2)),
        jnp.where(z == 0, 3, jnp.where(z == 3, 1, 2)),
    ]

    def near_z(n):
        return z if n == 0 else lax.rem(z + near[n - 1], 4)

    def up_down(g, yy, j):
        gi = GROUPS.index(g)
        own = piece(g, c, z, yy)
        send_if(z < 3, own, own, r.s_zs.at[gi, j, 0], r.s_zr.at[gi, j, 2], zp[1])
        send_if(z > 0, own, own, r.s_zs.at[gi, j, 1], r.s_zr.at[gi, j, 0], zp[3])

    def across(g, n):
        gi = GROUPS.index(g)
        ref = piece(g, c, near_z(n), y)
        send(ref, ref, r.s_ys.at[gi, n], r.s_yr.at[gi, n], yn)

    def to_core(g, n, j):
        gi = GROUPS.index(g)
        ref = piece(g, c, near_z(n), y if j == 0 else 1 - y)
        send(ref, ref, r.s_cs.at[gi, n, j], r.s_cr.at[gi, n, j], sib)

    def own(g):
        piece_ready(g)
        if g in Y_FIRST:
            across(g, 0)
            up_down(g, y, 0)
        else:
            up_down(g, y, 0)
            across(g, 0)
        to_core(g, 0, 0)

    def got_z(g, n, j=0):
        gi = GROUPS.index(g)
        got = piece(g, c, near_z(n), y if j == 0 else 1 - y)
        arrived(got, r.s_zr.at[gi, j, near[n - 1] - 1])
        src = near_z(n)
        to = jnp.where(src > z, z - 1, z + 1)
        slot = lax.rem(src - to + 4, 4) - 1
        send_if(inner, got, got, r.s_zs.at[gi, j, 1 + n], r.s_zr.at[gi, j, slot], dev(c, to, y, x))
        if g not in Y_FIRST:
            across(g, n)
        to_core(g, n, j)

    def got_y(g, n):
        gi = GROUPS.index(g)
        arrived(piece(g, c, near_z(n), 1 - y), r.s_yr.at[gi, n])
        if g in Y_FIRST:
            up_down(g, 1 - y, 1)
        to_core(g, n, 1)

    def spread_z(g):
        for j in range(2 if g in Y_FIRST else 1):
            for n in (1, 2, 3):
                got_z(g, n, j)

    def spread_y(g):
        for n in range(1 if g in Y_FIRST else 4):
            got_y(g, n)

    def whole(g):
        gi = GROUPS.index(g)
        for k in range(4):
            for j in range(2):
                arrived(piece(g, 1 - c, near_z(k), y if j == 0 else 1 - y), r.s_cr.at[gi, k, j])

    swaps = {}

    def swap(i, src, dst):
        swaps[i] = send(src, dst, r.s_es.at[i], r.s_er.at[i], xn, later=False)

    def swapped(i, dst):
        arrived(dst, r.s_er.at[i])

    def grad_sum(n, value=None):
        def out(slot, to):
            send(r.gs.at[min(slot, 3)], r.gr.at[slot], r.s_gs.at[slot], r.s_gr.at[slot], to)

        def got(slot):
            arrived(r.gr.at[slot], r.s_gr.at[slot])
            return r.gr[slot]

        if n == 0:
            r.gs[0] = value
            out(0, xn)
        elif n < 3:
            r.gs[n] = r.gs[n - 1] + got(n - 1)
            out(n, yn if n == 1 else sib)
        elif n == 3:
            r.gs[3] = r.gs[2] + got(2)
            for k in (1, 2, 3):
                send(r.gs.at[3], r.gr.at[6 - k], r.s_gs.at[2 + k], r.s_gr.at[6 - k], zp[k])
        else:
            return r.gs[3] + (got(3) + got(4) + got(5))

    def norm_rows(start, at, out):
        v = r.tok[pl.ds(start + at, 64), :].astype(F32)
        scale = lax.rsqrt(jnp.mean(v * v, axis=-1, keepdims=True) + EPS)
        out[pl.ds(start, 64), :] = v * scale

    def gain_rows(start):
        rows = pl.ds(start, 64)
        r.nrm[rows, :] = (r.po[rows, :] * r.gain[0:1, :]).astype(BF16)
        r.nrm[pl.ds(start + OWN, 64), :] = (r.rg[rows, :] * r.gain[0:1, :]).astype(BF16)

    def proj(at, width, shift=0):
        r.qkv[:, pl.ds(at + shift, width)] = dot(r.nrm[...], r.wa[:, pl.ds(at + shift + shift // 8, width)]).astype(BF16)

    def proj_gate(at, width):
        r.gp[:, pl.ds(at, width)] = dot(r.nrm[...], r.wa[:, pl.ds(1152 + HALF + at, width)])

    lane = lax.broadcasted_iota(jnp.int32, (64, 128), 1)
    row = lax.broadcasted_iota(jnp.int32, (64, 128), 0)
    left = lane < 64
    causal = (lane % 64) <= row

    def pair(v):
        zero = jnp.zeros_like(v)
        return jnp.concatenate([jnp.where(left, v, zero), jnp.where(left, zero, v)], axis=0)

    def half_sum(v):
        zero = jnp.zeros_like(v)
        a = jnp.sum(jnp.where(left, v, zero), axis=-1, keepdims=True)
        b = jnp.sum(jnp.where(left, zero, v), axis=-1, keepdims=True)
        return jnp.where(left, a, b)

    def half_max(v):
        low = jnp.full_like(v, -3e38)
        a = jnp.max(jnp.where(left, v, low), axis=-1, keepdims=True)
        b = jnp.max(jnp.where(left, low, v), axis=-1, keepdims=True)
        return jnp.where(left, a, b)

    def head_cols(base, h):
        return pl.ds(base + 128 * h, 128)

    def attend(start):
        rows, heads = pl.ds(start, 64), range(4)
        q = [r.qkv[rows, head_cols(0, h)] for h in heads]
        k = [r.qkv[rows, head_cols(HALF, h)] for h in heads]
        v = [r.qkv[rows, head_cols(2 * HALF, h)] for h in heads]
        g = [r.gp[rows, head_cols(0, h)] for h in heads]
        s = [jnp.where(causal, dot_t(a, pair(b)) * HDIM ** (-0.5), -1e30) for a, b in zip(q, k)]
        e = [jnp.exp(a - half_max(a)) for a in s]
        prob = [a / half_sum(a) for a in e]
        att = [dot(a.astype(BF16), pair(b)) for a, b in zip(prob, v)]
        mix = [(a * (b * jax.nn.sigmoid(b))).astype(BF16) for a, b in zip(att, g)]
        for h in heads:
            r.prob[rows, head_cols(0, h)] = prob[h]
            r.att[rows, head_cols(0, h)] = att[h]
            r.mix[rows, head_cols(0, h)] = mix[h]

    def partial_rows(left, right, slot, start, count):
        rows = pl.ds(start, count)

        def tile(at, width):
            acc = right(left[rows, :], at, width)
            if start < OWN:
                r.po[rows, pl.ds(at, width)] = acc
            else:
                r.es[slot, pl.ds(start - OWN, count), pl.ds(at, width)] = acc.astype(BF16)

        tile_loop(D, 256, tile)

    def out_product(v, at, width):
        return dot(v, r.wo[:, pl.ds(at, width)])

    def hidden_back(v, at, width):
        return dot_t(v, r.wf[pl.ds(at, width), :])

    def heads_back(v, at, width):
        left, right = v[:, : 2 * HALF], v[:, 2 * HALF :]
        return dot_t(left, r.wa[pl.ds(at, width), pl.ds(0, 1024)]) + dot_t(right, r.wa[pl.ds(at, width), pl.ds(1152, 1024)])

    def resid_rows(start):
        rows = pl.ds(start, 64)
        v = r.tok[rows, :].astype(F32) + r.po[rows, :] + r.er[0, rows, :].astype(F32)
        r.res[rows, :] = v
        scale = lax.rsqrt(jnp.mean(v * v, axis=-1, keepdims=True) + EPS)
        r.nt[rows, :] = (v * scale * r.gain[1:2, :]).astype(BF16)

    def hidden(at, width):
        a = dot(r.nt[...], r.wf[:, pl.ds(at, width)]).astype(BF16)
        b = dot(r.nt[...], r.wf[:, pl.ds(FH + at, width)]).astype(BF16)
        r.fs[:, pl.ds(at, width)] = a
        r.fs[:, pl.ds(FH + at, width)] = b
        r.pr[:, pl.ds(at, width)] = (a.astype(F32) * b.astype(F32)).astype(BF16)

    def hidden_grad(at, width):
        pg = dot_t(r.cot[...], r.wd[pl.ds(at, width), :]).astype(BF16).astype(F32)
        a = r.fs[:, pl.ds(at, width)].astype(F32)
        b = r.fs[:, pl.ds(FH + at, width)].astype(F32)
        r.fs[:, pl.ds(at, width)] = (pg * b).astype(BF16)
        r.fs[:, pl.ds(FH + at, width)] = (pg * a).astype(BF16)

    def resid_grad_rows(start):
        rows = pl.ds(start, 64)
        ng = r.po[rows, :] + r.er[1, rows, :].astype(F32)
        v = r.res[rows, :]
        scale = lax.rsqrt(jnp.mean(v * v, axis=-1, keepdims=True) + EPS)
        n = ng * r.gain[1:2, :]
        grad = r.cot[rows, :].astype(F32) + scale * n - v * (scale * scale * scale * jnp.mean(n * v, axis=-1, keepdims=True))
        r.rg[rows, :] = grad
        r.bg[rows, :] = grad.astype(BF16)
        r.gacc[1] += jnp.sum((ng * v * scale).reshape(8, 8, D), axis=0)

    def mixed_grad(start, count):
        rows = pl.ds(start, count)

        def tile(at, width):
            cols = pl.ds(at, width)
            mg = dot_t(r.bg[rows, :], r.wo[pl.ds(at, width), :]).astype(BF16).astype(F32)
            g = r.gp[rows, cols]
            s = jax.nn.sigmoid(g)
            r.dout[rows, cols] = (mg * (g * s)).astype(BF16)
            r.g4[rows, pl.ds(3 * HALF + at, width)] = (mg * r.att[rows, cols] * (s * (1.0 + g * (1.0 - s)))).astype(BF16)

        tile_loop(HALF, 256, tile)

    def attend_grad(start):
        rows, heads = pl.ds(start, 64), range(4)
        q = [r.qkv[rows, head_cols(0, h)] for h in heads]
        k = [r.qkv[rows, head_cols(HALF, h)] for h in heads]
        v = [r.qkv[rows, head_cols(2 * HALF, h)] for h in heads]
        do = [r.dout[rows, head_cols(0, h)] for h in heads]
        prob = [r.prob[rows, head_cols(0, h)] for h in heads]
        pg = [dot_t(a, pair(b)) for a, b in zip(do, v)]
        vg = [t_dot(a.astype(BF16), b) for a, b in zip(prob, do)]
        sg = [(a * (b - half_sum(a * b))).astype(BF16) for a, b in zip(prob, pg)]
        qg = [dot(a, pair(b)) * HDIM ** (-0.5) for a, b in zip(sg, k)]
        kg = [t_dot(a, b) for a, b in zip(sg, q)]
        for h in heads:
            r.g4[rows, head_cols(0, h)] = qg[h].astype(BF16)
            r.g4[rows, head_cols(HALF, h)] = (jnp.where(left, kg[h][:64], kg[h][64:]) * HDIM ** (-0.5)).astype(BF16)
            r.g4[rows, head_cols(2 * HALF, h)] = jnp.where(left, vg[h][:64], vg[h][64:]).astype(BF16)

    def block_out_rows(start):
        rows = pl.ds(start, 64)
        r.bo[rows, :] = (r.res[rows, :] + r.er[0, rows, :].astype(F32)).astype(BF16)

    def block_out_part(at, width):
        acc = dot(r.pr[...], r.wd[:, pl.ds(at, width)])
        r.res[:, pl.ds(at, width)] += acc[:OWN]
        r.es[0, :, pl.ds(at, width)] = acc[OWN:].astype(BF16)

    def tokens_grad_rows(start):
        rows = pl.ds(start, 64)
        ng = r.po[rows, :] + r.er[2, rows, :].astype(F32)
        v = r.tok[rows, :].astype(F32)
        scale = lax.rsqrt(jnp.mean(v * v, axis=-1, keepdims=True) + EPS)
        n = ng * r.gain[0:1, :]
        r.rg[rows, :] = r.rg[rows, :] + scale * n - v * (scale * scale * scale * jnp.mean(n * v, axis=-1, keepdims=True))
        r.gacc[0] += jnp.sum((ng * v * scale).reshape(8, 8, D), axis=0)

    def chunk_dot(i, cc):
        kind, at, cols = CHUNKS[i]
        if kind == "d":
            out = t_dot(r.pr[...], r.cot[:, lanes_of(512 * cc + at, cols)])
        elif kind == "f":
            out = t_dot(r.nt[:, lanes_of(512 * cc, 512)], r.fs[:, pl.ds(at, cols)])
        elif kind == "o":
            out = t_dot(r.mix[...], r.bg[:, lanes_of(512 * cc, cols)])
        else:
            out = t_dot(r.nrm[:, lanes_of(512 * cc, 512)], r.g4[:, pl.ds(at, cols)])
        return out.reshape(4, 2, piece_rows(kind), cols)

    buf = lambda name, i: getattr(r, f"{name}{i}")
    chunk_sends = {}

    def give(i):
        kind, _, cols = CHUNKS[i]
        if i >= 4 and i - 2 in chunk_sends:
            chunk_sends.pop(i - 2).wait_send()
        stage = r.sbd.at[i % 2] if kind == "d" else r.sbf.at[i % 2, :, :, :, pl.ds(0, cols)]
        stage[...] = chunk_dot(i, 1 - c).astype(BF16)
        chunk_sends[i] = send(stage, buf("rb", i), r.r_cs.at[i], r.r_cr.at[i], sib, later=False)

    def take(i):
        arrived(buf("rb", i), r.r_cr.at[i])
        own = buf("ow", i)
        own[...] = (chunk_dot(i, c) + buf("rb", i)[...].astype(F32)).astype(BF16)
        if Z_FIRST[i]:
            to_owners(i)
        else:
            send(own.at[:, 1 - y], buf("yr", i), r.r_ys.at[i], r.r_yr.at[i], yn)

    def z_slot(i, zz):
        own = buf("ow", i)
        return own.at[zz] if Z_FIRST[i] else own.at[zz, y]

    def to_owners(i):
        beside = dev(c, jnp.where(z == 3, 2, 1), y, x)
        far = jnp.where(z == 3, 0, 3)
        send_if(jnp.logical_not(inner), z_slot(i, far), buf("zx", i), r.r_zs.at[i, 2], r.r_zx.at[i], beside)
        for k in (1, 3):
            slot = z_slot(i, zk[k])
            send_if(z != (3 if k == 1 else 0), slot, buf("zr", i).at[3 - k], r.r_zs.at[i, 1 if k == 3 else 0], r.r_zr.at[i, 3 - k], zp[k])
        two = z_slot(i, zk[2])
        send_if(jnp.logical_not(inner), two, buf("zr", i).at[1], r.r_zt.at[i], r.r_zr.at[i, 1], zp[2])

    def pass_far(i):
        two = z_slot(i, zk[2])

        @pl.when(inner)
        def _():
            arrived(buf("zx", i), r.r_zx.at[i])
            two[...] = (two[...].astype(F32) + buf("zx", i)[...].astype(F32)).astype(BF16)

        send_if(inner, two, buf("zr", i).at[1], r.r_zs.at[i, 2], r.r_zr.at[i, 1], zp[2])

    def take_y(i):
        own, part = buf("ow", i), buf("yr", i)
        arrived(part, r.r_yr.at[i])
        if Z_FIRST[i]:
            return
        for k in range(4):
            slot = own.at[zk[k], y]
            slot[...] = (slot[...].astype(F32) + part[zk[k]].astype(F32)).astype(BF16)
        to_owners(i)

    finals = []

    def add_z(i, dst, first, half=None):
        part = buf("zr", i)
        take_part = (lambda j: part[j]) if half is None else (lambda j: part[j, half])
        if not half:
            arrived(part.at[1], r.r_zr.at[i, 1])
        dst[...] = first + take_part(1).astype(F32)
        for j, end in ((0, 3), (2, 0)):

            @pl.when(z != end)
            def _():
                if not half:
                    arrived(part.at[j], r.r_zr.at[i, j])
                dst[...] += take_part(j).astype(F32)

    def owner_sum(i):
        own, fin = buf("ow", i), buf("fin", i)
        for half in range(2):
            add_z(i, fin, own[z, half].astype(F32), half)
            own[z, half] = fin[...].astype(BF16)
        send(own.at[z, 1 - y], buf("yr", i), r.r_ys.at[i], r.r_yr.at[i], yn)

    def take_z(i):
        kind, at, cols = CHUNKS[i]
        own, fin = buf("ow", i), buf("fin", i)
        if Z_FIRST[i]:
            fin[...] = own[z, y].astype(F32) + buf("yr", i)[...].astype(F32)
        else:
            add_z(i, fin, own[z, y].astype(F32))
        if kind in ("f", "a"):
            if kind == "f":
                out, place = (r.g1, FH * x + at) if at < FH else (r.g2, FH * x + at - FH)
            else:
                out, place = (r.gq, r.gk, r.gv, r.gg)[at // 512], HALF * x + at % 512
            dst = out.at[:, lanes_of(place, cols)]
            finals.append(local(fin.at[rows_of(32 * x, 32, 32)], dst, r.r_fs.at[i, 0]))
            send(fin.at[rows_of(32 * (1 - x), 32, 32)], dst, r.r_fs.at[i, 1], r.r_fr.at[i, 0], xn)
            return
        out = r.gd if kind == "d" else r.go
        n = 88 if kind == "d" else 32
        dst = out.at[:, lanes_of(512 * c + at, cols)]
        for xx in range(2):
            src = fin.at[pl.ds(n * xx, n)]
            itself = jnp.logical_and(x == c, x == xx)

            @pl.when(itself)
            def _():
                local(src, dst, r.r_fr.at[i, c])

            @pl.when(jnp.logical_not(itself))
            def _():
                send(src, dst, r.r_fs.at[i, xx], r.r_fr.at[i, c], dev(x, z, y, xx), later=False)

    def finish(i):
        kind, at, cols = CHUNKS[i]
        if kind in ("f", "a"):
            if kind == "f":
                out, place = (r.g1, FH * (1 - x) + at) if at < FH else (r.g2, FH * (1 - x) + at - FH)
            else:
                out, place = (r.gq, r.gk, r.gv, r.gg)[at // 512], HALF * (1 - x) + at % 512
            arrived(out.at[:, lanes_of(place, cols)], r.r_fr.at[i, 0])
            return
        out = r.gd if kind == "d" else r.go
        n = 88 if kind == "d" else 32
        for cc in range(2):
            arrived(out.at[:, pl.ds(512 * cc + at, cols)], r.r_fr.at[i, cc])
        for xx in range(2):
            itself = jnp.logical_and(x == c, x == xx)

            @pl.when(jnp.logical_not(itself))
            def _():
                src = buf("fin", i).at[pl.ds(n * xx, n)]
                remote(src, src, r.r_fs.at[i, xx], r.r_fs.at[i, xx], xn).wait_send()

    def over(start, count, fn):
        row_loop(count, 64, lambda at: fn(at + start))

    def swap_rows(i, src, dst, start, count):
        swap(i, src.at[pl.ds(start, count)], dst.at[pl.ds(start, count)])

    def swapped_rows(i, dst, start, count):
        swapped(i, dst.at[pl.ds(start, count)])

    load_tok = local(r.tokens, r.tok.at[pl.ds(0, OWN)], r.s_loc.at[0])
    load_cot = local(r.cot_in, r.cot.at[pl.ds(0, OWN)], r.s_loc.at[1])
    outs = []

    def do_start():
        eye = lax.broadcasted_iota(jnp.int32, (32, 32), 0) == lax.broadcasted_iota(jnp.int32, (32, 32), 1)
        column = lax.broadcasted_iota(jnp.int32, (32, 128), 1)
        total = jnp.zeros((32, 128), F32)
        for i, ref in enumerate((r.gain_a, r.gain_f)):
            values = jnp.broadcast_to(ref[...].astype(F32)[None, :], (32, 32))
            upright = jnp.sum(jnp.where(eye, values, 0.0), axis=1, keepdims=True)
            total = total + jnp.where(column == i, upright, 0.0)
        r.gains[...] = total.astype(BF16)
        start_cols("a")
        start_cols("b")
        r.gacc[...] = jnp.zeros((2, 8, D), F32)

    def do_start2():
        start_rows("o")
        for g in "fsgt":
            start_cols(g)
        start_rows("d")
        swap(0, r.tokens, r.tok.at[pl.ds(OWN, OWN)])
        swap(1, r.cot_in, r.cot.at[pl.ds(OWN, OWN)])

    def do_norm_own():
        load_tok.wait()
        over(0, OWN, lambda start: norm_rows(start, 0, r.po))

    def do_norm_partner():
        swapped(0, r.tok.at[pl.ds(OWN, OWN)])
        over(0, OWN, lambda start: norm_rows(start, OWN, r.rg))

    def do_proj(part):
        if part:
            tile_loop(HALF, 256, lambda at, width: proj(at, width, 2 * HALF))
            tile_loop(HALF, 256, proj_gate)
            return
        unit_row = lax.broadcasted_iota(jnp.int32, (8, 128), 0)
        unit = jnp.where(unit_row == lax.broadcasted_iota(jnp.int32, (8, 128), 1), 1.0, 0.0).astype(BF16)
        r.gain[...] = dot_t(unit, r.wa[:, pl.ds(1024, 128)])
        row_loop(OWN, 64, gain_rows)
        tile_loop(2 * HALF, 256, proj)

    def do_out(start):
        partial_rows(r.mix, out_product, 0, start, 128)
        if start >= OWN:
            swap_rows(2 if start == 256 else 3, r.es.at[0], r.er.at[0], start - OWN, 128)

    def do_resid(start):
        swapped_rows(2 + start // 128, r.er.at[0], start, 128)
        over(start, 128, resid_rows)
        swap(4 + start // 128, r.nt.at[pl.ds(start, 128)], r.nt.at[pl.ds(OWN + start, 128)])

    def do_hidden(part):
        if part:
            tile_loop(640, 256, lambda at, width: hidden(at + 768, width))
            return
        swapped(4, r.nt.at[pl.ds(OWN, 128)])
        swapped(5, r.nt.at[pl.ds(OWN + 128, 128)])
        tile_loop(768, 256, hidden)

    def do_cot():
        load_cot.wait()
        swapped(1, r.cot.at[pl.ds(OWN, OWN)])

    def do_back(start):
        if start == 0:
            partial_rows(r.fs, hidden_back, 1, 0, 256)
            return
        partial_rows(r.fs, hidden_back, 1, start, 128)
        swap_rows(6 if start == 256 else 7, r.es.at[1], r.er.at[1], start - OWN, 128)

    def do_resid_grad(start):
        swapped_rows(6 + start // 128, r.er.at[1], start, 128)
        over(start, 128, resid_grad_rows)
        swap(8 + start // 128, r.bg.at[pl.ds(start, 128)], r.bg.at[pl.ds(OWN + start, 128)])

    def do_mixed_grad(start):
        if start == 0:
            mixed_grad(0, 256)
            return
        swapped(8 if start == 256 else 9, r.bg.at[pl.ds(start, 128)])
        mixed_grad(start, 128)

    def do_heads_back(start):
        partial_rows(r.g4, heads_back, 2, start, 256)
        if start:
            swap(11, r.es.at[2], r.er.at[2])

    def do_block_out():
        swaps.pop(2).wait_send()
        swaps.pop(3).wait_send()
        tile_loop(D, 256, block_out_part)
        swap(10, r.es.at[0], r.er.at[0])

    def do_tokens_grad():
        swapped(11, r.er.at[2])
        over(0, OWN, tokens_grad_rows)
        outs.append(local(r.rg, r.tokens_grad, r.s_out.at[1]))

    def do_block_rows():
        swapped(10, r.er.at[0])
        over(0, OWN, block_out_rows)
        outs.append(local(r.bo, r.block_out, r.s_out.at[0]))

    def do_gsum(n):
        if n == 0:
            which = lax.broadcasted_iota(jnp.int32, (8, D), 0)
            zero = jnp.zeros((8, D), F32)
            sums = [jnp.sum(r.gacc[i], axis=0, keepdims=True) for i in range(2)]
            grad_sum(0, jnp.where(which == 0, sums[0], zero) + jnp.where(which == 1, sums[1], zero))
        elif n < 4:
            grad_sum(n)
        else:
            r.gacc[0] = grad_sum(4)
            outs.append(local(r.gacc.at[0], r.gain_grads, r.s_out.at[2]))

    def do_take_z(i):
        if Z_FIRST[i]:
            take_y(i)
        take_z(i)

    def do_attend(start):
        over(start, 64, attend)

    def do_hidden_grad():
        tile_loop(FH, 256, hidden_grad)

    def do_attend_grad(start):
        over(start, 64, attend_grad)

    work = (
        (do_start,), (own, GH), (own, GA), (got_z, GH, 1, 0), (own, GB), (do_start2,), (got_z, GH, 2, 0),
        (got_y, GA, 0), (got_z, GA, 1, 0), (own, GO), (got_z, GA, 2, 0), (got_y, GH, 1), (got_y, GH, 0),
        (do_norm_own,), (got_z, GB, 1, 0), (got_z, GB, 2, 0), (got_z, GH, 3, 0), (got_z, GA, 3, 0), (got_y, GO, 0),
        (got_z, GB, 3, 0), (got_y, GA, 2), (got_y, GH, 2), (got_z, GO, 1, 0), (got_z, GO, 2, 0), (got_y, GB, 1),
        (got_z, GO, 3, 0), (own, GS), (own, GF), (got_y, GB, 2), (got_y, GA, 3), (got_y, GB, 0), (got_y, GH, 3),
        (own, GD), (got_y, GA, 1), (own, GT), (own, GG), (do_norm_partner,), (whole, GH), (got_y, GB, 3), (whole, GA),
        (do_proj, 0), (whole, GB), (do_proj, 1), (got_y, GO, 2), (got_y, GO, 1), (got_y, GO, 3), (got_z, GS, 1, 0),
        (do_attend, 256), (whole, GO), (do_attend, 320), (do_out, 256), (got_z, GT, 1, 0), (do_attend, 448),
        (got_z, GF, 1, 0), (got_z, GG, 1, 0), (got_z, GF, 2, 0), (got_z, GS, 2, 0), (got_z, GG, 2, 0),
        (do_attend, 384), (got_y, GD, 0), (got_y, GS, 0), (do_out, 384), (got_z, GS, 3, 0), (do_attend, 0),
        (do_attend, 64), (do_out, 0), (do_resid, 0), (got_z, GF, 3, 0), (got_z, GG, 3, 0), (got_y, GT, 1),
        (do_attend, 192), (got_z, GT, 2, 0), (got_y, GT, 0), (got_z, GS, 1, 1), (got_z, GS, 2, 1), (got_y, GG, 0),
        (got_z, GT, 3, 0), (do_attend, 128), (got_z, GD, 1, 0), (do_out, 128), (do_resid, 128), (got_y, GG, 1),
        (got_z, GD, 2, 0), (got_y, GG, 2), (got_z, GS, 3, 1), (whole, GS), (got_y, GG, 3), (got_y, GF, 3),
        (got_y, GF, 1), (got_y, GF, 2), (got_y, GF, 0), (whole, GG), (whole, GF), (got_y, GT, 2), (got_z, GD, 3, 0),
        (got_y, GT, 3), (do_hidden, 0), (whole, GT), (do_hidden, 1), (do_cot,), (give, 0), (give, 1), (got_y, GD, 2),
        (got_y, GD, 1), (take, 0), (got_y, GD, 3), (take, 1), (whole, GD), (do_hidden_grad,), (give, 2),
        (do_back, 256), (give, 3), (take, 2), (give, 4), (take, 3), (give, 5), (pass_far, 1), (take_y, 0),
        (do_back, 384), (take, 5), (do_back, 0), (do_resid_grad, 0), (take_y, 2), (do_resid_grad, 128),
        (do_mixed_grad, 0), (do_attend_grad, 64), (do_attend_grad, 192), (do_attend_grad, 0), (pass_far, 0),
        (do_mixed_grad, 256), (do_attend_grad, 320), (take_y, 3), (do_take_z, 0), (pass_far, 2), (take, 4),
        (do_mixed_grad, 384), (give, 6), (do_attend_grad, 448), (do_attend_grad, 256), (pass_far, 3), (take_y, 5),
        (give, 7), (do_attend_grad, 128), (do_take_z, 2), (do_attend_grad, 384), (do_heads_back, 256), (take, 6),
        (give, 8), (take, 7), (give, 9), (pass_far, 5), (take, 9), (take, 8), (give, 10), (give, 11), (take, 11),
        (pass_far, 7), (take_y, 4), (do_take_z, 3), (owner_sum, 1), (do_heads_back, 0), (do_block_out,),
        (do_tokens_grad,), (do_gsum, 0), (take_y, 9), (do_take_z, 5), (pass_far, 4), (do_take_z, 4), (take_y, 6),
        (take, 10), (finish, 0), (pass_far, 9), (take_y, 11), (owner_sum, 7), (take_y, 8), (do_take_z, 1),
        (do_take_z, 9), (finish, 2), (pass_far, 6), (pass_far, 11), (do_block_rows,), (do_gsum, 1), (pass_far, 8),
        (do_take_z, 6), (finish, 4), (take_y, 10), (do_take_z, 7), (do_gsum, 2), (finish, 3), (pass_far, 10),
        (finish, 9), (do_gsum, 3), (do_take_z, 8), (do_take_z, 11), (finish, 1), (finish, 6), (do_take_z, 10),
        (finish, 5), (finish, 10), (finish, 8), (finish, 7), (finish, 11), (do_gsum, 4),
    )
    for step, *args in work:
        step(*args)
    for copy in list(chunk_sends.values()) + list(swaps.values()) + sends:
        copy.wait_send()
    for pred, copy in guarded:
        pl.when(pred)(copy.wait_send)
    for copy in finals + outs:
        copy.wait()
    for g in "abfsgt":
        gi = GROUPS.index(g)
        own = col_shard(g, x)
        remote(own, own, r.s_xs.at[gi, 0], r.s_xs.at[gi, 0], xn).wait_send()
    for g in ("o", "d"):
        gi = GROUPS.index(g)
        block = r.wo.at[pl.ds(0, 32), pl.ds(0, 512)] if g == "o" else r.wds.at[0]

        @pl.when(x != c)
        def _():
            remote(block, block, r.s_xs.at[gi, 0], r.s_xs.at[gi, 0], xn).wait_send()

        remote(block, block, r.s_xs.at[gi, 1], r.s_xs.at[gi, 1], xn).wait_send()


def hand_over(gain_ref, *refs):
    count = (len(refs) - 4) // 3
    ins, (one, two), outs = refs[:count], refs[count : count + 2], refs[count + 2 : 2 * count + 2]
    held, (in_sems, out_sems) = refs[2 * count + 2 : -2], refs[-2:]
    loads = [pltpu.make_async_copy(a, b, in_sems.at[i]) for i, (a, b) in enumerate(zip(ins, held))]
    stores = [pltpu.make_async_copy(a, b, out_sems.at[i]) for i, (a, b) in enumerate(zip(held, outs))]
    for load in loads:
        load.start()
    me = lax.axis_index("dp") * 16 + lax.axis_index("fsdp")
    block = gain_ref[:, lanes_of(128 * (me // 4), 128)]
    block = pltpu.roll(block, lax.rem(128 - 32 * lax.rem(me, 4), 128), 1)
    one[...] = block[0, :32]
    two[...] = block[1, :32]
    for load, store in zip(loads, stores):
        load.wait()
        store.start()
    for store in stores:
        store.wait()


def fused_layer(
    tokens, attn_gain, w_query, w_key, w_value, w_gate, w_output, ffn_gain, w_first, w_second, w_down, cotangent
):
    items = scratch_list()
    names = IN_NAMES + OUT_NAMES + tuple(name for name, _ in items)
    shape = jax.ShapeDtypeStruct
    outs = pl.pallas_call(
        functools.partial(layer_kernel, names),
        out_shape=[
            shape((OWN, D), BF16), shape((OWN, D), F32), shape((8, D), F32),
            shape((32, D), F32), shape((32, D), F32), shape((32, D), F32), shape((32, D), F32), shape((32, D), F32),
            shape((32, FF), F32), shape((32, FF), F32), shape((88, D), F32),
        ],
        in_specs=[pl.BlockSpec(memory_space=pltpu.VMEM if n.startswith("gain") else pl.ANY) for n in IN_NAMES],
        out_specs=[pl.BlockSpec(memory_space=pl.ANY)] * len(OUT_NAMES),
        scratch_shapes=[spec for _, spec in items],
        compiler_params=pltpu.CompilerParams(collective_id=0, has_side_effects=True, vmem_limit_bytes=66 * 2**20 - 2**21),
        name="layer",
    )(tokens, attn_gain, ffn_gain, w_query, w_key, w_value, w_gate, w_output, w_first, w_second, w_down, cotangent)
    block_out, tokens_grad, gain_grads, gq, gk, gv, gg, go, g1, g2, gd = outs
    kept = (block_out, tokens_grad, gq, gk, gv, gg, go, g1, g2, gd)
    anywhere = pl.BlockSpec(memory_space=pl.ANY)
    in_vmem = pl.BlockSpec(memory_space=pltpu.VMEM)
    gain_one, gain_two, *rest = pl.pallas_call(
        hand_over,
        out_shape=[shape((32,), F32)] * 2 + [shape(v.shape, v.dtype) for v in kept],
        in_specs=[in_vmem] + [anywhere] * len(kept),
        out_specs=[in_vmem] * 2 + [anywhere] * len(kept),
        scratch_shapes=[pltpu.VMEM(v.shape, v.dtype) for v in kept] + [pltpu.SemaphoreType.DMA((len(kept),))] * 2,
        compiler_params=pltpu.CompilerParams(vmem_limit_bytes=63 * 2**20),
        name="hand_over",
    )(gain_grads, *kept)
    block_out, tokens_grad, gq, gk, gv, gg, go, g1, g2, gd = rest
    return block_out, tokens_grad, gain_one, gq, gk, gv, gg, go, gain_two, g1, g2, gd


def rms_scale(values, gain):
    return values * lax.rsqrt(jnp.mean(values * values, axis=-1, keepdims=True) + EPS) * gain


def gated(attended, gate_pre):
    return attended * jax.nn.silu(gate_pre)


def contract_rows(left, right):
    return lax.dot_general(
        left, right, (((0,), (0,)), ((), ())), preferred_element_type=jnp.float32
    )


def contract_cols(left, right):
    return lax.dot_general(
        left, right, (((1,), (1,)), ((), ())), preferred_element_type=jnp.float32
    )


def project(left, right):
    return jnp.dot(left, right, preferred_element_type=jnp.float32)


def flatten_rows(matrix):
    return matrix.reshape(-1, 128)


def restore_rows(flat, columns):
    return flat.reshape(-1, columns)


def split_heads(matrix):
    return matrix.reshape(matrix.shape[0] // BLK, BLK, HEADS, HDIM)


def block_scores(queries, keys):
    raw = jnp.einsum(
        "bqhd,bkhd->bhqk",
        split_heads(queries),
        split_heads(keys),
        preferred_element_type=jnp.float32,
    )
    causal = jnp.arange(BLK)[:, None] >= jnp.arange(BLK)[None, :]
    return jnp.where(causal, raw * HDIM ** (-0.5), -1e30)


def attend_forward(queries, keys, values):
    scores = block_scores(queries, keys)
    highest = jnp.max(scores, axis=-1, keepdims=True)
    weights = jnp.exp(scores - highest)
    total = jnp.sum(weights, axis=-1, keepdims=True)
    probs = (weights / total).astype(jnp.bfloat16)
    attended = jnp.einsum(
        "bhqk,bkhd->bqhd", probs, split_heads(values), preferred_element_type=jnp.float32
    )
    return (attended.reshape(queries.shape[0], D), highest + jnp.log(total))


def attend_backward(queries, keys, values, log_total, attended_grad):
    scores = block_scores(queries, keys)
    probs = jnp.exp(scores - log_total)
    grad_heads = split_heads(attended_grad)
    value_grad = jnp.einsum(
        "bhqk,bqhd->bkhd",
        probs.astype(jnp.bfloat16),
        grad_heads,
        preferred_element_type=jnp.float32,
    )
    prob_grad = jnp.einsum(
        "bqhd,bkhd->bhqk", grad_heads, split_heads(values), preferred_element_type=jnp.float32
    )
    score_grad = (probs * (prob_grad - jnp.sum(probs * prob_grad, axis=-1, keepdims=True))).astype(
        jnp.bfloat16
    )
    factor = HDIM ** (-0.5)
    query_grad = (
        jnp.einsum(
            "bhqk,bkhd->bqhd", score_grad, split_heads(keys), preferred_element_type=jnp.float32
        )
        * factor
    )
    key_grad = (
        jnp.einsum(
            "bhqk,bqhd->bkhd", score_grad, split_heads(queries), preferred_element_type=jnp.float32
        )
        * factor
    )
    length = queries.shape[0]
    return (
        query_grad.reshape(length, D).astype(jnp.bfloat16),
        key_grad.reshape(length, D).astype(jnp.bfloat16),
        value_grad.reshape(length, D).astype(jnp.bfloat16),
    )


def on_device(
    tokens,
    attn_gain,
    w_query,
    w_key,
    w_value,
    w_gate,
    w_output,
    ffn_gain,
    w_first,
    w_second,
    w_down,
    cotangent,
):
    attn_whole = (
        lax.all_gather(attn_gain, ("dp", "fsdp"), axis=0, tiled=True),
        lax.all_gather(w_query, ("dp", "fsdp"), axis=0, tiled=True),
        lax.all_gather(w_key, ("dp", "fsdp"), axis=0, tiled=True),
        lax.all_gather(w_value, ("dp", "fsdp"), axis=0, tiled=True),
        lax.all_gather(w_gate, ("dp", "fsdp"), axis=0, tiled=True),
        lax.all_gather(w_output, ("dp", "fsdp"), axis=0, tiled=True),
    )
    gain_one, query_full, key_full, value_full, gate_full, output_full = attn_whole
    inputs = tokens.astype(jnp.float32)
    normed_pre, norm_pull = jax.vjp(rms_scale, inputs, gain_one.astype(jnp.float32))
    normed = normed_pre.astype(jnp.bfloat16)
    queries = project(normed, query_full).astype(jnp.bfloat16)
    keys = project(normed, key_full).astype(jnp.bfloat16)
    values = project(normed, value_full).astype(jnp.bfloat16)
    gate_pre = project(normed, gate_full)
    attended, log_total = attend_forward(queries, keys, values)
    mixed_pre, gate_pull = jax.vjp(gated, attended, gate_pre)
    mixed = mixed_pre.astype(jnp.bfloat16)
    resid = inputs + project(mixed, output_full)
    ffn_whole = (
        lax.all_gather(ffn_gain, ("dp", "fsdp"), axis=0, tiled=True),
        lax.all_gather(w_first, ("dp", "fsdp"), axis=0, tiled=True),
        lax.all_gather(w_second, ("dp", "fsdp"), axis=0, tiled=True),
        lax.all_gather(w_down, ("dp", "fsdp"), axis=0, tiled=True),
    )
    gain_two, first_full, second_full, down_full = ffn_whole
    normed_two_pre, norm_two_pull = jax.vjp(rms_scale, resid, gain_two.astype(jnp.float32))
    normed_two = normed_two_pre.astype(jnp.bfloat16)
    first = project(normed_two, first_full).astype(jnp.bfloat16)
    second = project(normed_two, second_full).astype(jnp.bfloat16)
    product = (first.astype(jnp.float32) * second.astype(jnp.float32)).astype(jnp.bfloat16)
    block_out = (resid + project(product, down_full)).astype(jnp.bfloat16)
    gain_two, first_full, second_full, down_full = (
        lax.all_gather(ffn_gain, ("dp", "fsdp"), axis=0, tiled=True),
        lax.all_gather(w_first, ("dp", "fsdp"), axis=0, tiled=True),
        lax.all_gather(w_second, ("dp", "fsdp"), axis=0, tiled=True),
        lax.all_gather(w_down, ("dp", "fsdp"), axis=0, tiled=True),
    )
    product_grad = contract_cols(cotangent, down_full).astype(jnp.bfloat16)
    product_wide = product_grad.astype(jnp.float32)
    first_grad = (product_wide * second.astype(jnp.float32)).astype(jnp.bfloat16)
    second_grad = (product_wide * first.astype(jnp.float32)).astype(jnp.bfloat16)
    normed_two_grad = contract_cols(first_grad, first_full) + contract_cols(
        second_grad, second_full
    )
    resid_part, gain_two_grad = norm_two_pull(normed_two_grad)
    resid_grad = cotangent.astype(jnp.float32) + resid_part
    down_grad = contract_rows(product, cotangent)
    first_w_grad = contract_rows(normed_two, first_grad)
    second_w_grad = contract_rows(normed_two, second_grad)
    ffn_sums = (
        lax.psum_scatter(gain_two_grad, ("dp", "fsdp"), scatter_dimension=0, tiled=True),
        lax.psum_scatter(
            flatten_rows(first_w_grad), ("dp", "fsdp"), scatter_dimension=0, tiled=True
        ),
        lax.psum_scatter(
            flatten_rows(second_w_grad), ("dp", "fsdp"), scatter_dimension=0, tiled=True
        ),
        lax.psum_scatter(flatten_rows(down_grad), ("dp", "fsdp"), scatter_dimension=0, tiled=True),
    )
    gain_one, query_full, key_full, value_full, gate_full, output_full = (
        lax.all_gather(attn_gain, ("dp", "fsdp"), axis=0, tiled=True),
        lax.all_gather(w_query, ("dp", "fsdp"), axis=0, tiled=True),
        lax.all_gather(w_key, ("dp", "fsdp"), axis=0, tiled=True),
        lax.all_gather(w_value, ("dp", "fsdp"), axis=0, tiled=True),
        lax.all_gather(w_gate, ("dp", "fsdp"), axis=0, tiled=True),
        lax.all_gather(w_output, ("dp", "fsdp"), axis=0, tiled=True),
    )
    branch_grad = resid_grad.astype(jnp.bfloat16)
    mixed_grad = contract_cols(branch_grad, output_full).astype(jnp.bfloat16)
    attended_part, gate_part = gate_pull(mixed_grad.astype(jnp.float32))
    attended_grad = attended_part.astype(jnp.bfloat16)
    gate_grad = gate_part.astype(jnp.bfloat16)
    query_grad, key_grad, value_grad = attend_backward(
        queries, keys, values, log_total, attended_grad
    )
    normed_grad = contract_cols(query_grad, query_full) + contract_cols(key_grad, key_full)
    normed_grad = (
        normed_grad + contract_cols(value_grad, value_full) + contract_cols(gate_grad, gate_full)
    )
    input_part, gain_one_grad = norm_pull(normed_grad)
    tokens_grad = resid_grad + input_part
    output_w_grad = contract_rows(mixed, branch_grad)
    query_w_grad = contract_rows(normed, query_grad)
    key_w_grad = contract_rows(normed, key_grad)
    value_w_grad = contract_rows(normed, value_grad)
    gate_w_grad = contract_rows(normed, gate_grad)
    attn_sums = (
        lax.psum_scatter(gain_one_grad, ("dp", "fsdp"), scatter_dimension=0, tiled=True),
        lax.psum_scatter(
            flatten_rows(query_w_grad), ("dp", "fsdp"), scatter_dimension=0, tiled=True
        ),
        lax.psum_scatter(flatten_rows(key_w_grad), ("dp", "fsdp"), scatter_dimension=0, tiled=True),
        lax.psum_scatter(
            flatten_rows(value_w_grad), ("dp", "fsdp"), scatter_dimension=0, tiled=True
        ),
        lax.psum_scatter(
            flatten_rows(gate_w_grad), ("dp", "fsdp"), scatter_dimension=0, tiled=True
        ),
        lax.psum_scatter(
            flatten_rows(output_w_grad), ("dp", "fsdp"), scatter_dimension=0, tiled=True
        ),
    )
    gain_two_sum, first_flat, second_flat, down_flat = ffn_sums
    gain_one_sum, query_flat, key_flat, value_flat, gate_flat, output_flat = attn_sums
    query_sum = restore_rows(query_flat, D)
    key_sum = restore_rows(key_flat, D)
    value_sum = restore_rows(value_flat, D)
    gate_sum = restore_rows(gate_flat, D)
    output_sum = restore_rows(output_flat, D)
    first_sum = restore_rows(first_flat, FF)
    second_sum = restore_rows(second_flat, FF)
    down_sum = restore_rows(down_flat, D)
    return (
        block_out,
        tokens_grad,
        gain_one_sum,
        query_sum,
        key_sum,
        value_sum,
        gate_sum,
        output_sum,
        gain_two_sum,
        first_sum,
        second_sum,
        down_sum,
    )


def solution(mesh):
    fits = dict(mesh.shape) == {"dp": 2, "fsdp": 16}
    return jax.shard_map(
        fused_layer if fits else on_device,
        mesh=mesh,
        in_specs=(
            P(("dp", "fsdp"), None),
            P(("dp", "fsdp")),
            P(("dp", "fsdp"), None),
            P(("dp", "fsdp"), None),
            P(("dp", "fsdp"), None),
            P(("dp", "fsdp"), None),
            P(("dp", "fsdp"), None),
            P(("dp", "fsdp")),
            P(("dp", "fsdp"), None),
            P(("dp", "fsdp"), None),
            P(("dp", "fsdp"), None),
            P(("dp", "fsdp"), None),
        ),
        out_specs=(
            P(("dp", "fsdp"), None),
            P(("dp", "fsdp"), None),
            P(("dp", "fsdp")),
            P(("dp", "fsdp"), None),
            P(("dp", "fsdp"), None),
            P(("dp", "fsdp"), None),
            P(("dp", "fsdp"), None),
            P(("dp", "fsdp"), None),
            P(("dp", "fsdp")),
            P(("dp", "fsdp"), None),
            P(("dp", "fsdp"), None),
            P(("dp", "fsdp"), None),
        ),
        check_vma=False,
    )
```

```python
import functools

import jax
import jax.numpy as jnp
from jax import lax
from jax.experimental import pallas as pl
from jax.experimental.pallas import tpu as pltpu
from jax.sharding import PartitionSpec as P

D = 1024
HEADS = 16
HDIM = 64
FF = 2816
BLK = 64


EPS = 1e-06


MESH = pl.DeviceIdType.MESH
F32, BF16 = jnp.float32, jnp.bfloat16

OWN = 256
ROWS = 512
HALF = 512
FH = 1408
CHUNKS = (
    ("d", 0, 256), ("d", 256, 256),
    ("f", 0, 768), ("f", 768, 640), ("f", 1408, 768), ("f", 2176, 640),
    ("o", 0, 512),
    ("a", 1536, 512), ("a", 1024, 512), ("a", 512, 512), ("a", 0, 256), ("a", 256, 256),
)
NCH = len(CHUNKS)
Z_FIRST = tuple(i in (1, 7,) for i in range(NCH))
Y_FIRST = ("s",)
GROUPS = ("h", "a", "b", "o", "f", "s", "g", "t", "d")
GH, GA, GB, GO, GF, GS, GG, GT, GD = GROUPS
SPANS = {"h": (0, 1152), "a": (0, 1152), "b": (1152, 1024), "f": (0, 768), "g": (768, 640), "s": (FH, 768), "t": (FH + 768, 640)}


def piece_rows(kind):
    return 176 if kind == "d" else 64


def scratch_list():
    vm, dma = pltpu.VMEM, pltpu.SemaphoreType.DMA
    items = [
        ("wa", vm((D, 4 * HALF + 128), BF16)), ("wf", vm((D, 2 * FH), BF16)),
        ("wo", vm((HALF, D), BF16)), ("wd", vm((FH, D), BF16)), ("wds", vm((2, 88, 512), BF16)),
        ("tok", vm((ROWS, D), BF16)), ("cot", vm((ROWS, D), BF16)), ("nrm", vm((ROWS, D), BF16)),
        ("qkv", vm((ROWS, 3 * HALF), BF16)), ("gp", vm((ROWS, HALF), F32)), ("att", vm((ROWS, HALF), F32)),
        ("prob", vm((ROWS, HALF), F32)), ("mix", vm((ROWS, HALF), BF16)), ("dout", vm((ROWS, HALF), BF16)),
        ("res", vm((OWN, D), F32)), ("nt", vm((ROWS, D), BF16)), ("fs", vm((ROWS, 2 * FH), BF16)),
        ("pr", vm((ROWS, FH), BF16)), ("g4", vm((ROWS, 4 * HALF), BF16)), ("bg", vm((ROWS, D), BF16)),
        ("rg", vm((OWN, D), F32)), ("po", vm((OWN, D), F32)), ("bo", vm((OWN, D), BF16)),
        ("es", vm((3, OWN, D), BF16)), ("er", vm((3, OWN, D), BF16)),
        ("gs", vm((4, 8, D), F32)), ("gr", vm((6, 8, D), F32)), ("gain", vm((8, D), F32)), ("gains", vm((32, 128), BF16)), ("gacc", vm((2, 8, D), F32)),
        ("sbd", vm((2, 4, 2, 176, 256), BF16)), ("sbf", vm((2, 4, 2, 64, 768), BF16)),
    ]
    for i, (kind, _, cols) in enumerate(CHUNKS):
        r = piece_rows(kind)
        items += [
            (f"rb{i}", vm((4, 2, r, cols), BF16)), (f"ow{i}", vm((4, 2, r, cols), BF16)),
            (f"yr{i}", vm((r, cols) if Z_FIRST[i] else (4, r, cols), BF16)),
            (f"zr{i}", vm((3, 2, r, cols) if Z_FIRST[i] else (3, r, cols), BF16)),
            (f"zx{i}", vm((2, r, cols) if Z_FIRST[i] else (r, cols), BF16)),
            (f"fin{i}", vm((r, cols), F32)),
        ]
    n = len(GROUPS)
    items += [
        ("s_loc", dma((4,))), ("s_wl", dma((n,))), ("s_xs", dma((n, 2))), ("s_xr", dma((n,))),
        ("s_es", dma((16,))), ("s_er", dma((16,))),
        ("s_zs", dma((n, 2, 5))), ("s_zr", dma((n, 2, 3))), ("s_ys", dma((n, 4))), ("s_yr", dma((n, 4))),
        ("s_cs", dma((n, 4, 2))), ("s_cr", dma((n, 4, 2))),
        ("s_gs", dma((6,))), ("s_gr", dma((6,))),
        ("r_cs", dma((NCH,))), ("r_cr", dma((NCH,))), ("r_ys", dma((NCH,))), ("r_yr", dma((NCH,))),
        ("r_zs", dma((NCH, 3))), ("r_zr", dma((NCH, 3))), ("r_zx", dma((NCH,))), ("r_zt", dma((NCH,))), ("r_fs", dma((NCH, 2))), ("r_fr", dma((NCH, 2))),
        ("s_out", dma((4,))),
    ]
    return items


IN_NAMES = ("tokens", "gain_a", "gain_f", "wq", "wk", "wv", "wg", "wo_in", "w1", "w2", "wd_in", "cot_in")
OUT_NAMES = ("block_out", "tokens_grad", "gain_grads", "gq", "gk", "gv", "gg", "go", "g1", "g2", "gd")


class Refs:
    def __init__(self, names, refs):
        self.__dict__.update(zip(names, refs))


def rows_of(start, count, unit=8):
    return pl.ds(pl.multiple_of(start, unit), count)


def lanes_of(start, count):
    return pl.ds(pl.multiple_of(start, 128), count)


def dot(a, b):
    return jnp.dot(a, b, preferred_element_type=F32)


def dot_t(a, b):
    return lax.dot_general(a, b, (((1,), (1,)), ((), ())), preferred_element_type=F32)


def t_dot(a, b):
    return lax.dot_general(a, b, (((0,), (0,)), ((), ())), preferred_element_type=F32)


def tile_loop(total, width, fn):
    count = total // width
    if count == 1:
        fn(0, width)
    else:
        lax.fori_loop(0, count, lambda i, u: (fn(pl.multiple_of(i * width, width), width), u)[1], 0)
    if total % width:
        fn(count * width, total % width)


def row_loop(total, step, fn):
    lax.fori_loop(0, total // step, lambda i, u: (fn(pl.multiple_of(i * step, step)), u)[1], 0)


def layer_kernel(names, *refs):
    r = Refs(names, refs)
    c = lax.axis_index("dp")
    f = lax.axis_index("fsdp")
    z, y, x = f // 4, (f // 2) % 2, f % 2

    def dev(cc, zz, yy, xx):
        return (cc, zz * 4 + yy * 2 + xx)

    xn, yn, sib, diag = dev(c, z, y, 1 - x), dev(c, z, 1 - y, x), dev(1 - c, z, y, x), dev(1 - c, z, y, 1 - x)
    zk = [(z + k) % 4 for k in range(4)]
    zp = [dev(c, zk[k], y, x) for k in range(4)]

    barrier = pltpu.get_barrier_semaphore()
    for peer in (xn, yn, sib, diag, zp[1], zp[2], zp[3]):
        pl.semaphore_signal(barrier, inc=1, device_id=peer, device_id_type=MESH)
    pl.semaphore_wait(barrier, 7)

    sends, guarded = [], []
    inner = jnp.logical_and(z != 0, z != 3)

    def remote(src, dst, ss, rs, to):
        return pltpu.make_async_remote_copy(
            src_ref=src, dst_ref=dst, send_sem=ss, recv_sem=rs, device_id=to, device_id_type=MESH
        )

    def send(src, dst, ss, rs, to, later=True):
        copy = remote(src, dst, ss, rs, to)
        copy.start()
        if later:
            sends.append(copy)
        return copy

    def send_if(pred, src, dst, ss, rs, to):
        copy = remote(src, dst, ss, rs, to)
        pl.when(pred)(copy.start)
        guarded.append((pred, copy))

    def arrived(ref, sem):
        remote(ref, ref, sem, sem, xn).wait_recv()

    def local(src, dst, sem):
        copy = pltpu.make_async_copy(src, dst, sem)
        copy.start()
        return copy

    mine = x
    p = c * 8 + z * 2 + y
    m = z * 2 + y

    def piece(g, cc, zz, yy):
        if g in "ha":
            part = x if g == "h" else 1 - x
            return r.wa.at[rows_of(64 * (cc * 8 + zz * 2 + yy) + 32 * part, 32, 32), pl.ds(*SPANS[g])]
        if g in SPANS:
            full = r.wa if g == "b" else r.wf
            return full.at[rows_of(64 * (cc * 8 + zz * 2 + yy), 64, 64), pl.ds(*SPANS[g])]
        if g == "o":
            return r.wo.at[rows_of(64 * (zz * 2 + yy), 64, 64), lanes_of(512 * cc, 512)]
        return r.wd.at[rows_of(176 * (zz * 2 + yy), 176, 16), lanes_of(512 * cc, 512)]

    def col_shard(g, who):
        row = rows_of(64 * p + 32 * who, 32, 32)
        return (r.wa if g in "hab" else r.wf).at[row, pl.ds(*SPANS[g])]

    def start_cols(g):
        gi = GROUPS.index(g)
        if g == "a":
            parts = [(r.wq, HALF, 0, HALF, 0), (r.wk, HALF, 0, HALF, HALF)]
        elif g == "b":
            parts = [(r.wv, HALF, 0, HALF, 1152), (r.wg, HALF, 0, HALF, 1152 + HALF)]
        else:
            at, cols = SPANS[g]
            parts = [(r.w1 if g in "fg" else r.w2, FH, at % FH, cols, at)]
        full = r.wa if g in "ab" else r.wf
        row = rows_of(64 * p + 32 * x, 32, 32)
        if g == "a":
            local(r.gains, full.at[row, pl.ds(1024, 128)], r.s_wl.at[gi])
            send(r.gains, full.at[row, pl.ds(1024, 128)], r.s_xs.at[gi, 0], r.s_xr.at[gi], xn, later=False)
        for w, half, first, cols, at in parts:
            dst = full.at[row, pl.ds(at, cols)]
            local(w.at[:, lanes_of(half * x + first, cols)], dst, r.s_wl.at[gi])
            send(
                w.at[:, lanes_of(half * (1 - x) + first, cols)], dst,
                r.s_xs.at[gi, 0], r.s_xr.at[gi], xn, later=False,
            )

    def start_rows(g):
        gi = GROUPS.index(g)
        w = r.wo_in if g == "o" else r.wd_in

        def place(h):
            if g == "o":
                return r.wo.at[rows_of(64 * m + 32 * x, 32, 32), lanes_of(512 * h, 512)]
            return r.wds.at[x]

        @pl.when(x == c)
        def _():
            local(w.at[:, lanes_of(512 * c, 512)], place(c), r.s_xr.at[gi])

        @pl.when(x != c)
        def _():
            send(w.at[:, lanes_of(512 * c, 512)], place(c), r.s_xs.at[gi, 0], r.s_xr.at[gi], xn, later=False)

        send(
            w.at[:, lanes_of(512 * (1 - c), 512)], place(1 - c), r.s_xs.at[gi, 1], r.s_xr.at[gi], dev(1 - c, z, y, c),
            later=False,
        )

    def piece_ready(g):
        gi = GROUPS.index(g)
        if g == "a":
            arrived(col_shard(g, 1 - x), r.s_xr.at[gi])
        elif g in SPANS:
            own = col_shard(g, x)
            pltpu.make_async_copy(own, own, r.s_wl.at[GROUPS.index("a") if g == "h" else gi]).wait()
            if g != "h":
                arrived(col_shard(g, 1 - x), r.s_xr.at[gi])
        elif g == "o":
            arrived(piece("o", c, z, y), r.s_xr.at[gi])
        else:
            arrived(r.wds, r.s_xr.at[gi])
            both = jnp.concatenate([r.wds[0].astype(F32), r.wds[1].astype(F32)], axis=0)
            r.wd[rows_of(176 * m, 176, 16), lanes_of(512 * c, 512)] = both.astype(BF16)

    near = [
        jnp.where(z < 2, 1, 3),
        jnp.where(z == 1, 3, jnp.where(z == 2, 1, 2)),
        jnp.where(z == 0, 3, jnp.where(z == 3, 1, 2)),
    ]

    def near_z(n):
        return z if n == 0 else lax.rem(z + near[n - 1], 4)

    def up_down(g, yy, j):
        gi = GROUPS.index(g)
        own = piece(g, c, z, yy)
        send_if(z < 3, own, own, r.s_zs.at[gi, j, 0], r.s_zr.at[gi, j, 2], zp[1])
        send_if(z > 0, own, own, r.s_zs.at[gi, j, 1], r.s_zr.at[gi, j, 0], zp[3])

    def across(g, n):
        gi = GROUPS.index(g)
        ref = piece(g, c, near_z(n), y)
        send(ref, ref, r.s_ys.at[gi, n], r.s_yr.at[gi, n], yn)

    def to_core(g, n, j):
        gi = GROUPS.index(g)
        ref = piece(g, c, near_z(n), y if j == 0 else 1 - y)
        send(ref, ref, r.s_cs.at[gi, n, j], r.s_cr.at[gi, n, j], sib)

    def own(g):
        piece_ready(g)
        if g in Y_FIRST:
            across(g, 0)
            up_down(g, y, 0)
        else:
            up_down(g, y, 0)
            across(g, 0)
        to_core(g, 0, 0)

    def got_z(g, n, j=0):
        gi = GROUPS.index(g)
        got = piece(g, c, near_z(n), y if j == 0 else 1 - y)
        arrived(got, r.s_zr.at[gi, j, near[n - 1] - 1])
        src = near_z(n)
        to = jnp.where(src > z, z - 1, z + 1)
        slot = lax.rem(src - to + 4, 4) - 1
        send_if(inner, got, got, r.s_zs.at[gi, j, 1 + n], r.s_zr.at[gi, j, slot], dev(c, to, y, x))
        if g not in Y_FIRST:
            across(g, n)
        to_core(g, n, j)

    def got_y(g, n):
        gi = GROUPS.index(g)
        arrived(piece(g, c, near_z(n), 1 - y), r.s_yr.at[gi, n])
        if g in Y_FIRST:
            up_down(g, 1 - y, 1)
        to_core(g, n, 1)

    def spread_z(g):
        for j in range(2 if g in Y_FIRST else 1):
            for n in (1, 2, 3):
                got_z(g, n, j)

    def spread_y(g):
        for n in range(1 if g in Y_FIRST else 4):
            got_y(g, n)

    def whole(g):
        gi = GROUPS.index(g)
        for k in range(4):
            for j in range(2):
                arrived(piece(g, 1 - c, near_z(k), y if j == 0 else 1 - y), r.s_cr.at[gi, k, j])

    swaps = {}

    def swap(i, src, dst):
        swaps[i] = send(src, dst, r.s_es.at[i], r.s_er.at[i], xn, later=False)

    def swapped(i, dst):
        arrived(dst, r.s_er.at[i])

    def grad_sum(n, value=None):
        def out(slot, to):
            send(r.gs.at[min(slot, 3), pl.ds(0, 2)], r.gr.at[slot, pl.ds(0, 2)], r.s_gs.at[slot], r.s_gr.at[slot], to)

        def got(slot):
            arrived(r.gr.at[slot, pl.ds(0, 2)], r.s_gr.at[slot])
            return r.gr[slot, 0:2, :]

        if n == 0:
            r.gs[0] = value
            out(0, xn)
        elif n < 3:
            r.gs[n, 0:2, :] = r.gs[n - 1, 0:2, :] + got(n - 1)
            out(n, yn if n == 1 else sib)
        elif n == 3:
            r.gs[3, 0:2, :] = r.gs[2, 0:2, :] + got(2)
            for k in (1, 2, 3):
                send(r.gs.at[3, pl.ds(0, 2)], r.gr.at[6 - k, pl.ds(0, 2)], r.s_gs.at[2 + k], r.s_gr.at[6 - k], zp[k])
        else:
            return r.gs[3, 0:2, :] + (got(3) + got(4) + got(5))

    def norm_rows(start, at, out):
        v = r.tok[pl.ds(start + at, 64), :].astype(F32)
        scale = lax.rsqrt(jnp.mean(v * v, axis=-1, keepdims=True) + EPS)
        out[pl.ds(start, 64), :] = v * scale

    def gain_rows(start):
        rows = pl.ds(start, 64)
        r.nrm[rows, :] = (r.po[rows, :] * r.gain[0:1, :]).astype(BF16)
        r.nrm[pl.ds(start + OWN, 64), :] = (r.rg[rows, :] * r.gain[0:1, :]).astype(BF16)

    def proj(at, width, shift=0):
        r.qkv[:, pl.ds(at + shift, width)] = dot(r.nrm[...], r.wa[:, pl.ds(at + shift + shift // 8, width)]).astype(BF16)

    def proj_gate(at, width):
        r.gp[:, pl.ds(at, width)] = dot(r.nrm[...], r.wa[:, pl.ds(1152 + HALF + at, width)])

    lane = lax.broadcasted_iota(jnp.int32, (64, 128), 1)
    row = lax.broadcasted_iota(jnp.int32, (64, 128), 0)
    left = lane < 64
    causal = (lane % 64) <= row

    def pair(v):
        zero = jnp.zeros_like(v)
        return jnp.concatenate([jnp.where(left, v, zero), jnp.where(left, zero, v)], axis=0)

    def half_sum(v):
        zero = jnp.zeros_like(v)
        a = jnp.sum(jnp.where(left, v, zero), axis=-1, keepdims=True)
        b = jnp.sum(jnp.where(left, zero, v), axis=-1, keepdims=True)
        return jnp.where(left, a, b)

    def half_max(v):
        low = jnp.full_like(v, -3e38)
        a = jnp.max(jnp.where(left, v, low), axis=-1, keepdims=True)
        b = jnp.max(jnp.where(left, low, v), axis=-1, keepdims=True)
        return jnp.where(left, a, b)

    def head_cols(base, h):
        return pl.ds(base + 128 * h, 128)

    def attend(start):
        rows, heads = pl.ds(start, 64), range(4)
        q = [r.qkv[rows, head_cols(0, h)] for h in heads]
        k = [r.qkv[rows, head_cols(HALF, h)] for h in heads]
        v = [r.qkv[rows, head_cols(2 * HALF, h)] for h in heads]
        g = [r.gp[rows, head_cols(0, h)] for h in heads]
        s = [jnp.where(causal, dot_t(a, pair(b)) * HDIM ** (-0.5), -1e30) for a, b in zip(q, k)]
        e = [jnp.exp(a - half_max(a)) for a in s]
        prob = [a / half_sum(a) for a in e]
        att = [dot(a.astype(BF16), pair(b)) for a, b in zip(prob, v)]
        mix = [(a * (b * jax.nn.sigmoid(b))).astype(BF16) for a, b in zip(att, g)]
        for h in heads:
            r.prob[rows, head_cols(0, h)] = prob[h]
            r.att[rows, head_cols(0, h)] = att[h]
            r.mix[rows, head_cols(0, h)] = mix[h]

    def partial_rows(left, right, slot, start, count):
        rows = pl.ds(start, count)

        def tile(at, width):
            acc = right(left[rows, :], at, width)
            if start < OWN:
                r.po[rows, pl.ds(at, width)] = acc
            else:
                r.es[slot, pl.ds(start - OWN, count), pl.ds(at, width)] = acc.astype(BF16)

        tile_loop(D, 256, tile)

    def out_product(v, at, width):
        return dot(v, r.wo[:, pl.ds(at, width)])

    def hidden_back(v, at, width):
        return dot_t(v, r.wf[pl.ds(at, width), :])

    def heads_back(v, at, width):
        left, right = v[:, : 2 * HALF], v[:, 2 * HALF :]
        return dot_t(left, r.wa[pl.ds(at, width), pl.ds(0, 1024)]) + dot_t(right, r.wa[pl.ds(at, width), pl.ds(1152, 1024)])

    def resid_rows(start):
        rows = pl.ds(start, 64)
        v = r.tok[rows, :].astype(F32) + r.po[rows, :] + r.er[0, rows, :].astype(F32)
        r.res[rows, :] = v
        scale = lax.rsqrt(jnp.mean(v * v, axis=-1, keepdims=True) + EPS)
        r.nt[rows, :] = (v * scale * r.gain[1:2, :]).astype(BF16)

    def hidden(at, width):
        a = dot(r.nt[...], r.wf[:, pl.ds(at, width)]).astype(BF16)
        b = dot(r.nt[...], r.wf[:, pl.ds(FH + at, width)]).astype(BF16)
        r.fs[:, pl.ds(at, width)] = a
        r.fs[:, pl.ds(FH + at, width)] = b
        r.pr[:, pl.ds(at, width)] = (a.astype(F32) * b.astype(F32)).astype(BF16)

    def hidden_grad(at, width):
        pg = dot_t(r.cot[...], r.wd[pl.ds(at, width), :]).astype(BF16).astype(F32)
        a = r.fs[:, pl.ds(at, width)].astype(F32)
        b = r.fs[:, pl.ds(FH + at, width)].astype(F32)
        r.fs[:, pl.ds(at, width)] = (pg * b).astype(BF16)
        r.fs[:, pl.ds(FH + at, width)] = (pg * a).astype(BF16)

    def resid_grad_rows(start):
        rows = pl.ds(start, 64)
        ng = r.po[rows, :] + r.er[1, rows, :].astype(F32)
        v = r.res[rows, :]
        scale = lax.rsqrt(jnp.mean(v * v, axis=-1, keepdims=True) + EPS)
        n = ng * r.gain[1:2, :]
        grad = r.cot[rows, :].astype(F32) + scale * n - v * (scale * scale * scale * jnp.mean(n * v, axis=-1, keepdims=True))
        r.rg[rows, :] = grad
        r.bg[rows, :] = grad.astype(BF16)
        r.gacc[1] += jnp.sum((ng * v * scale).reshape(8, 8, D), axis=0)

    def mixed_grad(start, count):
        rows = pl.ds(start, count)

        def tile(at, width):
            cols = pl.ds(at, width)
            mg = dot_t(r.bg[rows, :], r.wo[pl.ds(at, width), :]).astype(BF16).astype(F32)
            g = r.gp[rows, cols]
            s = jax.nn.sigmoid(g)
            r.dout[rows, cols] = (mg * (g * s)).astype(BF16)
            r.g4[rows, pl.ds(3 * HALF + at, width)] = (mg * r.att[rows, cols] * (s * (1.0 + g * (1.0 - s)))).astype(BF16)

        tile_loop(HALF, 256, tile)

    def attend_grad(start):
        rows, heads = pl.ds(start, 64), range(4)
        q = [r.qkv[rows, head_cols(0, h)] for h in heads]
        k = [r.qkv[rows, head_cols(HALF, h)] for h in heads]
        v = [r.qkv[rows, head_cols(2 * HALF, h)] for h in heads]
        do = [r.dout[rows, head_cols(0, h)] for h in heads]
        prob = [r.prob[rows, head_cols(0, h)] for h in heads]
        pg = [dot_t(a, pair(b)) for a, b in zip(do, v)]
        vg = [t_dot(a.astype(BF16), b) for a, b in zip(prob, do)]
        sg = [(a * (b - half_sum(a * b))).astype(BF16) for a, b in zip(prob, pg)]
        qg = [dot(a, pair(b)) * HDIM ** (-0.5) for a, b in zip(sg, k)]
        kg = [t_dot(a, b) for a, b in zip(sg, q)]
        for h in heads:
            r.g4[rows, head_cols(0, h)] = qg[h].astype(BF16)
            r.g4[rows, head_cols(HALF, h)] = (jnp.where(left, kg[h][:64], kg[h][64:]) * HDIM ** (-0.5)).astype(BF16)
            r.g4[rows, head_cols(2 * HALF, h)] = jnp.where(left, vg[h][:64], vg[h][64:]).astype(BF16)

    def block_out_rows(start):
        rows = pl.ds(start, 64)
        r.bo[rows, :] = (r.res[rows, :] + r.er[0, rows, :].astype(F32)).astype(BF16)

    def block_out_part(at, width):
        acc = dot(r.pr[...], r.wd[:, pl.ds(at, width)])
        r.res[:, pl.ds(at, width)] += acc[:OWN]
        r.es[0, :, pl.ds(at, width)] = acc[OWN:].astype(BF16)

    def tokens_grad_rows(start):
        rows = pl.ds(start, 64)
        ng = r.po[rows, :] + r.er[2, rows, :].astype(F32)
        v = r.tok[rows, :].astype(F32)
        scale = lax.rsqrt(jnp.mean(v * v, axis=-1, keepdims=True) + EPS)
        n = ng * r.gain[0:1, :]
        r.rg[rows, :] = r.rg[rows, :] + scale * n - v * (scale * scale * scale * jnp.mean(n * v, axis=-1, keepdims=True))
        r.gacc[0] += jnp.sum((ng * v * scale).reshape(8, 8, D), axis=0)

    def chunk_dot(i, cc):
        kind, at, cols = CHUNKS[i]
        if kind == "d":
            out = t_dot(r.pr[...], r.cot[:, lanes_of(512 * cc + at, cols)])
        elif kind == "f":
            out = t_dot(r.nt[:, lanes_of(512 * cc, 512)], r.fs[:, pl.ds(at, cols)])
        elif kind == "o":
            out = t_dot(r.mix[...], r.bg[:, lanes_of(512 * cc, cols)])
        else:
            out = t_dot(r.nrm[:, lanes_of(512 * cc, 512)], r.g4[:, pl.ds(at, cols)])
        return out.reshape(4, 2, piece_rows(kind), cols)

    buf = lambda name, i: getattr(r, f"{name}{i}")
    chunk_sends = {}

    def give(i):
        kind, _, cols = CHUNKS[i]
        if i >= 4 and i - 2 in chunk_sends:
            chunk_sends.pop(i - 2).wait_send()
        stage = r.sbd.at[i % 2] if kind == "d" else r.sbf.at[i % 2, :, :, :, pl.ds(0, cols)]
        stage[...] = chunk_dot(i, 1 - c).astype(BF16)
        chunk_sends[i] = send(stage, buf("rb", i), r.r_cs.at[i], r.r_cr.at[i], sib, later=False)

    def take(i):
        arrived(buf("rb", i), r.r_cr.at[i])
        own = buf("ow", i)
        own[...] = (chunk_dot(i, c) + buf("rb", i)[...].astype(F32)).astype(BF16)
        if Z_FIRST[i]:
            to_owners(i)
        else:
            send(own.at[:, 1 - y], buf("yr", i), r.r_ys.at[i], r.r_yr.at[i], yn)

    def z_slot(i, zz):
        own = buf("ow", i)
        return own.at[zz] if Z_FIRST[i] else own.at[zz, y]

    def to_owners(i):
        beside = dev(c, jnp.where(z == 3, 2, 1), y, x)
        far = jnp.where(z == 3, 0, 3)
        send_if(jnp.logical_not(inner), z_slot(i, far), buf("zx", i), r.r_zs.at[i, 2], r.r_zx.at[i], beside)
        for k in (1, 3):
            slot = z_slot(i, zk[k])
            send_if(z != (3 if k == 1 else 0), slot, buf("zr", i).at[3 - k], r.r_zs.at[i, 1 if k == 3 else 0], r.r_zr.at[i, 3 - k], zp[k])
        two = z_slot(i, zk[2])
        send_if(jnp.logical_not(inner), two, buf("zr", i).at[1], r.r_zt.at[i], r.r_zr.at[i, 1], zp[2])

    def pass_far(i):
        two = z_slot(i, zk[2])

        @pl.when(inner)
        def _():
            arrived(buf("zx", i), r.r_zx.at[i])
            two[...] = (two[...].astype(F32) + buf("zx", i)[...].astype(F32)).astype(BF16)

        send_if(inner, two, buf("zr", i).at[1], r.r_zs.at[i, 2], r.r_zr.at[i, 1], zp[2])

    def take_y(i):
        own, part = buf("ow", i), buf("yr", i)
        arrived(part, r.r_yr.at[i])
        if Z_FIRST[i]:
            return
        for k in range(4):
            slot = own.at[zk[k], y]
            slot[...] = (slot[...].astype(F32) + part[zk[k]].astype(F32)).astype(BF16)
        to_owners(i)

    finals = []

    def add_z(i, dst, first, half=None):
        part = buf("zr", i)
        take_part = (lambda j: part[j]) if half is None else (lambda j: part[j, half])
        if not half:
            arrived(part.at[1], r.r_zr.at[i, 1])
        dst[...] = first + take_part(1).astype(F32)
        for j, end in ((0, 3), (2, 0)):

            @pl.when(z != end)
            def _():
                if not half:
                    arrived(part.at[j], r.r_zr.at[i, j])
                dst[...] += take_part(j).astype(F32)

    def owner_sum(i):
        own, fin = buf("ow", i), buf("fin", i)
        for half in range(2):
            add_z(i, fin, own[z, half].astype(F32), half)
            own[z, half] = fin[...].astype(BF16)
        send(own.at[z, 1 - y], buf("yr", i), r.r_ys.at[i], r.r_yr.at[i], yn)

    def take_z(i):
        kind, at, cols = CHUNKS[i]
        own, fin = buf("ow", i), buf("fin", i)
        if Z_FIRST[i]:
            fin[...] = own[z, y].astype(F32) + buf("yr", i)[...].astype(F32)
        else:
            add_z(i, fin, own[z, y].astype(F32))
        if kind in ("f", "a"):
            if kind == "f":
                out, place = (r.g1, FH * x + at) if at < FH else (r.g2, FH * x + at - FH)
            else:
                out, place = (r.gq, r.gk, r.gv, r.gg)[at // 512], HALF * x + at % 512
            dst = out.at[:, lanes_of(place, cols)]
            finals.append(local(fin.at[rows_of(32 * x, 32, 32)], dst, r.r_fs.at[i, 0]))
            send(fin.at[rows_of(32 * (1 - x), 32, 32)], dst, r.r_fs.at[i, 1], r.r_fr.at[i, 0], xn)
            return
        out = r.gd if kind == "d" else r.go
        n = 88 if kind == "d" else 32
        dst = out.at[:, lanes_of(512 * c + at, cols)]
        for xx in range(2):
            src = fin.at[pl.ds(n * xx, n)]
            itself = jnp.logical_and(x == c, x == xx)

            @pl.when(itself)
            def _():
                local(src, dst, r.r_fr.at[i, c])

            @pl.when(jnp.logical_not(itself))
            def _():
                send(src, dst, r.r_fs.at[i, xx], r.r_fr.at[i, c], dev(x, z, y, xx), later=False)

    def finish(i):
        kind, at, cols = CHUNKS[i]
        if kind in ("f", "a"):
            if kind == "f":
                out, place = (r.g1, FH * (1 - x) + at) if at < FH else (r.g2, FH * (1 - x) + at - FH)
            else:
                out, place = (r.gq, r.gk, r.gv, r.gg)[at // 512], HALF * (1 - x) + at % 512
            arrived(out.at[:, lanes_of(place, cols)], r.r_fr.at[i, 0])
            return
        out = r.gd if kind == "d" else r.go
        n = 88 if kind == "d" else 32
        for cc in range(2):
            arrived(out.at[:, pl.ds(512 * cc + at, cols)], r.r_fr.at[i, cc])
        for xx in range(2):
            itself = jnp.logical_and(x == c, x == xx)

            @pl.when(jnp.logical_not(itself))
            def _():
                src = buf("fin", i).at[pl.ds(n * xx, n)]
                remote(src, src, r.r_fs.at[i, xx], r.r_fs.at[i, xx], xn).wait_send()

    def over(start, count, fn):
        row_loop(count, 64, lambda at: fn(at + start))

    def swap_rows(i, src, dst, start, count):
        swap(i, src.at[pl.ds(start, count)], dst.at[pl.ds(start, count)])

    def swapped_rows(i, dst, start, count):
        swapped(i, dst.at[pl.ds(start, count)])

    load_tok = local(r.tokens, r.tok.at[pl.ds(0, OWN)], r.s_loc.at[0])
    load_cot = local(r.cot_in, r.cot.at[pl.ds(0, OWN)], r.s_loc.at[1])
    outs = []

    def do_start():
        eye = lax.broadcasted_iota(jnp.int32, (32, 32), 0) == lax.broadcasted_iota(jnp.int32, (32, 32), 1)
        column = lax.broadcasted_iota(jnp.int32, (32, 128), 1)
        total = jnp.zeros((32, 128), F32)
        for i, ref in enumerate((r.gain_a, r.gain_f)):
            values = jnp.broadcast_to(ref[...].astype(F32)[None, :], (32, 32))
            upright = jnp.sum(jnp.where(eye, values, 0.0), axis=1, keepdims=True)
            total = total + jnp.where(column == i, upright, 0.0)
        r.gains[...] = total.astype(BF16)
        start_cols("a")
        start_cols("b")
        r.gacc[...] = jnp.zeros((2, 8, D), F32)

    def do_start2():
        start_rows("o")
        for g in "fsgt":
            start_cols(g)
        start_rows("d")
        swap(0, r.tokens, r.tok.at[pl.ds(OWN, OWN)])
        swap(1, r.cot_in, r.cot.at[pl.ds(OWN, OWN)])

    def do_norm_own():
        load_tok.wait()
        over(0, OWN, lambda start: norm_rows(start, 0, r.po))

    def do_norm_partner():
        swapped(0, r.tok.at[pl.ds(OWN, OWN)])
        over(0, OWN, lambda start: norm_rows(start, OWN, r.rg))

    def do_proj(part):
        if part:
            tile_loop(HALF, 256, lambda at, width: proj(at, width, 2 * HALF))
            tile_loop(HALF, 256, proj_gate)
            return
        unit_row = lax.broadcasted_iota(jnp.int32, (8, 128), 0)
        unit = jnp.where(unit_row == lax.broadcasted_iota(jnp.int32, (8, 128), 1), 1.0, 0.0).astype(BF16)
        r.gain[...] = dot_t(unit, r.wa[:, pl.ds(1024, 128)])
        row_loop(OWN, 64, gain_rows)
        tile_loop(2 * HALF, 256, proj)

    def do_out(start):
        partial_rows(r.mix, out_product, 0, start, 128)
        if start >= OWN:
            swap_rows(2 if start == 256 else 3, r.es.at[0], r.er.at[0], start - OWN, 128)

    def do_resid(start):
        swapped_rows(2 + start // 128, r.er.at[0], start, 128)
        over(start, 128, resid_rows)
        swap(4 + start // 128, r.nt.at[pl.ds(start, 128)], r.nt.at[pl.ds(OWN + start, 128)])

    def do_hidden(part):
        if part:
            tile_loop(640, 256, lambda at, width: hidden(at + 768, width))
            return
        swapped(4, r.nt.at[pl.ds(OWN, 128)])
        swapped(5, r.nt.at[pl.ds(OWN + 128, 128)])
        tile_loop(768, 256, hidden)

    def do_cot():
        load_cot.wait()
        swapped(1, r.cot.at[pl.ds(OWN, OWN)])

    def do_back(start):
        if start == 0:
            partial_rows(r.fs, hidden_back, 1, 0, 256)
            return
        partial_rows(r.fs, hidden_back, 1, start, 128)
        swap_rows(6 if start == 256 else 7, r.es.at[1], r.er.at[1], start - OWN, 128)

    def do_resid_grad(start):
        swapped_rows(6 + start // 128, r.er.at[1], start, 128)
        over(start, 128, resid_grad_rows)
        swap(8 + start // 128, r.bg.at[pl.ds(start, 128)], r.bg.at[pl.ds(OWN + start, 128)])

    def do_mixed_grad(start):
        if start == 0:
            mixed_grad(0, 256)
            return
        swapped(8 if start == 256 else 9, r.bg.at[pl.ds(start, 128)])
        mixed_grad(start, 128)

    def do_heads_back(start):
        partial_rows(r.g4, heads_back, 2, start, 256)
        if start:
            swap(11, r.es.at[2], r.er.at[2])

    def do_block_out():
        swaps.pop(2).wait_send()
        swaps.pop(3).wait_send()
        tile_loop(D, 256, block_out_part)
        swap(10, r.es.at[0], r.er.at[0])

    def do_tokens_grad():
        swapped(11, r.er.at[2])
        over(0, OWN, tokens_grad_rows)
        outs.append(local(r.rg, r.tokens_grad, r.s_out.at[1]))

    def do_block_rows():
        swapped(10, r.er.at[0])
        over(0, OWN, block_out_rows)
        outs.append(local(r.bo, r.block_out, r.s_out.at[0]))

    def do_gsum(n):
        if n == 0:
            which = lax.broadcasted_iota(jnp.int32, (8, D), 0)
            zero = jnp.zeros((8, D), F32)
            sums = [jnp.sum(r.gacc[i], axis=0, keepdims=True) for i in range(2)]
            grad_sum(0, jnp.where(which == 0, sums[0], zero) + jnp.where(which == 1, sums[1], zero))
        elif n < 4:
            grad_sum(n)
        else:
            r.gacc[0, 0:2, :] = grad_sum(4)
            outs.append(local(r.gacc.at[0], r.gain_grads, r.s_out.at[2]))

    def do_take_z(i):
        if Z_FIRST[i]:
            take_y(i)
        take_z(i)

    def do_attend(start):
        over(start, 64, attend)

    def do_hidden_grad():
        tile_loop(FH, 256, hidden_grad)

    def do_attend_grad(start):
        over(start, 64, attend_grad)

    work = (
        (do_start,), (own, GH), (own, GA), (got_z, GH, 1, 0), (own, GB), (do_start2,), (got_z, GH, 2, 0),
        (got_y, GA, 0), (got_z, GA, 1, 0), (own, GO), (got_z, GA, 2, 0), (got_y, GH, 1), (got_y, GH, 0),
        (do_norm_own,), (got_z, GB, 1, 0), (got_z, GB, 2, 0), (got_z, GH, 3, 0), (got_z, GA, 3, 0), (got_y, GO, 0),
        (got_z, GB, 3, 0), (got_y, GA, 2), (got_y, GH, 2), (got_z, GO, 1, 0), (got_z, GO, 2, 0), (got_y, GB, 1),
        (got_z, GO, 3, 0), (own, GS), (own, GF), (got_y, GB, 2), (got_y, GA, 3), (got_y, GB, 0), (got_y, GH, 3),
        (own, GD), (got_y, GA, 1), (own, GT), (own, GG), (do_norm_partner,), (whole, GH), (got_y, GB, 3), (whole, GA),
        (do_proj, 0), (whole, GB), (do_proj, 1), (got_y, GO, 2), (got_y, GO, 1), (got_y, GO, 3), (got_z, GS, 1, 0),
        (do_attend, 256), (whole, GO), (do_attend, 320), (do_out, 256), (got_z, GT, 1, 0), (do_attend, 448),
        (got_z, GF, 1, 0), (got_z, GG, 1, 0), (got_z, GF, 2, 0), (got_z, GS, 2, 0), (got_z, GG, 2, 0),
        (do_attend, 384), (got_y, GD, 0), (got_y, GS, 0), (do_out, 384), (got_z, GS, 3, 0), (do_attend, 0),
        (do_attend, 64), (do_out, 0), (do_resid, 0), (got_z, GF, 3, 0), (got_z, GG, 3, 0), (got_y, GT, 1),
        (do_attend, 192), (got_z, GT, 2, 0), (got_y, GT, 0), (got_z, GS, 1, 1), (got_z, GS, 2, 1), (got_y, GG, 0),
        (got_z, GT, 3, 0), (do_attend, 128), (got_z, GD, 1, 0), (do_out, 128), (do_resid, 128), (got_y, GG, 1),
        (got_z, GD, 2, 0), (got_y, GG, 2), (got_z, GS, 3, 1), (whole, GS), (got_y, GG, 3), (got_y, GF, 3),
        (got_y, GF, 1), (got_y, GF, 2), (got_y, GF, 0), (whole, GG), (whole, GF), (got_y, GT, 2), (got_z, GD, 3, 0),
        (got_y, GT, 3), (do_hidden, 0), (whole, GT), (do_hidden, 1), (do_cot,), (give, 0), (give, 1), (got_y, GD, 2),
        (got_y, GD, 1), (take, 0), (got_y, GD, 3), (take, 1), (whole, GD), (do_hidden_grad,), (give, 2),
        (do_back, 256), (give, 3), (take, 2), (give, 4), (take, 3), (give, 5), (pass_far, 1), (take_y, 0),
        (do_back, 384), (take, 5), (do_back, 0), (do_resid_grad, 0), (take_y, 2), (do_resid_grad, 128),
        (do_mixed_grad, 0), (do_attend_grad, 64), (do_attend_grad, 192), (do_attend_grad, 0), (pass_far, 0),
        (do_mixed_grad, 256), (do_attend_grad, 320), (take_y, 3), (do_take_z, 0), (pass_far, 2), (take, 4),
        (do_mixed_grad, 384), (give, 6), (do_attend_grad, 448), (do_attend_grad, 256), (pass_far, 3), (take_y, 5),
        (give, 7), (do_attend_grad, 128), (do_take_z, 2), (do_attend_grad, 384), (do_heads_back, 256), (take, 6),
        (give, 8), (take, 7), (give, 9), (pass_far, 5), (take, 9), (take, 8), (give, 10), (give, 11), (take, 11),
        (pass_far, 7), (take_y, 4), (do_take_z, 3), (owner_sum, 1), (do_heads_back, 0), (do_block_out,),
        (do_tokens_grad,), (do_gsum, 0), (take_y, 9), (do_take_z, 5), (pass_far, 4), (do_take_z, 4), (take_y, 6),
        (take, 10), (finish, 0), (pass_far, 9), (take_y, 11), (owner_sum, 7), (take_y, 8), (do_take_z, 1),
        (do_take_z, 9), (finish, 2), (pass_far, 6), (pass_far, 11), (do_block_rows,), (do_gsum, 1), (pass_far, 8),
        (do_take_z, 6), (finish, 4), (take_y, 10), (do_take_z, 7), (do_gsum, 2), (finish, 3), (pass_far, 10),
        (finish, 9), (do_gsum, 3), (do_take_z, 8), (do_take_z, 11), (finish, 1), (finish, 6), (do_take_z, 10),
        (finish, 5), (finish, 10), (finish, 8), (finish, 7), (finish, 11), (do_gsum, 4),
    )
    for step, *args in work:
        step(*args)
    for copy in list(chunk_sends.values()) + list(swaps.values()) + sends:
        copy.wait_send()
    for pred, copy in guarded:
        pl.when(pred)(copy.wait_send)
    for copy in finals + outs:
        copy.wait()
    for g in "abfsgt":
        gi = GROUPS.index(g)
        own = col_shard(g, x)
        remote(own, own, r.s_xs.at[gi, 0], r.s_xs.at[gi, 0], xn).wait_send()
    for g in ("o", "d"):
        gi = GROUPS.index(g)
        block = r.wo.at[pl.ds(0, 32), pl.ds(0, 512)] if g == "o" else r.wds.at[0]

        @pl.when(x != c)
        def _():
            remote(block, block, r.s_xs.at[gi, 0], r.s_xs.at[gi, 0], xn).wait_send()

        remote(block, block, r.s_xs.at[gi, 1], r.s_xs.at[gi, 1], xn).wait_send()


def hand_over(gain_ref, *refs):
    count = (len(refs) - 4) // 3
    ins, (one, two), outs = refs[:count], refs[count : count + 2], refs[count + 2 : 2 * count + 2]
    held, (in_sems, out_sems) = refs[2 * count + 2 : -2], refs[-2:]
    loads = [pltpu.make_async_copy(a, b, in_sems.at[i]) for i, (a, b) in enumerate(zip(ins, held))]
    stores = [pltpu.make_async_copy(a, b, out_sems.at[i]) for i, (a, b) in enumerate(zip(held, outs))]
    for load in loads:
        load.start()
    me = lax.axis_index("dp") * 16 + lax.axis_index("fsdp")
    block = gain_ref[:, lanes_of(128 * (me // 4), 128)]
    block = pltpu.roll(block, lax.rem(128 - 32 * lax.rem(me, 4), 128), 1)
    one[...] = block[0, :32]
    two[...] = block[1, :32]
    for load, store in zip(loads, stores):
        load.wait()
        store.start()
    for store in stores:
        store.wait()


def fused_layer(
    tokens, attn_gain, w_query, w_key, w_value, w_gate, w_output, ffn_gain, w_first, w_second, w_down, cotangent
):
    items = scratch_list()
    names = IN_NAMES + OUT_NAMES + tuple(name for name, _ in items)
    shape = jax.ShapeDtypeStruct
    outs = pl.pallas_call(
        functools.partial(layer_kernel, names),
        out_shape=[
            shape((OWN, D), BF16), shape((OWN, D), F32), shape((8, D), F32),
            shape((32, D), F32), shape((32, D), F32), shape((32, D), F32), shape((32, D), F32), shape((32, D), F32),
            shape((32, FF), F32), shape((32, FF), F32), shape((88, D), F32),
        ],
        in_specs=[pl.BlockSpec(memory_space=pltpu.VMEM if n.startswith("gain") else pl.ANY) for n in IN_NAMES],
        out_specs=[pl.BlockSpec(memory_space=pl.ANY)] * len(OUT_NAMES),
        scratch_shapes=[spec for _, spec in items],
        compiler_params=pltpu.CompilerParams(collective_id=0, has_side_effects=True, vmem_limit_bytes=66 * 2**20 - 2**21),
        name="layer",
    )(tokens, attn_gain, ffn_gain, w_query, w_key, w_value, w_gate, w_output, w_first, w_second, w_down, cotangent)
    block_out, tokens_grad, gain_grads, gq, gk, gv, gg, go, g1, g2, gd = outs
    kept = (block_out, tokens_grad, gq, gk, gv, gg, go, g1, g2, gd)
    anywhere = pl.BlockSpec(memory_space=pl.ANY)
    in_vmem = pl.BlockSpec(memory_space=pltpu.VMEM)
    gain_one, gain_two, *rest = pl.pallas_call(
        hand_over,
        out_shape=[shape((32,), F32)] * 2 + [shape(v.shape, v.dtype) for v in kept],
        in_specs=[in_vmem] + [anywhere] * len(kept),
        out_specs=[in_vmem] * 2 + [anywhere] * len(kept),
        scratch_shapes=[pltpu.VMEM(v.shape, v.dtype) for v in kept] + [pltpu.SemaphoreType.DMA((len(kept),))] * 2,
        compiler_params=pltpu.CompilerParams(vmem_limit_bytes=63 * 2**20),
        name="hand_over",
    )(gain_grads, *kept)
    block_out, tokens_grad, gq, gk, gv, gg, go, g1, g2, gd = rest
    return block_out, tokens_grad, gain_one, gq, gk, gv, gg, go, gain_two, g1, g2, gd


def rms_scale(values, gain):
    return values * lax.rsqrt(jnp.mean(values * values, axis=-1, keepdims=True) + EPS) * gain


def gated(attended, gate_pre):
    return attended * jax.nn.silu(gate_pre)


def contract_rows(left, right):
    return lax.dot_general(
        left, right, (((0,), (0,)), ((), ())), preferred_element_type=jnp.float32
    )


def contract_cols(left, right):
    return lax.dot_general(
        left, right, (((1,), (1,)), ((), ())), preferred_element_type=jnp.float32
    )


def project(left, right):
    return jnp.dot(left, right, preferred_element_type=jnp.float32)


def flatten_rows(matrix):
    return matrix.reshape(-1, 128)


def restore_rows(flat, columns):
    return flat.reshape(-1, columns)


def split_heads(matrix):
    return matrix.reshape(matrix.shape[0] // BLK, BLK, HEADS, HDIM)


def block_scores(queries, keys):
    raw = jnp.einsum(
        "bqhd,bkhd->bhqk",
        split_heads(queries),
        split_heads(keys),
        preferred_element_type=jnp.float32,
    )
    causal = jnp.arange(BLK)[:, None] >= jnp.arange(BLK)[None, :]
    return jnp.where(causal, raw * HDIM ** (-0.5), -1e30)


def attend_forward(queries, keys, values):
    scores = block_scores(queries, keys)
    highest = jnp.max(scores, axis=-1, keepdims=True)
    weights = jnp.exp(scores - highest)
    total = jnp.sum(weights, axis=-1, keepdims=True)
    probs = (weights / total).astype(jnp.bfloat16)
    attended = jnp.einsum(
        "bhqk,bkhd->bqhd", probs, split_heads(values), preferred_element_type=jnp.float32
    )
    return (attended.reshape(queries.shape[0], D), highest + jnp.log(total))


def attend_backward(queries, keys, values, log_total, attended_grad):
    scores = block_scores(queries, keys)
    probs = jnp.exp(scores - log_total)
    grad_heads = split_heads(attended_grad)
    value_grad = jnp.einsum(
        "bhqk,bqhd->bkhd",
        probs.astype(jnp.bfloat16),
        grad_heads,
        preferred_element_type=jnp.float32,
    )
    prob_grad = jnp.einsum(
        "bqhd,bkhd->bhqk", grad_heads, split_heads(values), preferred_element_type=jnp.float32
    )
    score_grad = (probs * (prob_grad - jnp.sum(probs * prob_grad, axis=-1, keepdims=True))).astype(
        jnp.bfloat16
    )
    factor = HDIM ** (-0.5)
    query_grad = (
        jnp.einsum(
            "bhqk,bkhd->bqhd", score_grad, split_heads(keys), preferred_element_type=jnp.float32
        )
        * factor
    )
    key_grad = (
        jnp.einsum(
            "bhqk,bqhd->bkhd", score_grad, split_heads(queries), preferred_element_type=jnp.float32
        )
        * factor
    )
    length = queries.shape[0]
    return (
        query_grad.reshape(length, D).astype(jnp.bfloat16),
        key_grad.reshape(length, D).astype(jnp.bfloat16),
        value_grad.reshape(length, D).astype(jnp.bfloat16),
    )


def on_device(
    tokens,
    attn_gain,
    w_query,
    w_key,
    w_value,
    w_gate,
    w_output,
    ffn_gain,
    w_first,
    w_second,
    w_down,
    cotangent,
):
    attn_whole = (
        lax.all_gather(attn_gain, ("dp", "fsdp"), axis=0, tiled=True),
        lax.all_gather(w_query, ("dp", "fsdp"), axis=0, tiled=True),
        lax.all_gather(w_key, ("dp", "fsdp"), axis=0, tiled=True),
        lax.all_gather(w_value, ("dp", "fsdp"), axis=0, tiled=True),
        lax.all_gather(w_gate, ("dp", "fsdp"), axis=0, tiled=True),
        lax.all_gather(w_output, ("dp", "fsdp"), axis=0, tiled=True),
    )
    gain_one, query_full, key_full, value_full, gate_full, output_full = attn_whole
    inputs = tokens.astype(jnp.float32)
    normed_pre, norm_pull = jax.vjp(rms_scale, inputs, gain_one.astype(jnp.float32))
    normed = normed_pre.astype(jnp.bfloat16)
    queries = project(normed, query_full).astype(jnp.bfloat16)
    keys = project(normed, key_full).astype(jnp.bfloat16)
    values = project(normed, value_full).astype(jnp.bfloat16)
    gate_pre = project(normed, gate_full)
    attended, log_total = attend_forward(queries, keys, values)
    mixed_pre, gate_pull = jax.vjp(gated, attended, gate_pre)
    mixed = mixed_pre.astype(jnp.bfloat16)
    resid = inputs + project(mixed, output_full)
    ffn_whole = (
        lax.all_gather(ffn_gain, ("dp", "fsdp"), axis=0, tiled=True),
        lax.all_gather(w_first, ("dp", "fsdp"), axis=0, tiled=True),
        lax.all_gather(w_second, ("dp", "fsdp"), axis=0, tiled=True),
        lax.all_gather(w_down, ("dp", "fsdp"), axis=0, tiled=True),
    )
    gain_two, first_full, second_full, down_full = ffn_whole
    normed_two_pre, norm_two_pull = jax.vjp(rms_scale, resid, gain_two.astype(jnp.float32))
    normed_two = normed_two_pre.astype(jnp.bfloat16)
    first = project(normed_two, first_full).astype(jnp.bfloat16)
    second = project(normed_two, second_full).astype(jnp.bfloat16)
    product = (first.astype(jnp.float32) * second.astype(jnp.float32)).astype(jnp.bfloat16)
    block_out = (resid + project(product, down_full)).astype(jnp.bfloat16)
    gain_two, first_full, second_full, down_full = (
        lax.all_gather(ffn_gain, ("dp", "fsdp"), axis=0, tiled=True),
        lax.all_gather(w_first, ("dp", "fsdp"), axis=0, tiled=True),
        lax.all_gather(w_second, ("dp", "fsdp"), axis=0, tiled=True),
        lax.all_gather(w_down, ("dp", "fsdp"), axis=0, tiled=True),
    )
    product_grad = contract_cols(cotangent, down_full).astype(jnp.bfloat16)
    product_wide = product_grad.astype(jnp.float32)
    first_grad = (product_wide * second.astype(jnp.float32)).astype(jnp.bfloat16)
    second_grad = (product_wide * first.astype(jnp.float32)).astype(jnp.bfloat16)
    normed_two_grad = contract_cols(first_grad, first_full) + contract_cols(
        second_grad, second_full
    )
    resid_part, gain_two_grad = norm_two_pull(normed_two_grad)
    resid_grad = cotangent.astype(jnp.float32) + resid_part
    down_grad = contract_rows(product, cotangent)
    first_w_grad = contract_rows(normed_two, first_grad)
    second_w_grad = contract_rows(normed_two, second_grad)
    ffn_sums = (
        lax.psum_scatter(gain_two_grad, ("dp", "fsdp"), scatter_dimension=0, tiled=True),
        lax.psum_scatter(
            flatten_rows(first_w_grad), ("dp", "fsdp"), scatter_dimension=0, tiled=True
        ),
        lax.psum_scatter(
            flatten_rows(second_w_grad), ("dp", "fsdp"), scatter_dimension=0, tiled=True
        ),
        lax.psum_scatter(flatten_rows(down_grad), ("dp", "fsdp"), scatter_dimension=0, tiled=True),
    )
    gain_one, query_full, key_full, value_full, gate_full, output_full = (
        lax.all_gather(attn_gain, ("dp", "fsdp"), axis=0, tiled=True),
        lax.all_gather(w_query, ("dp", "fsdp"), axis=0, tiled=True),
        lax.all_gather(w_key, ("dp", "fsdp"), axis=0, tiled=True),
        lax.all_gather(w_value, ("dp", "fsdp"), axis=0, tiled=True),
        lax.all_gather(w_gate, ("dp", "fsdp"), axis=0, tiled=True),
        lax.all_gather(w_output, ("dp", "fsdp"), axis=0, tiled=True),
    )
    branch_grad = resid_grad.astype(jnp.bfloat16)
    mixed_grad = contract_cols(branch_grad, output_full).astype(jnp.bfloat16)
    attended_part, gate_part = gate_pull(mixed_grad.astype(jnp.float32))
    attended_grad = attended_part.astype(jnp.bfloat16)
    gate_grad = gate_part.astype(jnp.bfloat16)
    query_grad, key_grad, value_grad = attend_backward(
        queries, keys, values, log_total, attended_grad
    )
    normed_grad = contract_cols(query_grad, query_full) + contract_cols(key_grad, key_full)
    normed_grad = (
        normed_grad + contract_cols(value_grad, value_full) + contract_cols(gate_grad, gate_full)
    )
    input_part, gain_one_grad = norm_pull(normed_grad)
    tokens_grad = resid_grad + input_part
    output_w_grad = contract_rows(mixed, branch_grad)
    query_w_grad = contract_rows(normed, query_grad)
    key_w_grad = contract_rows(normed, key_grad)
    value_w_grad = contract_rows(normed, value_grad)
    gate_w_grad = contract_rows(normed, gate_grad)
    attn_sums = (
        lax.psum_scatter(gain_one_grad, ("dp", "fsdp"), scatter_dimension=0, tiled=True),
        lax.psum_scatter(
            flatten_rows(query_w_grad), ("dp", "fsdp"), scatter_dimension=0, tiled=True
        ),
        lax.psum_scatter(flatten_rows(key_w_grad), ("dp", "fsdp"), scatter_dimension=0, tiled=True),
        lax.psum_scatter(
            flatten_rows(value_w_grad), ("dp", "fsdp"), scatter_dimension=0, tiled=True
        ),
        lax.psum_scatter(
            flatten_rows(gate_w_grad), ("dp", "fsdp"), scatter_dimension=0, tiled=True
        ),
        lax.psum_scatter(
            flatten_rows(output_w_grad), ("dp", "fsdp"), scatter_dimension=0, tiled=True
        ),
    )
    gain_two_sum, first_flat, second_flat, down_flat = ffn_sums
    gain_one_sum, query_flat, key_flat, value_flat, gate_flat, output_flat = attn_sums
    query_sum = restore_rows(query_flat, D)
    key_sum = restore_rows(key_flat, D)
    value_sum = restore_rows(value_flat, D)
    gate_sum = restore_rows(gate_flat, D)
    output_sum = restore_rows(output_flat, D)
    first_sum = restore_rows(first_flat, FF)
    second_sum = restore_rows(second_flat, FF)
    down_sum = restore_rows(down_flat, D)
    return (
        block_out,
        tokens_grad,
        gain_one_sum,
        query_sum,
        key_sum,
        value_sum,
        gate_sum,
        output_sum,
        gain_two_sum,
        first_sum,
        second_sum,
        down_sum,
    )


def solution(mesh):
    fits = dict(mesh.shape) == {"dp": 2, "fsdp": 16}
    return jax.shard_map(
        fused_layer if fits else on_device,
        mesh=mesh,
        in_specs=(
            P(("dp", "fsdp"), None),
            P(("dp", "fsdp")),
            P(("dp", "fsdp"), None),
            P(("dp", "fsdp"), None),
            P(("dp", "fsdp"), None),
            P(("dp", "fsdp"), None),
            P(("dp", "fsdp"), None),
            P(("dp", "fsdp")),
            P(("dp", "fsdp"), None),
            P(("dp", "fsdp"), None),
            P(("dp", "fsdp"), None),
            P(("dp", "fsdp"), None),
        ),
        out_specs=(
            P(("dp", "fsdp"), None),
            P(("dp", "fsdp"), None),
            P(("dp", "fsdp")),
            P(("dp", "fsdp"), None),
            P(("dp", "fsdp"), None),
            P(("dp", "fsdp"), None),
            P(("dp", "fsdp"), None),
            P(("dp", "fsdp"), None),
            P(("dp", "fsdp")),
            P(("dp", "fsdp"), None),
            P(("dp", "fsdp"), None),
            P(("dp", "fsdp"), None),
        ),
        check_vma=False,
    )
```
